32 devices in a mesh: gx: 4 (over x, core), gy: 8 (over z, y).
Axes of the slice: x: 2, y: 2, z: 4, core: 2. Of those that a mesh axis runs over, the one named last changes fastest.
Arguments:
- thickness: float32 [1536, 3072], P('gx', 'gy'), may hold values from 0.5 to 3
- bed_uplift: float32 [1536, 3072], P('gx', 'gy'), may hold values from -6 to 6
- flux_x: float32 [1536, 3072], P('gx', 'gy'), may hold values from -6 to 6
- flux_y: float32 [1536, 3072], P('gx', 'gy'), may hold values from -6 to 6
- mass_balance: float32 [1536, 3072], P('gx', 'gy'), may hold values from -3 to 3
- ice_mask: int32 [1536, 3072], P('gx', 'gy'), may hold values from 0 to 2
Outputs:
- thickness_new: float32 [1536, 3072], P('gx', 'gy')
- bed_new: float32 [1536, 3072], P('gx', 'gy')
The draws below stay inside these ranges and needn't reach their ends.
All inputs are finite; a program needn't handle non-finite values.
Results may differ from the reference program's by a relative error of at most 0.000092.
Values sent between devices are 32-bit elements; how exact they have to be, the bound alone decides.
No kernel may reach another device: no remote copies, remote signals or barrier semaphores. Data moves between devices by JAX's collectives and lax.ppermute only.
A program may use at most 64 MiB of HBM per device.

```python
import math
import jax
import jax.numpy as jnp

NX = 1536
NY = 3072


def plant(array, key, least, high):
    longest = array.shape.index(max(array.shape))
    spots = []
    for shift in (0, 1):
        where = [jax.random.randint(jax.random.fold_in(key, axis), (), 0, length) for axis, length in enumerate(array.shape)]
        where[longest] = (where[longest] + shift) % array.shape[longest]
        spots.append(tuple(where))
    return array.at[spots[0]].set(least).at[spots[1]].set(high)


def shard_levels(own_key, dims, split, least, top_value):
    def one(position, shards_of):
        draws = jax.random.uniform(jax.random.fold_in(jax.random.fold_in(own_key, 6), position), (shards_of,), jnp.float32, least / len(split), top_value / len(split))
        return jnp.repeat(jnp.exp(draws), dims[position] // shards_of).reshape((-1,) + (1,) * (len(dims) - position - 1))

    level = one(*split[0])
    for cut in split[1:]:
        level = level * one(*cut)
    return level


def gaussian(key, shape, scale, most, pieces=(), dtype=jnp.bfloat16):
    drawn = scale * jax.random.normal(key, shape, jnp.float32)
    if pieces:
        drawn = drawn * shard_levels(key, shape, pieces, -0.22, 0.18)
    return jnp.clip(drawn, -most, most).astype(dtype)


def setup_inputs(seed: int = 0) -> dict:
    streams_of = jax.random.split(jax.random.key(seed), 7)
    return {
        "thickness": jnp.clip(0.5 + 2.5 * jax.random.uniform(streams_of[0], (NX, NY), jnp.float32) ** shard_levels(streams_of[0], (NX, NY), ((0, 4), (1, 8)), -0.2, 0.2), 0.5, 3.0),
        "bed_uplift": gaussian(streams_of[1], (NX, NY), 1.0, 6.0, ((0, 4), (1, 8)), jnp.float32),
        "flux_x": gaussian(streams_of[2], (NX, NY), 1.0, 6.0, ((0, 4), (1, 8)), jnp.float32),
        "flux_y": gaussian(streams_of[3], (NX, NY), 1.0, 6.0, ((0, 4), (1, 8)), jnp.float32),
        "mass_balance": gaussian(streams_of[4], (NX, NY), 0.5, 3.0, ((0, 4), (1, 8)), jnp.float32),
        "ice_mask": plant(jax.random.randint(streams_of[5], (NX, NY), 0, 3), jax.random.fold_in(streams_of[5], 1), 0, 2).astype(jnp.int32),
    }


time_step = 0.5
viscous = 4.0
buoyant = 0.01
flexural = 50.0

def wave_numbers(length):
    index = jnp.arange(length)
    signed = jnp.where(2 * index >= length, index - length, index)
    return signed.astype(jnp.float32) * (2.0 * math.pi / length)

def reference(thickness, bed_uplift, flux_x, flux_y, mass_balance, ice_mask):
    flux_below = jnp.pad(flux_x, ((1, 0), (0, 0)))[:-1, :]
    flux_left = jnp.pad(flux_y, ((0, 0), (1, 0)))[:, :-1]
    divergence = flux_x - flux_below + flux_y - flux_left
    trial = thickness + time_step * (mass_balance - divergence)
    thickness_new = jnp.where(ice_mask == 2, 0.0, jnp.maximum(trial, 0.0))
    load = jnp.where(ice_mask == 0, thickness_new - thickness, 0.0)
    kx_part = wave_numbers(NX)[:, None]
    ky_part = wave_numbers(NY)[None, :]
    kappa = jnp.sqrt(kx_part * kx_part + ky_part * ky_part)
    uplift_hat = jnp.fft.fft2(bed_uplift)
    load_hat = jnp.fft.fft2(load)
    damping = viscous * kappa
    denominator = damping + buoyant + flexural * kappa ** 4
    bed_hat = (damping * uplift_hat - load_hat) / denominator
    bed_new = jnp.real(jnp.fft.ifft2(bed_hat)).astype(jnp.float32)
    return (thickness_new, bed_new)
```

```python
import math

import jax
import jax.numpy as jnp
import numpy as np
from jax import lax
from jax.sharding import PartitionSpec as P

time_step = 0.5
viscous = 4.0
buoyant = 0.01
flexural = 50.0
lanes = 128
highest = lax.Precision.HIGHEST


class Plan:
    def __init__(self, mesh, length_x, length_y):
        self.gx, self.gy = mesh.shape["gx"], mesh.shape["gy"]
        self.devices = self.gx * self.gy
        self.length_x, self.length_y = length_x, length_y
        self.radix = length_x // lanes
        self.here = self.radix // self.gx
        self.groups = self.radix // 2
        self.cols = length_y // self.devices
        self.m_parts = min(self.devices, lanes)
        self.g_parts = self.devices // self.m_parts
        self.deep = lanes // self.m_parts
        self.own_groups = self.groups // self.g_parts
        self.rows = 2 * self.deep

    def slot_matrix(self):
        n2 = np.arange(lanes)[None, :]
        m = np.arange(lanes)[:, None]
        theta = 2 * np.pi * (m * n2 % lanes) / lanes
        cos, sin = np.cos(theta), np.sin(theta)
        general = np.stack([np.concatenate([cos, sin], 1), np.concatenate([-sin, cos], 1)])
        half = lanes // 2
        turned = 2 * np.pi * ((2 * (m - half) + 1) * n2 % (2 * lanes)) / (2 * lanes)
        low = np.arange(lanes)[:, None] < half
        real = np.concatenate([np.where(low, cos, 0), np.where(low, 0, np.cos(turned))], 1)
        imag = np.concatenate([np.where(low, -sin, 0), np.where(low, 0, -np.sin(turned))], 1)
        imag[0, :lanes] = np.where(np.arange(lanes) % 2 == 0, 1.0, -1.0)
        first = np.stack([real, imag])
        return np.stack([self._by_part(general), self._by_part(first)]).astype(np.float32)

    def _by_part(self, table):
        split = table.reshape(2, self.m_parts, self.deep, 2 * lanes)
        return split.transpose(1, 0, 2, 3).reshape(2 * lanes, 2 * lanes)

    def slot_inverse(self):
        m = np.arange(lanes)[:, None]
        n2 = np.arange(lanes)[None, :]
        theta = 2 * np.pi * (m * n2 % lanes) / lanes
        cos, sin = np.cos(theta), np.sin(theta)
        general = 2 * np.stack([np.concatenate([cos, sin], 1), np.concatenate([-sin, cos], 1)])
        half = lanes // 2
        turned = 2 * np.pi * ((2 * (m - half) + 1) * n2 % (2 * lanes)) / (2 * lanes)
        low = m < half
        real = 2 * np.concatenate([np.where(low, cos, 0), np.where(low, 0, np.cos(turned))], 1)
        imag = 2 * np.concatenate([np.where(low, -sin, 0), np.where(low, 0, -np.sin(turned))], 1)
        real[0, :lanes] = 1.0
        imag[0, :lanes] = np.where(np.arange(lanes) % 2 == 0, 1.0, -1.0)
        first = np.stack([real, imag])
        return (np.stack([self._by_part(general), self._by_part(first)]) / self.length_x).astype(np.float32)

    def slot_twiddle(self):
        angle = 2 * np.pi * np.arange(self.groups)[:, None] * np.arange(lanes)[None, :] / self.length_x
        return np.stack([np.cos(angle), np.sin(angle)]).astype(np.float32)

    def source_matrix(self):
        count, deep = self.devices, self.deep
        index = np.arange(count)
        theta = 2 * np.pi * (index[:, None] * index[None, :] % count) / count
        cos, sin = np.cos(theta), np.sin(theta)
        out = np.zeros((count, 2, deep, 2, count, deep))
        for q in range(deep):
            out[:, 0, q, 0, :, q] = cos
            out[:, 1, q, 0, :, q] = sin
            out[:, 0, q, 1, :, q] = -sin
            out[:, 1, q, 1, :, q] = cos
        return out.reshape(count * 2 * deep, 2 * count * deep).astype(np.float32)

    def line_matrix(self):
        index = np.arange(self.cols)
        theta = 2 * np.pi * (index[:, None] * index[None, :] % self.cols) / self.cols
        cos, sin = np.cos(theta), np.sin(theta)
        return np.block([[cos, sin], [-sin, cos]]).astype(np.float32)

    def line_twiddle(self):
        angle = 2 * np.pi * np.arange(self.cols)[:, None] * np.arange(self.devices)[None, :] / self.length_y
        angle = np.repeat(angle, self.deep, axis=1)
        return np.stack([np.cos(angle), np.sin(angle)]).astype(np.float32)


def weighted(terms):
    groups = {}
    for coefficient, value in terms:
        size = round(abs(coefficient), 12)
        if size == 0.0:
            continue
        groups.setdefault(size, []).append((coefficient > 0, value))
    total = None
    for size, members in groups.items():
        members.sort(key=lambda member: not member[0])
        positive, part = members[0]
        for sign, value in members[1:]:
            part = part + value if sign == positive else part - value
        if size != 1.0:
            part = part * np.float32(size)
        if total is None:
            total = part if positive else -part
        else:
            total = total + part if positive else total - part
    return total


def radix_forward(values):
    count = len(values)
    half = count // 2
    even = [values[j] + values[count - j] for j in range(1, half)]
    odd = [values[j] - values[count - j] for j in range(1, half)]
    real, imag = [], []
    for g in range(half + 1):
        terms = [(1.0, values[0]), ((-1.0) ** g, values[half])]
        terms += [(math.cos(2 * math.pi * g * (j + 1) / count), even[j]) for j in range(half - 1)]
        real.append(weighted(terms))
        if 0 < g < half:
            imag.append(weighted([(-math.sin(2 * math.pi * g * (j + 1) / count), odd[j]) for j in range(half - 1)]))
    return real, imag


def radix_inverse(first, middle, real, imag):
    half = len(real) + 1
    count = 2 * half
    out = [None] * count
    for j in range(half + 1):
        terms = [(1.0, first), ((-1.0) ** j, middle)]
        terms += [(math.cos(2 * math.pi * g * j / count), real[g - 1]) for g in range(1, half)]
        together = weighted(terms)
        if j in (0, half):
            out[j] = together
            continue
        apart = weighted([(math.sin(2 * math.pi * g * j / count), imag[g - 1]) for g in range(1, half)])
        out[j] = together - apart
        out[count - j] = together + apart
    return out


def mul(a, b):
    return jnp.matmul(a, b, precision=highest)


def exchange_gx(value):
    count = lax.axis_size("gx")
    own = lax.axis_index("gx")
    if count > 8:
        return lax.all_to_all(value, "gx", split_axis=0, concat_axis=0, tiled=True)
    pieces = [lax.dynamic_index_in_dim(value, own, 0, False)]
    for step in range(1, count):
        piece = lax.dynamic_index_in_dim(value, own ^ step, 0, False)
        pieces.append(lax.ppermute(piece, "gx", [(k, k ^ step) for k in range(count)]))
    stacked = jnp.stack(pieces)
    return jnp.stack([lax.dynamic_index_in_dim(stacked, own ^ k, 0, False) for k in range(count)])


def exchange_all(value):
    return lax.all_to_all(value, ("gy", "gx"), split_axis=0, concat_axis=0, tiled=True)


def passed_along(value, axis, steps):
    count = lax.axis_size(axis)
    leading, last = (max(0, -steps), min(count, count - steps))
    return lax.ppermute(value, axis, [(source, source + steps) for source in range(leading, last)])


def forward_x(plan, lines):
    table = plan.slot_matrix()
    cos, sin = plan.slot_twiddle()
    real, imag = radix_forward([lines[:, n] for n in range(plan.radix)])
    blocks = [jnp.concatenate([real[0], real[plan.groups]], -1)]
    for g in range(1, plan.groups):
        re, im = real[g], imag[g - 1]
        blocks.append(jnp.concatenate([re * cos[g] + im * sin[g], im * cos[g] - re * sin[g]], -1))
    first = jnp.einsum("ok,fck->ofc", table[1], blocks[0], precision=highest)
    row = first[plan.deep, 0]
    first = first.at[plan.deep, 0].set(first[0, 1]).at[0, 1].set(row)
    rest = jnp.einsum("ok,gfck->ogfc", table[0], jnp.stack(blocks[1:]), precision=highest)
    spectrum = jnp.concatenate([first[:, None], rest], 1)
    spectrum = spectrum.reshape(plan.m_parts, plan.rows, plan.g_parts, -1)
    return spectrum.transpose(2, 0, 1, 3).reshape(plan.devices, plan.rows, -1)


def spectral_kernels(square):
    kappa = jnp.sqrt(square)
    damping = viscous * kappa
    across = 1.0 / (damping + buoyant + flexural * kappa**4)
    return damping, across


def wave_square(index, length):
    signed = jnp.where(2 * index >= length, index - length, index)
    wave = signed.astype(jnp.float32) * (2.0 * math.pi / length)
    return wave * wave


def middle_y(plan, received, position):
    deep, count, cols = plan.deep, plan.devices, plan.cols
    width = count * deep
    flat = received.reshape(count * plan.rows, -1).T
    mixed = mul(flat, plan.source_matrix())
    mixed = mixed.reshape(plan.own_groups, 2, cols, 2, width)
    cos, sin = plan.line_twiddle()
    re, im = mixed[:, :, :, 0], mixed[:, :, :, 1]
    turned = jnp.concatenate([re * cos + im * sin, im * cos - re * sin], 2)
    spectra = jnp.einsum("wk,gfkl->gfwl", plan.line_matrix(), turned, precision=highest)
    lane = lax.broadcasted_iota(jnp.int32, (1, width), 1)
    q, t = lane % deep, lane // deep
    w = lax.broadcasted_iota(jnp.int32, (cols, 1), 0)
    ky = wave_square(t + count * w, plan.length_y)
    m = (position % plan.m_parts) * deep + q
    base = (position // plan.m_parts) * plan.own_groups
    special = (position == 0) & (q == 0)
    results = []
    for group in range(plan.own_groups):
        g = base + group
        half = lanes // 2
        first = jnp.where(m < half, plan.radix * m, plan.radix // 2 + plan.radix * (m - half))
        index = jnp.where(g == 0, first, g + plan.radix * m)
        damping, across = spectral_kernels(wave_square(index, plan.length_x) + ky)
        u, v = spectra[group, 0], spectra[group, 1]
        ur, ui, vr, vi = u[:cols], u[cols:], v[:cols], v[cols:]
        out_r, out_i = across * (damping * ur - vr), across * (damping * ui - vi)
        if group == 0:
            out_r = jnp.where(special, across * (damping * ur - ui), out_r)
            out_i = jnp.where(special, across * (damping * ui + ur), out_i)
            damping, across = spectral_kernels(np.float32(math.pi) ** 2 + ky)
            extra = jnp.concatenate([across * (damping * vr - vi), across * (damping * vi + vr)], 0)
        results.append(jnp.concatenate([out_r, out_i], 0))
    results.append(extra)
    back = jnp.einsum("kw,gkl->gwl", plan.line_matrix() * np.float32(1.0 / plan.length_y), jnp.stack(results), precision=highest)
    re, im = back[:, :cols], back[:, cols:]
    turned = jnp.concatenate([re * cos - im * sin, im * cos + re * sin], 2)
    lines = jnp.einsum("gcl,sl->gcs", turned, plan.source_matrix(), precision=highest)
    place = lax.broadcasted_iota(jnp.int32, (1, count * plan.rows), 1)
    moved = (position == 0) & (place % plan.rows == deep)
    fixed = jnp.where(moved, jnp.roll(lines[-1], deep, axis=1), lines[0])
    lines = jnp.concatenate([fixed[None], lines[1:-1]], 0)
    return lines.reshape(plan.own_groups * cols, count * plan.rows).T.reshape(count, plan.rows, -1)


def inverse_x(plan, received):
    cols = plan.cols
    table = plan.slot_inverse()
    cos, sin = plan.slot_twiddle()
    split = received.reshape(plan.g_parts, 2 * lanes, plan.own_groups, cols)
    split = split.transpose(0, 2, 3, 1).reshape(plan.groups, cols, 2 * lanes)
    first = mul(split[0], table[1])
    rest = mul(split[1:], table[0])
    real, imag = [], []
    for g in range(1, plan.groups):
        re, im = rest[g - 1, :, :lanes], rest[g - 1, :, lanes:]
        real.append(re * cos[g] - im * sin[g])
        imag.append(im * cos[g] + re * sin[g])
    return radix_inverse(first[:, :lanes], first[:, lanes:], real, imag)


def to_lines(plan, field):
    split = field.reshape(plan.here, lanes, plan.gx, plan.cols)
    return split.transpose(2, 0, 3, 1)


def build(plan):
    def local(thickness, bed_uplift, flux_x, flux_y, mass_balance, ice_mask):
        lower_face = passed_along(flux_x[-1:, :], "gx", 1)
        left_face = passed_along(flux_y[:, -1:], "gy", 1)
        flux_below = jnp.concatenate([lower_face, flux_x[:-1, :]], axis=0)
        flux_left = jnp.concatenate([left_face, flux_y[:, :-1]], axis=1)
        divergence = flux_x - flux_below + flux_y - flux_left
        trial = thickness + time_step * (mass_balance - divergence)
        thickness_new = jnp.where(ice_mask == 2, 0.0, jnp.maximum(trial, 0.0))
        load = jnp.where(ice_mask == 0, thickness_new - thickness, 0.0)
        fields = jnp.stack([to_lines(plan, bed_uplift), to_lines(plan, load)], 1)
        lines = exchange_gx(fields)
        lines = lines.transpose(1, 0, 2, 3, 4).reshape(2, plan.radix, plan.cols, lanes)
        received = exchange_all(forward_x(plan, lines))
        position = lax.axis_index("gy") * plan.gx + lax.axis_index("gx")
        back = exchange_all(middle_y(plan, received, position))
        bed = inverse_x(plan, back)
        bed = jnp.stack(bed).reshape(plan.gx, plan.here, plan.cols, lanes)
        bed = exchange_gx(bed)
        bed_new = bed.transpose(1, 3, 0, 2).reshape(plan.here * lanes, plan.gx * plan.cols)
        return thickness_new, bed_new

    return local


def solution(mesh):
    spec = P("gx", "gy")

    def step(*args):
        length_x, length_y = args[0].shape
        plan = Plan(mesh, length_x, length_y)
        body = jax.shard_map(build(plan), mesh=mesh, in_specs=(spec,) * 6, out_specs=(spec, spec), check_vma=False)
        return body(*args)

    return step
```

```python
import math

import jax
import jax.numpy as jnp
import numpy as np
from jax import lax
from jax.experimental import pallas as pl
from jax.experimental.pallas import tpu as pltpu
from jax.sharding import PartitionSpec as P

time_step = 0.5
viscous = 4.0
buoyant = 0.01
flexural = 50.0
lanes = 128
highest = lax.Precision.HIGHEST


class Plan:
    def __init__(self, mesh, length_x, length_y):
        self.gx, self.gy = mesh.shape["gx"], mesh.shape["gy"]
        self.devices = self.gx * self.gy
        self.length_x, self.length_y = length_x, length_y
        self.radix = length_x // lanes
        self.here = self.radix // self.gx
        self.groups = self.radix // 2
        self.cols = length_y // self.devices
        self.m_parts = min(self.devices, lanes)
        self.g_parts = self.devices // self.m_parts
        self.deep = lanes // self.m_parts
        self.own_groups = self.groups // self.g_parts
        self.rows = 2 * self.deep

    def slot_matrix(self):
        n2 = np.arange(lanes)[None, :]
        m = np.arange(lanes)[:, None]
        theta = 2 * np.pi * (m * n2 % lanes) / lanes
        cos, sin = np.cos(theta), np.sin(theta)
        general = np.stack([np.concatenate([cos, sin], 1), np.concatenate([-sin, cos], 1)])
        half = lanes // 2
        turned = 2 * np.pi * ((2 * (m - half) + 1) * n2 % (2 * lanes)) / (2 * lanes)
        low = np.arange(lanes)[:, None] < half
        real = np.concatenate([np.where(low, cos, 0), np.where(low, 0, np.cos(turned))], 1)
        imag = np.concatenate([np.where(low, -sin, 0), np.where(low, 0, -np.sin(turned))], 1)
        imag[0, :lanes] = np.where(np.arange(lanes) % 2 == 0, 1.0, -1.0)
        first = np.stack([real, imag])
        return np.stack([self._by_part(general), self._by_part(first)]).astype(np.float32)

    def _by_part(self, table):
        split = table.reshape(2, self.m_parts, self.deep, 2 * lanes)
        return split.transpose(1, 0, 2, 3).reshape(2 * lanes, 2 * lanes)

    def slot_inverse(self):
        m = np.arange(lanes)[:, None]
        n2 = np.arange(lanes)[None, :]
        theta = 2 * np.pi * (m * n2 % lanes) / lanes
        cos, sin = np.cos(theta), np.sin(theta)
        general = 2 * np.stack([np.concatenate([cos, sin], 1), np.concatenate([-sin, cos], 1)])
        half = lanes // 2
        turned = 2 * np.pi * ((2 * (m - half) + 1) * n2 % (2 * lanes)) / (2 * lanes)
        low = m < half
        real = 2 * np.concatenate([np.where(low, cos, 0), np.where(low, 0, np.cos(turned))], 1)
        imag = 2 * np.concatenate([np.where(low, -sin, 0), np.where(low, 0, -np.sin(turned))], 1)
        real[0, :lanes] = 1.0
        imag[0, :lanes] = np.where(np.arange(lanes) % 2 == 0, 1.0, -1.0)
        first = np.stack([real, imag])
        return (np.stack([self._by_part(general), self._by_part(first)]) / self.length_x).astype(np.float32)

    def slot_twiddle(self):
        angle = 2 * np.pi * np.arange(self.groups)[:, None] * np.arange(lanes)[None, :] / self.length_x
        return np.stack([np.cos(angle), np.sin(angle)]).astype(np.float32)

    def source_matrix(self):
        count, deep = self.devices, self.deep
        index = np.arange(count)
        theta = 2 * np.pi * (index[:, None] * index[None, :] % count) / count
        cos, sin = np.cos(theta), np.sin(theta)
        out = np.zeros((count, 2, deep, 2, count, deep))
        for q in range(deep):
            out[:, 0, q, 0, :, q] = cos
            out[:, 1, q, 0, :, q] = sin
            out[:, 0, q, 1, :, q] = -sin
            out[:, 1, q, 1, :, q] = cos
        return out.reshape(count * 2 * deep, 2 * count * deep).astype(np.float32)

    def line_matrix(self):
        index = np.arange(self.cols)
        theta = 2 * np.pi * (index[:, None] * index[None, :] % self.cols) / self.cols
        cos, sin = np.cos(theta), np.sin(theta)
        return np.block([[cos, sin], [-sin, cos]]).astype(np.float32)

    def line_twiddle(self):
        angle = 2 * np.pi * np.arange(self.cols)[:, None] * np.arange(self.devices)[None, :] / self.length_y
        angle = np.repeat(angle, self.deep, axis=1)
        return np.stack([np.cos(angle), np.sin(angle)]).astype(np.float32)


def weighted(terms):
    groups = {}
    for coefficient, value in terms:
        size = round(abs(coefficient), 12)
        if size == 0.0:
            continue
        groups.setdefault(size, []).append((coefficient > 0, value))
    total = None
    for size, members in groups.items():
        members.sort(key=lambda member: not member[0])
        positive, part = members[0]
        for sign, value in members[1:]:
            part = part + value if sign == positive else part - value
        if size != 1.0:
            part = part * np.float32(size)
        if total is None:
            total = part if positive else -part
        else:
            total = total + part if positive else total - part
    return total


def radix_forward(values):
    count = len(values)
    half = count // 2
    even = [values[j] + values[count - j] for j in range(1, half)]
    odd = [values[j] - values[count - j] for j in range(1, half)]
    real, imag = [], []
    for g in range(half + 1):
        terms = [(1.0, values[0]), ((-1.0) ** g, values[half])]
        terms += [(math.cos(2 * math.pi * g * (j + 1) / count), even[j]) for j in range(half - 1)]
        real.append(weighted(terms))
        if 0 < g < half:
            imag.append(weighted([(-math.sin(2 * math.pi * g * (j + 1) / count), odd[j]) for j in range(half - 1)]))
    return real, imag


def radix_inverse(first, middle, real, imag):
    half = len(real) + 1
    count = 2 * half
    out = [None] * count
    for j in range(half + 1):
        terms = [(1.0, first), ((-1.0) ** j, middle)]
        terms += [(math.cos(2 * math.pi * g * j / count), real[g - 1]) for g in range(1, half)]
        together = weighted(terms)
        if j in (0, half):
            out[j] = together
            continue
        apart = weighted([(math.sin(2 * math.pi * g * j / count), imag[g - 1]) for g in range(1, half)])
        out[j] = together - apart
        out[count - j] = together + apart
    return out


def mul(a, b):
    return jnp.matmul(a, b, precision=highest)


def exchange_gx(value):
    count = lax.axis_size("gx")
    own = lax.axis_index("gx")
    if count > 8:
        return lax.all_to_all(value, "gx", split_axis=0, concat_axis=0, tiled=True)
    pieces = [lax.dynamic_index_in_dim(value, own, 0, False)]
    for step in range(1, count):
        piece = lax.dynamic_index_in_dim(value, own ^ step, 0, False)
        pieces.append(lax.ppermute(piece, "gx", [(k, k ^ step) for k in range(count)]))
    stacked = jnp.stack(pieces)
    return jnp.stack([lax.dynamic_index_in_dim(stacked, own ^ k, 0, False) for k in range(count)])


def exchange_all(value):
    return lax.all_to_all(value, ("gy", "gx"), split_axis=0, concat_axis=0, tiled=True)


def passed_along(value, axis, steps):
    count = lax.axis_size(axis)
    leading, last = (max(0, -steps), min(count, count - steps))
    return lax.ppermute(value, axis, [(source, source + steps) for source in range(leading, last)])


def forward_x(plan, lines):
    table = plan.slot_matrix()
    cos, sin = plan.slot_twiddle()
    real, imag = radix_forward([lines[:, n] for n in range(plan.radix)])
    blocks = [jnp.concatenate([real[0], real[plan.groups]], -1)]
    for g in range(1, plan.groups):
        re, im = real[g], imag[g - 1]
        blocks.append(jnp.concatenate([re * cos[g] + im * sin[g], im * cos[g] - re * sin[g]], -1))
    first = jnp.einsum("ok,fck->ofc", table[1], blocks[0], precision=highest)
    row = first[plan.deep, 0]
    first = first.at[plan.deep, 0].set(first[0, 1]).at[0, 1].set(row)
    rest = jnp.einsum("ok,gfck->ogfc", table[0], jnp.stack(blocks[1:]), precision=highest)
    spectrum = jnp.concatenate([first[:, None], rest], 1)
    spectrum = spectrum.reshape(plan.m_parts, plan.rows, plan.g_parts, -1)
    return spectrum.transpose(2, 0, 1, 3).reshape(plan.devices, plan.rows, -1)


def spectral_kernels(square):
    kappa = jnp.sqrt(square)
    damping = viscous * kappa
    across = 1.0 / (damping + buoyant + flexural * kappa**4)
    return damping, across


def wave_square(index, length):
    signed = jnp.where(2 * index >= length, index - length, index)
    wave = signed.astype(jnp.float32) * (2.0 * math.pi / length)
    return wave * wave


def middle_y(plan, received, position):
    deep, count, cols = plan.deep, plan.devices, plan.cols
    width = count * deep
    flat = received.reshape(count * plan.rows, -1).T
    mixed = mul(flat, plan.source_matrix())
    mixed = mixed.reshape(plan.own_groups, 2, cols, 2, width)
    cos, sin = plan.line_twiddle()
    re, im = mixed[:, :, :, 0], mixed[:, :, :, 1]
    turned = jnp.concatenate([re * cos + im * sin, im * cos - re * sin], 2)
    spectra = jnp.einsum("wk,gfkl->gfwl", plan.line_matrix(), turned, precision=highest)
    lane = lax.broadcasted_iota(jnp.int32, (1, width), 1)
    q, t = lane % deep, lane // deep
    w = lax.broadcasted_iota(jnp.int32, (cols, 1), 0)
    ky = wave_square(t + count * w, plan.length_y)
    m = (position % plan.m_parts) * deep + q
    base = (position // plan.m_parts) * plan.own_groups
    special = (position == 0) & (q == 0)
    results = []
    for group in range(plan.own_groups):
        g = base + group
        half = lanes // 2
        first = jnp.where(m < half, plan.radix * m, plan.radix // 2 + plan.radix * (m - half))
        index = jnp.where(g == 0, first, g + plan.radix * m)
        damping, across = spectral_kernels(wave_square(index, plan.length_x) + ky)
        u, v = spectra[group, 0], spectra[group, 1]
        ur, ui, vr, vi = u[:cols], u[cols:], v[:cols], v[cols:]
        out_r, out_i = across * (damping * ur - vr), across * (damping * ui - vi)
        if group == 0:
            out_r = jnp.where(special, across * (damping * ur - ui), out_r)
            out_i = jnp.where(special, across * (damping * ui + ur), out_i)
            damping, across = spectral_kernels(np.float32(math.pi) ** 2 + ky)
            extra = jnp.concatenate([across * (damping * vr - vi), across * (damping * vi + vr)], 0)
        results.append(jnp.concatenate([out_r, out_i], 0))
    results.append(extra)
    back = jnp.einsum("kw,gkl->gwl", plan.line_matrix() * np.float32(1.0 / plan.length_y), jnp.stack(results), precision=highest)
    re, im = back[:, :cols], back[:, cols:]
    turned = jnp.concatenate([re * cos - im * sin, im * cos + re * sin], 2)
    lines = jnp.einsum("gcl,sl->gcs", turned, plan.source_matrix(), precision=highest)
    place = lax.broadcasted_iota(jnp.int32, (1, count * plan.rows), 1)
    moved = (position == 0) & (place % plan.rows == deep)
    fixed = jnp.where(moved, jnp.roll(lines[-1], deep, axis=1), lines[0])
    lines = jnp.concatenate([fixed[None], lines[1:-1]], 0)
    return lines.reshape(plan.own_groups * cols, count * plan.rows).T.reshape(count, plan.rows, -1)


def inverse_x(plan, received):
    cols = plan.cols
    table = plan.slot_inverse()
    cos, sin = plan.slot_twiddle()
    split = received.reshape(plan.g_parts, 2 * lanes, plan.own_groups, cols)
    split = split.transpose(0, 2, 3, 1).reshape(plan.groups, cols, 2 * lanes)
    first = mul(split[0], table[1])
    rest = mul(split[1:], table[0])
    real, imag = [], []
    for g in range(1, plan.groups):
        re, im = rest[g - 1, :, :lanes], rest[g - 1, :, lanes:]
        real.append(re * cos[g] - im * sin[g])
        imag.append(im * cos[g] + re * sin[g])
    return radix_inverse(first[:, :lanes], first[:, lanes:], real, imag)


def to_lines(plan, field):
    split = field.reshape(plan.here, lanes, plan.gx, plan.cols)
    return split.transpose(2, 0, 3, 1)


def halves(value):
    high = value.astype(jnp.bfloat16)
    return high, (value - high.astype(jnp.float32)).astype(jnp.bfloat16)


def table_halves(table):
    high = table.astype(jnp.bfloat16)
    return np.stack([high, (table - high.astype(np.float32)).astype(jnp.bfloat16)])


def product(left, right, turned=False):
    dims = (((1,), (1 if turned else 0,)), ((), ()))

    def one(a, b):
        return lax.dot_general(a, b, dims, preferred_element_type=jnp.float32)

    return one(left[0], right[0]) + (one(left[0], right[1]) + one(left[1], right[0]))


def call(body, outs, scratch, scalars, *operands):
    scalar = pl.BlockSpec(memory_space=pltpu.SMEM)
    whole = pl.BlockSpec(memory_space=pltpu.VMEM)
    shapes = [jax.ShapeDtypeStruct(shape, jnp.float32) for shape in outs]
    run = pl.pallas_call(
        body,
        out_shape=shapes,
        in_specs=[scalar] * len(scalars) + [whole] * len(operands),
        out_specs=[whole] * len(outs),
        scratch_shapes=scratch,
        compiler_params=pltpu.CompilerParams(vmem_limit_bytes=48 << 20),
    )
    return run(*scalars, *operands)


def lines_out(plan, own, block, here, out_ref):
    turned = block.T
    for part in range(plan.gx):
        out_ref[own ^ part, here] = turned[part * plan.cols : (part + 1) * plan.cols]


def uplift_kernel(plan, own_ref, uplift_ref, flux_x_ref, flux_y_ref, out_ref, face_x_ref, face_y_ref):
    own = own_ref[0]
    size = flux_x_ref.shape[0]
    face_x_ref[...] = flux_x_ref[7:8, :]
    face_y_ref[...] = flux_y_ref[...].T[lanes - 1 : lanes, :]
    for here in range(plan.here):
        lines_out(plan, own, uplift_ref[here * lanes : (here + 1) * lanes, :], here, out_ref)


def send_uplift(plan, own, bed_uplift, flux_x, flux_y):
    rows, cols = bed_uplift.shape
    run = pl.pallas_call(
        lambda *refs: uplift_kernel(plan, *refs),
        grid=(1,),
        out_shape=[
            jax.ShapeDtypeStruct((plan.gx, plan.here, plan.cols, lanes), jnp.float32),
            jax.ShapeDtypeStruct((1, cols), jnp.float32),
            jax.ShapeDtypeStruct((1, rows), jnp.float32),
        ],
        in_specs=[
            pl.BlockSpec(memory_space=pltpu.SMEM),
            pl.BlockSpec((rows, cols), lambda i: (0, 0)),
            pl.BlockSpec((8, cols), lambda i: (rows // 8 - 1, 0)),
            pl.BlockSpec((rows, lanes), lambda i: (0, cols // lanes - 1)),
        ],
    )
    return run(own, bed_uplift, flux_x, flux_y)


def load_kernel(plan, own_ref, thick_ref, fx_ref, fy_ref, mb_ref, mask_ref, face_x_ref, face_y_ref, out_ref, line_ref):
    own = own_ref[0]
    for here in range(plan.here):
        rows = slice(here * lanes, (here + 1) * lanes)
        fx, fy = fx_ref[rows, :], fy_ref[rows, :]
        row = lax.broadcasted_iota(jnp.int32, fx.shape, 0)
        col = lax.broadcasted_iota(jnp.int32, fx.shape, 1)
        above = face_x_ref[...] if here == 0 else fx_ref[here * lanes - 1 : here * lanes, :]
        below = jnp.where(row == 0, jnp.broadcast_to(above, fx.shape), pltpu.roll(fx, 1, 0))
        side = jnp.broadcast_to(face_y_ref[:, rows], (lanes, lanes)).T
        left = jnp.where(col == 0, jnp.concatenate([side] * (fx.shape[1] // lanes), 1), pltpu.roll(fy, 1, 1))
        divergence = fx - below + fy - left
        thick, mask = thick_ref[rows, :], mask_ref[rows, :]
        trial = thick + time_step * (mb_ref[rows, :] - divergence)
        new = jnp.where(mask == 2, 0.0, jnp.maximum(trial, 0.0))
        out_ref[rows, :] = new
        lines_out(plan, own, jnp.where(mask == 0, new - thick, 0.0), here, line_ref)


def forward_kernel(plan, own_ref, *refs):
    pieces, (twiddle_ref, table_ref, out_ref, line_ref, high_ref, low_ref) = refs[:-6], refs[-6:]
    own = own_ref[0]
    cols, radix, groups, here = plan.cols, plan.radix, plan.groups, plan.here
    step_rows = 16
    for field in range(2):
        for step in range(plan.gx):
            piece = pieces[field * plan.gx + step]
            for a in range(here):
                line_ref[(own ^ step) * here + a] = piece[a]

        def chunk(index, carry, field=field):
            row = pl.multiple_of(index * step_rows, step_rows)
            real, imag = radix_forward([line_ref[n, pl.ds(row, step_rows), :] for n in range(radix)])
            for g in range(groups):
                if g == 0:
                    first, second = real[0], real[groups]
                else:
                    cos, sin = twiddle_ref[0, g : g + 1, :], twiddle_ref[1, g : g + 1, :]
                    first = real[g] * cos + imag[g - 1] * sin
                    second = imag[g - 1] * cos - real[g] * sin
                high, low = halves(jnp.concatenate([first, second], 1))
                place = pl.ds((2 * g + field) * cols + row, step_rows)
                high_ref[place, :] = high
                low_ref[place, :] = low
            return carry

        lax.fori_loop(0, cols // step_rows, chunk, 0)

    general = (table_ref[0, 0], table_ref[0, 1])
    special = (table_ref[1, 0], table_ref[1, 1])
    edge = 2 * cols
    starts = []
    for start in range(0, 2 * groups * cols, lanes):
        rows = slice(start, start + lanes)
        data = (high_ref[rows, :], low_ref[rows, :])
        if start + lanes <= edge:
            out = product(special, data, True)
        else:
            out = product(general, data, True)
            if start < edge:
                lane = lax.broadcasted_iota(jnp.int32, out.shape, 1)
                out = jnp.where(lane < edge - start, product(special, data, True), out)
        out_ref[:, :, start : start + lanes] = out.reshape(plan.devices, plan.rows, lanes)
    size = 2 * lanes
    block = out_ref[0, :, :size]
    row = lax.broadcasted_iota(jnp.int32, block.shape, 0)
    lane = lax.broadcasted_iota(jnp.int32, block.shape, 1)
    swapped = pltpu.roll(block, plan.deep, 0)
    to_left, to_right = pltpu.roll(swapped, size - cols, 1), pltpu.roll(swapped, cols, 1)
    block = jnp.where((row == plan.deep) & (lane < cols), to_left, block)
    block = jnp.where((row == 0) & (lane >= cols) & (lane < 2 * cols), to_right, block)
    out_ref[0, :, :size] = block


def middle_kernel(plan, position_ref, in_ref, t1_ref, t2_ref, t2i_ref, t1i_ref, twiddle_ref, out_ref, high_ref, low_ref, back_high, back_low, turn_ref):
    position = position_ref[0]
    cols, groups, deep, count = plan.cols, plan.groups, plan.deep, plan.devices
    width, size = lanes, 2 * lanes
    for start in range(0, 2 * groups * cols, lanes):
        block = in_ref[:, :, start : start + lanes].reshape(size, lanes).T
        high_ref[start : start + lanes, :], low_ref[start : start + lanes, :] = halves(block)
    t1 = (t1_ref[0], t1_ref[1])
    t2 = (t2_ref[0], t2_ref[1])
    t2i = (t2i_ref[0], t2i_ref[1])
    t1i = (t1i_ref[0], t1i_ref[1])
    cos, sin = twiddle_ref[0], twiddle_ref[1]
    lane = lax.broadcasted_iota(jnp.int32, (1, width), 1)
    q, t = lane % deep, lane // deep
    w = lax.broadcasted_iota(jnp.int32, (cols, width), 0)
    ky = wave_square(t + count * w, plan.length_y)
    m = position * deep + q
    special = jnp.broadcast_to((position == 0) & (q == 0), (cols, width))
    results = []
    for g in range(groups):
        rows = slice(2 * g * cols, 2 * (g + 1) * cols)
        mixed = product((high_ref[rows, :], low_ref[rows, :]), t1)
        sides = []
        for field in range(2):
            part = mixed[field * cols : (field + 1) * cols]
            re, im = part[:, :width], part[:, width:]
            sides.append(jnp.concatenate([re * cos + im * sin, im * cos - re * sin], 0))
        spectra = product(t2, halves(jnp.concatenate(sides, 1)))
        ur, vr = spectra[:cols, :width], spectra[:cols, width:]
        ui, vi = spectra[cols:, :width], spectra[cols:, width:]
        half = lanes // 2
        if g == 0:
            index = jnp.where(m < half, plan.radix * m, plan.radix // 2 + plan.radix * (m - half))
        else:
            index = g + plan.radix * m
        damping, across = spectral_kernels(wave_square(index, plan.length_x) + ky)
        out_r, out_i = across * (damping * ur - vr), across * (damping * ui - vi)
        if g == 0:
            out_r = jnp.where(special, across * (damping * ur - ui), out_r)
            out_i = jnp.where(special, across * (damping * ui + ur), out_i)
            damping, across = spectral_kernels(np.float32(math.pi) ** 2 + ky)
            extra = jnp.concatenate([across * (damping * vr - vi), across * (damping * vi + vr)], 0)
        results.append(jnp.concatenate([out_r, out_i], 0))
    results.append(extra)
    for g in range(0, groups + 1, 2):
        pair = results[g : g + 2]
        back = product(t2i, halves(jnp.concatenate(pair, 1)))
        for k in range(len(pair)):
            re, im = back[:cols, k * width : (k + 1) * width], back[cols:, k * width : (k + 1) * width]
            turned = jnp.concatenate([re * cos - im * sin, im * cos + re * sin], 1)
            place = slice((g + k) * cols, (g + k + 1) * cols)
            back_high[place, :], back_low[place, :] = halves(turned)
    last = slice(groups * cols, (groups + 1) * cols)
    extra = product((back_high[last, :], back_low[last, :]), t1i)
    place = lax.broadcasted_iota(jnp.int32, (cols, size), 1)
    moved = (position == 0) & (place % plan.rows == deep)
    for g in range(groups):
        rows = slice(g * cols, (g + 1) * cols)
        lines = product((back_high[rows, :], back_low[rows, :]), t1i)
        if g == 0:
            lines = jnp.where(moved, pltpu.roll(extra, deep, 1), lines)
        turn_ref[rows, :] = lines
    for start in range(0, groups * cols, lanes):
        block = turn_ref[start : start + lanes, :].T
        keep = min(lanes, groups * cols - start)
        out_ref[:, :, start : start + keep] = block.reshape(count, plan.rows, lanes)[:, :, :keep]


def inverse_kernel(plan, own_ref, in_ref, twiddle_ref, table_ref, out_ref, turn_ref, mid_ref):
    own = own_ref[0]
    cols, groups, here = plan.cols, plan.groups, plan.here
    size = 2 * lanes
    total = groups * cols
    for start in range(0, total, lanes):
        keep = min(lanes, total - start)
        block = in_ref[:, :, start : start + keep].reshape(size, keep)
        turn_ref[start : start + keep, :] = block.T
    for g in range(groups):
        rows = slice(g * cols, (g + 1) * cols)
        kind = 1 if g == 0 else 0
        mid_ref[rows, :] = product(halves(turn_ref[rows, :]), (table_ref[kind, 0], table_ref[kind, 1]))
    step_rows = 16

    def chunk(index, carry):
        row = pl.multiple_of(index * step_rows, step_rows)
        real, imag = [], []
        for g in range(1, groups):
            place = pl.ds(g * cols + row, step_rows)
            re, im = mid_ref[place, :lanes], mid_ref[place, lanes:]
            cos, sin = twiddle_ref[0, g : g + 1, :], twiddle_ref[1, g : g + 1, :]
            real.append(re * cos - im * sin)
            imag.append(im * cos + re * sin)
        place = pl.ds(row, step_rows)
        values = radix_inverse(mid_ref[place, :lanes], mid_ref[place, lanes:], real, imag)
        for n, value in enumerate(values):
            out_ref[own ^ (n // here), n % here, place, :] = value
        return carry

    lax.fori_loop(0, cols // step_rows, chunk, 0)


def final_kernel(plan, own_ref, *refs):
    pieces, (out_ref, line_ref) = refs[:-2], refs[-2:]
    own = own_ref[0]
    for step in range(plan.gx):
        start = pl.multiple_of((own ^ step) * plan.cols, 8)
        for a in range(plan.here):
            line_ref[a, pl.ds(start, plan.cols), :] = pieces[step][a]
    for a in range(plan.here):
        out_ref[a * lanes : (a + 1) * lanes, :] = line_ref[a].T


def swap_gx(plan, pieces):
    got = [pieces[0]]
    for step in range(1, plan.gx):
        got.append(lax.ppermute(pieces[step], "gx", [(k, k ^ step) for k in range(plan.gx)]))
    return got


def build_kernels(plan):
    vmem, f32, bf16 = pltpu.VMEM, jnp.float32, jnp.bfloat16
    size, cols, groups = 2 * lanes, plan.cols, plan.groups
    piece_shape = (plan.gx, plan.here, cols, lanes)

    def local(thickness, bed_uplift, flux_x, flux_y, mass_balance, ice_mask):
        own = lax.axis_index("gx").reshape(1)
        position = (lax.axis_index("gy") * plan.gx + lax.axis_index("gx")).reshape(1)
        uplift, face_x, face_y = send_uplift(plan, own, bed_uplift, flux_x, flux_y)
        lower_face = passed_along(face_x, "gx", 1)
        left_face = passed_along(face_y, "gy", 1)
        lines_u = swap_gx(plan, uplift)
        thickness_new, load = call(
            lambda *refs: load_kernel(plan, *refs),
            [thickness.shape, piece_shape],
            [],
            [own],
            *(thickness, flux_x, flux_y, mass_balance, ice_mask, lower_face, left_face),
        )
        lines_v = swap_gx(plan, load)
        twiddle = plan.slot_twiddle()
        forward = np.stack([table_halves(table) for table in plan.slot_matrix()])
        (spectrum,) = call(
            lambda *refs: forward_kernel(plan, *refs),
            [(plan.devices, plan.rows, 2 * groups * cols)],
            [vmem((plan.radix, cols, lanes), f32)] + [vmem((2 * groups * cols, size), bf16)] * 2,
            [own],
            *(lines_u + lines_v + [twiddle, forward]),
        )
        received = exchange_all(spectrum)
        source, line = plan.source_matrix(), plan.line_matrix()
        scale = np.float32(1.0 / plan.length_y)
        tables = [table_halves(table) for table in (source, line, line.T * scale, source.T)]
        (middle,) = call(
            lambda *refs: middle_kernel(plan, *refs),
            [(plan.devices, plan.rows, groups * cols)],
            [vmem((2 * groups * cols, size), bf16)] * 2 + [vmem(((groups + 1) * cols, size), bf16)] * 2 + [vmem(((groups + 1) * cols, size), f32)],
            [position],
            *([received] + tables + [plan.line_twiddle()]),
        )
        back = exchange_all(middle)
        inverse = np.stack([table_halves(table) for table in plan.slot_inverse()])
        (bed,) = call(
            lambda *refs: inverse_kernel(plan, *refs),
            [piece_shape],
            [vmem((groups * cols, size), f32)] * 2,
            [own],
            *(back, twiddle, inverse),
        )
        (bed_new,) = call(
            lambda *refs: final_kernel(plan, *refs),
            [thickness.shape],
            [vmem((plan.here, plan.gx * cols, lanes), f32)],
            [own],
            *swap_gx(plan, bed),
        )
        return thickness_new, bed_new

    return local


def build(plan):
    if plan.devices * plan.rows == 2 * lanes and plan.cols % 16 == 0 and plan.radix <= 16 and plan.gx in (2, 4, 8):
        return build_kernels(plan)

    def local(thickness, bed_uplift, flux_x, flux_y, mass_balance, ice_mask):
        lower_face = passed_along(flux_x[-1:, :], "gx", 1)
        left_face = passed_along(flux_y[:, -1:], "gy", 1)
        flux_below = jnp.concatenate([lower_face, flux_x[:-1, :]], axis=0)
        flux_left = jnp.concatenate([left_face, flux_y[:, :-1]], axis=1)
        divergence = flux_x - flux_below + flux_y - flux_left
        trial = thickness + time_step * (mass_balance - divergence)
        thickness_new = jnp.where(ice_mask == 2, 0.0, jnp.maximum(trial, 0.0))
        load = jnp.where(ice_mask == 0, thickness_new - thickness, 0.0)
        fields = jnp.stack([to_lines(plan, bed_uplift), to_lines(plan, load)], 1)
        lines = exchange_gx(fields)
        lines = lines.transpose(1, 0, 2, 3, 4).reshape(2, plan.radix, plan.cols, lanes)
        received = exchange_all(forward_x(plan, lines))
        position = lax.axis_index("gy") * plan.gx + lax.axis_index("gx")
        back = exchange_all(middle_y(plan, received, position))
        bed = inverse_x(plan, back)
        bed = jnp.stack(bed).reshape(plan.gx, plan.here, plan.cols, lanes)
        bed = exchange_gx(bed)
        bed_new = bed.transpose(1, 3, 0, 2).reshape(plan.here * lanes, plan.gx * plan.cols)
        return thickness_new, bed_new

    return local


def solution(mesh):
    spec = P("gx", "gy")

    def step(*args):
        length_x, length_y = args[0].shape
        plan = Plan(mesh, length_x, length_y)
        body = jax.shard_map(build(plan), mesh=mesh, in_specs=(spec,) * 6, out_specs=(spec, spec), check_vma=False)
        return body(*args)

    return step
```

```python
import math

import jax
import jax.numpy as jnp
import numpy as np
from jax import lax
from jax.experimental import pallas as pl
from jax.experimental.pallas import tpu as pltpu
from jax.sharding import PartitionSpec as P

time_step = 0.5
viscous = 4.0
buoyant = 0.01
flexural = 50.0
lanes = 128
highest = lax.Precision.HIGHEST


class Plan:
    def __init__(self, mesh, length_x, length_y):
        self.gx, self.gy = mesh.shape["gx"], mesh.shape["gy"]
        self.devices = self.gx * self.gy
        self.length_x, self.length_y = length_x, length_y
        self.radix = length_x // lanes
        self.here = self.radix // self.gx
        self.groups = self.radix // 2
        self.cols = length_y // self.devices
        self.m_parts = min(self.devices, lanes)
        self.g_parts = self.devices // self.m_parts
        self.deep = lanes // self.m_parts
        self.own_groups = self.groups // self.g_parts
        self.rows = 2 * self.deep
        self.tail = -(-(2 + 2 * self.here) // 8) * 8
        self.piece_rows = self.here * self.cols + self.tail

    def slot_matrix(self):
        n2 = np.arange(lanes)[None, :]
        m = np.arange(lanes)[:, None]
        theta = 2 * np.pi * (m * n2 % lanes) / lanes
        cos, sin = np.cos(theta), np.sin(theta)
        general = np.stack([np.concatenate([cos, sin], 1), np.concatenate([-sin, cos], 1)])
        half = lanes // 2
        turned = 2 * np.pi * ((2 * (m - half) + 1) * n2 % (2 * lanes)) / (2 * lanes)
        low = np.arange(lanes)[:, None] < half
        real = np.concatenate([np.where(low, cos, 0), np.where(low, 0, np.cos(turned))], 1)
        imag = np.concatenate([np.where(low, -sin, 0), np.where(low, 0, -np.sin(turned))], 1)
        imag[0, :lanes] = np.where(np.arange(lanes) % 2 == 0, 1.0, -1.0)
        first = np.stack([real, imag])
        return np.stack([self._by_part(general), self._by_part(first)]).astype(np.float32)

    def _by_part(self, table):
        split = table.reshape(2, self.m_parts, self.deep, 2 * lanes)
        return split.transpose(1, 0, 2, 3).reshape(2 * lanes, 2 * lanes)

    def slot_inverse(self):
        m = np.arange(lanes)[:, None]
        n2 = np.arange(lanes)[None, :]
        theta = 2 * np.pi * (m * n2 % lanes) / lanes
        cos, sin = np.cos(theta), np.sin(theta)
        general = 2 * np.stack([np.concatenate([cos, sin], 1), np.concatenate([-sin, cos], 1)])
        half = lanes // 2
        turned = 2 * np.pi * ((2 * (m - half) + 1) * n2 % (2 * lanes)) / (2 * lanes)
        low = m < half
        real = 2 * np.concatenate([np.where(low, cos, 0), np.where(low, 0, np.cos(turned))], 1)
        imag = 2 * np.concatenate([np.where(low, -sin, 0), np.where(low, 0, -np.sin(turned))], 1)
        real[0, :lanes] = 1.0
        imag[0, :lanes] = np.where(np.arange(lanes) % 2 == 0, 1.0, -1.0)
        first = np.stack([real, imag])
        return (np.stack([self._by_part(general), self._by_part(first)]) / self.length_x).astype(np.float32)

    def slot_twiddle(self):
        angle = 2 * np.pi * np.arange(self.groups)[:, None] * np.arange(lanes)[None, :] / self.length_x
        return np.stack([np.cos(angle), np.sin(angle)]).astype(np.float32)

    def source_matrix(self):
        count, deep = self.devices, self.deep
        index = np.arange(count)
        theta = 2 * np.pi * (index[:, None] * index[None, :] % count) / count
        cos, sin = np.cos(theta), np.sin(theta)
        out = np.zeros((count, 2, deep, 2, count, deep))
        for q in range(deep):
            out[:, 0, q, 0, :, q] = cos
            out[:, 1, q, 0, :, q] = sin
            out[:, 0, q, 1, :, q] = -sin
            out[:, 1, q, 1, :, q] = cos
        return out.reshape(count * 2 * deep, 2 * count * deep).astype(np.float32)

    def line_matrix(self):
        index = np.arange(self.cols)
        theta = 2 * np.pi * (index[:, None] * index[None, :] % self.cols) / self.cols
        cos, sin = np.cos(theta), np.sin(theta)
        return np.block([[cos, sin], [-sin, cos]]).astype(np.float32)

    def line_twiddle(self):
        angle = 2 * np.pi * np.arange(self.cols)[:, None] * np.arange(self.devices)[None, :] / self.length_y
        angle = np.repeat(angle, self.deep, axis=1)
        return np.stack([np.cos(angle), np.sin(angle)]).astype(np.float32)


def weighted(terms):
    groups = {}
    for coefficient, value in terms:
        size = round(abs(coefficient), 12)
        if size == 0.0:
            continue
        groups.setdefault(size, []).append((coefficient > 0, value))
    total = None
    for size, members in groups.items():
        members.sort(key=lambda member: not member[0])
        positive, part = members[0]
        for sign, value in members[1:]:
            part = part + value if sign == positive else part - value
        if size != 1.0:
            part = part * np.float32(size)
        if total is None:
            total = part if positive else -part
        else:
            total = total + part if positive else total - part
    return total


def radix_forward(values):
    count = len(values)
    half = count // 2
    even = [values[j] + values[count - j] for j in range(1, half)]
    odd = [values[j] - values[count - j] for j in range(1, half)]
    real, imag = [], []
    for g in range(half + 1):
        terms = [(1.0, values[0]), ((-1.0) ** g, values[half])]
        terms += [(math.cos(2 * math.pi * g * (j + 1) / count), even[j]) for j in range(half - 1)]
        real.append(weighted(terms))
        if 0 < g < half:
            imag.append(weighted([(-math.sin(2 * math.pi * g * (j + 1) / count), odd[j]) for j in range(half - 1)]))
    return real, imag


def radix_inverse(first, middle, real, imag):
    half = len(real) + 1
    count = 2 * half
    out = [None] * count
    for j in range(half + 1):
        terms = [(1.0, first), ((-1.0) ** j, middle)]
        terms += [(math.cos(2 * math.pi * g * j / count), real[g - 1]) for g in range(1, half)]
        together = weighted(terms)
        if j in (0, half):
            out[j] = together
            continue
        apart = weighted([(math.sin(2 * math.pi * g * j / count), imag[g - 1]) for g in range(1, half)])
        out[j] = together - apart
        out[count - j] = together + apart
    return out


def mul(a, b):
    return jnp.matmul(a, b, precision=highest)


def exchange_gx(value):
    count = lax.axis_size("gx")
    own = lax.axis_index("gx")
    if count > 8:
        return lax.all_to_all(value, "gx", split_axis=0, concat_axis=0, tiled=True)
    pieces = [lax.dynamic_index_in_dim(value, own, 0, False)]
    for step in range(1, count):
        piece = lax.dynamic_index_in_dim(value, own ^ step, 0, False)
        pieces.append(lax.ppermute(piece, "gx", [(k, k ^ step) for k in range(count)]))
    stacked = jnp.stack(pieces)
    return jnp.stack([lax.dynamic_index_in_dim(stacked, own ^ k, 0, False) for k in range(count)])


def exchange_all(value):
    return lax.all_to_all(value, ("gy", "gx"), split_axis=0, concat_axis=0, tiled=True)


def passed_along(value, axis, steps):
    count = lax.axis_size(axis)
    leading, last = (max(0, -steps), min(count, count - steps))
    return lax.ppermute(value, axis, [(source, source + steps) for source in range(leading, last)])


def forward_x(plan, lines):
    table = plan.slot_matrix()
    cos, sin = plan.slot_twiddle()
    real, imag = radix_forward([lines[:, n] for n in range(plan.radix)])
    blocks = [jnp.concatenate([real[0], real[plan.groups]], -1)]
    for g in range(1, plan.groups):
        re, im = real[g], imag[g - 1]
        blocks.append(jnp.concatenate([re * cos[g] + im * sin[g], im * cos[g] - re * sin[g]], -1))
    first = jnp.einsum("ok,fck->ofc", table[1], blocks[0], precision=highest)
    row = first[plan.deep, 0]
    first = first.at[plan.deep, 0].set(first[0, 1]).at[0, 1].set(row)
    rest = jnp.einsum("ok,gfck->ogfc", table[0], jnp.stack(blocks[1:]), precision=highest)
    spectrum = jnp.concatenate([first[:, None], rest], 1)
    spectrum = spectrum.reshape(plan.m_parts, plan.rows, plan.g_parts, -1)
    return spectrum.transpose(2, 0, 1, 3).reshape(plan.devices, plan.rows, -1)


def spectral_kernels(square):
    kappa = jnp.sqrt(square)
    damping = viscous * kappa
    across = 1.0 / (damping + buoyant + flexural * kappa**4)
    return damping, across


def wave_square(index, length):
    signed = jnp.where(2 * index >= length, index - length, index)
    wave = signed.astype(jnp.float32) * (2.0 * math.pi / length)
    return wave * wave


def middle_y(plan, received, position):
    deep, count, cols = plan.deep, plan.devices, plan.cols
    width = count * deep
    flat = received.reshape(count * plan.rows, -1).T
    mixed = mul(flat, plan.source_matrix())
    mixed = mixed.reshape(plan.own_groups, 2, cols, 2, width)
    cos, sin = plan.line_twiddle()
    re, im = mixed[:, :, :, 0], mixed[:, :, :, 1]
    turned = jnp.concatenate([re * cos + im * sin, im * cos - re * sin], 2)
    spectra = jnp.einsum("wk,gfkl->gfwl", plan.line_matrix(), turned, precision=highest)
    lane = lax.broadcasted_iota(jnp.int32, (1, width), 1)
    q, t = lane % deep, lane // deep
    w = lax.broadcasted_iota(jnp.int32, (cols, 1), 0)
    ky = wave_square(t + count * w, plan.length_y)
    m = (position % plan.m_parts) * deep + q
    base = (position // plan.m_parts) * plan.own_groups
    special = (position == 0) & (q == 0)
    results = []
    for group in range(plan.own_groups):
        g = base + group
        half = lanes // 2
        first = jnp.where(m < half, plan.radix * m, plan.radix // 2 + plan.radix * (m - half))
        index = jnp.where(g == 0, first, g + plan.radix * m)
        damping, across = spectral_kernels(wave_square(index, plan.length_x) + ky)
        u, v = spectra[group, 0], spectra[group, 1]
        ur, ui, vr, vi = u[:cols], u[cols:], v[:cols], v[cols:]
        out_r, out_i = across * (damping * ur - vr), across * (damping * ui - vi)
        if group == 0:
            out_r = jnp.where(special, across * (damping * ur - ui), out_r)
            out_i = jnp.where(special, across * (damping * ui + ur), out_i)
            damping, across = spectral_kernels(np.float32(math.pi) ** 2 + ky)
            extra = jnp.concatenate([across * (damping * vr - vi), across * (damping * vi + vr)], 0)
        results.append(jnp.concatenate([out_r, out_i], 0))
    results.append(extra)
    back = jnp.einsum("kw,gkl->gwl", plan.line_matrix() * np.float32(1.0 / plan.length_y), jnp.stack(results), precision=highest)
    re, im = back[:, :cols], back[:, cols:]
    turned = jnp.concatenate([re * cos - im * sin, im * cos + re * sin], 2)
    lines = jnp.einsum("gcl,sl->gcs", turned, plan.source_matrix(), precision=highest)
    place = lax.broadcasted_iota(jnp.int32, (1, count * plan.rows), 1)
    moved = (position == 0) & (place % plan.rows == deep)
    fixed = jnp.where(moved, jnp.roll(lines[-1], deep, axis=1), lines[0])
    lines = jnp.concatenate([fixed[None], lines[1:-1]], 0)
    return lines.reshape(plan.own_groups * cols, count * plan.rows).T.reshape(count, plan.rows, -1)


def inverse_x(plan, received):
    cols = plan.cols
    table = plan.slot_inverse()
    cos, sin = plan.slot_twiddle()
    split = received.reshape(plan.g_parts, 2 * lanes, plan.own_groups, cols)
    split = split.transpose(0, 2, 3, 1).reshape(plan.groups, cols, 2 * lanes)
    first = mul(split[0], table[1])
    rest = mul(split[1:], table[0])
    real, imag = [], []
    for g in range(1, plan.groups):
        re, im = rest[g - 1, :, :lanes], rest[g - 1, :, lanes:]
        real.append(re * cos[g] - im * sin[g])
        imag.append(im * cos[g] + re * sin[g])
    return radix_inverse(first[:, :lanes], first[:, lanes:], real, imag)


def to_lines(plan, field):
    split = field.reshape(plan.here, lanes, plan.gx, plan.cols)
    return split.transpose(2, 0, 3, 1)


def halves(value):
    high = value.astype(jnp.bfloat16)
    return high, (value - high.astype(jnp.float32)).astype(jnp.bfloat16)


def table_halves(table):
    high = table.astype(jnp.bfloat16)
    return np.stack([high, (table - high.astype(np.float32)).astype(jnp.bfloat16)])


def product(left, right, turned=False):
    dims = (((1,), (1 if turned else 0,)), ((), ()))

    def one(a, b):
        return lax.dot_general(a, b, dims, preferred_element_type=jnp.float32)

    return one(left[0], right[0]) + (one(left[0], right[1]) + one(left[1], right[0]))


def call(body, outs, scratch, scalars, *operands):
    scalar = pl.BlockSpec(memory_space=pltpu.SMEM)
    whole = pl.BlockSpec(memory_space=pltpu.VMEM)
    run = pl.pallas_call(
        body,
        out_shape=outs,
        in_specs=[scalar] * len(scalars) + [whole] * len(operands),
        out_specs=[whole] * len(outs),
        scratch_shapes=scratch,
        compiler_params=pltpu.CompilerParams(vmem_limit_bytes=16 << 20),
    )
    return run(*scalars, *operands)


def real_array(*shape):
    return jax.ShapeDtypeStruct(shape, jnp.float32)


def lines_out(plan, own, block, here, turned_ref, out_refs):
    turned_ref[here] = block.T
    for step in range(plan.gx):
        start = pl.multiple_of((own ^ step) * plan.cols, 8)
        out_refs[step][here * plan.cols : (here + 1) * plan.cols, :] = turned_ref[here, pl.ds(start, plan.cols), :]


def own_part(plan, part, row):
    wide = jnp.concatenate([row, row[:, :lanes]], 1)
    wide = jnp.broadcast_to(wide, (8, wide.shape[1]))
    out = wide[:, :lanes]
    for k in range(1, plan.gx):
        start = k * plan.cols
        low = start // lanes * lanes
        block = wide[:, low : low + 2 * lanes]
        if start % lanes:
            block = pltpu.roll(block, 2 * lanes - start % lanes, 1)
        out = jnp.where(part == k, block[:, :lanes], out)
    return out[:1]


def kernel_call(body, outs, scratch, scalars, inputs, faces=()):
    whole = pl.BlockSpec(memory_space=pltpu.VMEM)
    run = pl.pallas_call(
        body,
        out_shape=outs,
        in_specs=[pl.BlockSpec(memory_space=pltpu.SMEM)] * len(scalars) + [pl.BlockSpec(memory_space=pl.ANY)] * len(inputs) + [whole] * len(faces),
        out_specs=[whole] * len(outs),
        scratch_shapes=scratch,
    )
    return run(*scalars, *inputs, *faces)


def uplift_kernel(plan, own_ref, uplift_hbm, flux_x_hbm, flux_y_hbm, *refs):
    own = own_ref[0]
    out_refs = refs[: plan.gx]
    field_ref, turned_ref, last_x_ref, last_y_ref, sems = refs[plan.gx :]
    rows, cols = uplift_hbm.shape
    copies = [
        pltpu.make_async_copy(flux_x_hbm.at[pl.ds(rows - 8, 8), :], last_x_ref, sems.at[0]),
        pltpu.make_async_copy(flux_y_hbm.at[:, pl.ds(cols - lanes, lanes)], last_y_ref, sems.at[1]),
    ]
    for here in range(plan.here):
        source = uplift_hbm.at[pl.ds(here * lanes, lanes), :]
        copies.append(pltpu.make_async_copy(source, field_ref.at[here], sems.at[2 + here]))
    for copy in copies:
        copy.start()
    for here in range(plan.here):
        copies[2 + here].wait()
        lines_out(plan, own, field_ref[here], here, turned_ref, out_refs)
    copies[0].wait()
    last_x = last_x_ref[7:8, :]
    copies[1].wait()
    last_y = last_y_ref[...].T[lanes - 1 : lanes, :]
    tail = plan.here * plan.cols
    parts = [last[:, a * lanes : (a + 1) * lanes] for last in (last_x, last_y) for a in range(plan.here)]
    parts.append(jnp.zeros((plan.tail - 2 * plan.here, lanes), jnp.float32))
    parts = jnp.concatenate(parts, 0)
    for step in range(plan.gx):
        out_refs[step][tail : tail + plan.tail, :] = parts


def send_uplift(plan, own, bed_uplift, flux_x, flux_y):
    rows, cols = bed_uplift.shape
    return kernel_call(
        lambda *refs: uplift_kernel(plan, *refs),
        [real_array(plan.piece_rows, lanes)] * plan.gx,
        [
            pltpu.VMEM((plan.here, lanes, cols), jnp.float32),
            pltpu.VMEM((plan.here, cols, lanes), jnp.float32),
            pltpu.VMEM((8, cols), jnp.float32),
            pltpu.VMEM((rows, lanes), jnp.float32),
            pltpu.SemaphoreType.DMA((2 + plan.here,)),
        ],
        [own],
        (bed_uplift, flux_x, flux_y),
    )


def fetch_fields(plan, sources, mask_ref, floats_ref, sems):
    targets = [floats_ref.at[k] for k in range(4)] + [mask_ref]
    copies = []
    for here in range(plan.here):
        rows = pl.ds(here * lanes, lanes)
        group = [
            pltpu.make_async_copy(source.at[rows, :], target.at[rows, :], sems.at[here, k])
            for k, (source, target) in enumerate(zip(sources, targets))
        ]
        for copy in group:
            copy.start()
        copies.append(group)
    return copies


def trial_block(floats_ref, here, above, left_edge):
    rows = slice(here * lanes, (here + 1) * lanes)
    fx, fy = floats_ref[1, rows, :], floats_ref[2, rows, :]
    row = lax.broadcasted_iota(jnp.int32, fx.shape, 0)
    col = lax.broadcasted_iota(jnp.int32, fx.shape, 1)
    if here:
        above = floats_ref[1, here * lanes - 1 : here * lanes, :]
    below = jnp.where(row == 0, jnp.broadcast_to(above, fx.shape) if here or above.ndim else above, pltpu.roll(fx, 1, 0))
    left = jnp.where(col == 0, left_edge, pltpu.roll(fy, 1, 1))
    divergence = fx - below + fy - left
    return floats_ref[0, rows, :] + time_step * (floats_ref[3, rows, :] - divergence)


hidden = np.float32(-1e30)


def load_kernel(plan, own_ref, *refs):
    own = own_ref[0]
    sources, refs = refs[:5], refs[5:]
    line_refs, (mask_ref, floats_ref, turned_ref, sems) = refs[: plan.gx], refs[plan.gx :]
    copies = fetch_fields(plan, sources, mask_ref, floats_ref, sems)
    columns_trial, columns_thick = [], []
    for here in range(plan.here):
        for copy in copies[here]:
            copy.wait()
        rows = slice(here * lanes, (here + 1) * lanes)
        trial = trial_block(floats_ref, here, jnp.float32(0.0), 0.0)
        free = mask_ref[rows, :] == 0
        thick = jnp.where(free, floats_ref[0, rows, :], 0.0)
        trial = jnp.where(free, trial, hidden)
        lines_out(plan, own, jnp.maximum(trial, 0.0) - thick, here, turned_ref, line_refs)
        lane = lax.broadcasted_iota(jnp.int32, (lanes, lanes), 1)
        packed = jnp.where(lane == 0, trial[:, :lanes], pltpu.roll(thick[:, :lanes], 1, 1)).T
        columns_trial.append(packed[0:1])
        columns_thick.append(packed[1:2])
        if here == 0:
            row_trial, row_thick = trial[0:1], thick[0:1]
    tail = plan.here * plan.cols
    rest = plan.tail - 2 - 2 * plan.here
    for step in range(plan.gx):
        parts = [own_part(plan, own ^ step, row_trial), own_part(plan, own ^ step, row_thick)] + columns_trial + columns_thick
        if rest:
            parts.append(jnp.zeros((rest, lanes), jnp.float32))
        line_refs[step][tail : tail + plan.tail, :] = jnp.concatenate(parts, 0)


def field_scratch(shape):
    return [
        pltpu.VMEM(shape, jnp.int32),
        pltpu.VMEM((4,) + shape, jnp.float32),
    ]


def make_load(plan, own, fields):
    shape = fields[0].shape
    scratch = field_scratch(shape) + [
        pltpu.VMEM((plan.here, shape[1], lanes), jnp.float32),
        pltpu.SemaphoreType.DMA((plan.here, 5)),
    ]
    outs = [real_array(plan.piece_rows, lanes)] * plan.gx
    return kernel_call(lambda *refs: load_kernel(plan, *refs), outs, scratch, [own], fields)


def row_above(plan, own, block, tails):
    above = [jnp.zeros((1, lanes), jnp.float32)] * plan.here
    for step in range(plan.gx):
        match = (own ^ step) + 1 == block
        above = [jnp.where(match, tails[step][a : a + 1, :], above[a]) for a in range(plan.here)]
    return jnp.concatenate(above, 1)


def thickness_kernel(plan, own_ref, *refs):
    own = own_ref[0]
    sources, (tails_ref, side_ref, out_ref, mask_ref, floats_ref, sems) = refs[:5], refs[5:]
    copies = fetch_fields(plan, sources, mask_ref, floats_ref, sems)
    above = row_above(plan, own, own, [tails_ref[step] for step in range(plan.gx)])
    for here in range(plan.here):
        for copy in copies[here]:
            copy.wait()
        rows = slice(here * lanes, (here + 1) * lanes)
        side = jnp.broadcast_to(side_ref[own * plan.here + here], (lanes, lanes)).T
        side = jnp.concatenate([side] * (out_ref.shape[1] // lanes), 1)
        trial = trial_block(floats_ref, here, above, side)
        out_ref[rows, :] = jnp.where(mask_ref[rows, :] == 2, 0.0, jnp.maximum(trial, 0.0))


def make_thickness(plan, own, fields, faces):
    shape = fields[0].shape
    scratch = field_scratch(shape) + [pltpu.SemaphoreType.DMA((plan.here, 5))]
    return kernel_call(lambda *refs: thickness_kernel(plan, *refs), [real_array(*shape)], scratch, [own], fields, faces)[0]


def finish_load(plan, own, line_ref, uplift_tails, load_tails, side_ref):
    cols, here = plan.cols, plan.here
    row = lax.broadcasted_iota(jnp.int32, (8, lanes), 0)
    lane = lax.broadcasted_iota(jnp.int32, (8, lanes), 1)
    wide_lane = lax.broadcasted_iota(jnp.int32, (cols, lanes), 1)
    for step in range(plan.gx):
        block = own ^ step
        above = own_part(plan, own, row_above(plan, own, block, uplift_tails))
        tail = load_tails[step]
        new = jnp.maximum(tail[0:1, :] + time_step * above, 0.0) - tail[1:2, :]
        turned = jnp.broadcast_to(new, (lanes, lanes)).T[:cols]
        line_ref[block * here] = jnp.where(wide_lane == 0, turned, line_ref[block * here])

        @pl.when(own == 0)
        def _(block=block, tail=tail, above=above):
            for a in range(here):
                corner = jnp.where(lane[:1] == 0, jnp.broadcast_to(above[:, :1], (1, lanes)), 0.0) if a == 0 else 0.0
                trial = tail[2 + a : 3 + a, :] + time_step * (side_ref[block * here + a] + corner)
                line_ref[block * here + a, 0:1, :] = jnp.maximum(trial, 0.0) - tail[2 + here + a : 3 + here + a, :]


def forward_kernel(plan, lead, own_ref, *refs):
    pieces, refs = refs[: plan.gx], refs[plan.gx :]
    cols, radix, groups, here = plan.cols, plan.radix, plan.groups, plan.here
    own = own_ref[0]
    tail = slice(here * cols, here * cols + plan.tail)
    if lead:
        uplift_tails, side_ref, other_ref, *refs = refs
        twiddle_ref, table_ref, out_ref, line_ref, high_ref, low_ref = refs
    else:
        twiddle_ref, table_ref, out_ref, tails_ref, edge_ref, line_ref, high_ref, low_ref = refs
        for step in range(plan.gx):
            tails_ref[step] = pieces[step][tail, :]
            for a in range(here):
                edge_ref[(own ^ step) * here + a] = pieces[step][here * (cols + 1) + a : here * (cols + 1) + a + 1, :]
    step_rows = 16
    total = groups * cols
    for step in range(plan.gx):
        for a in range(here):
            line_ref[(own ^ step) * here + a] = pieces[step][a * cols : (a + 1) * cols, :]
    if lead:
        finish_load(plan, own, line_ref, [uplift_tails[k] for k in range(plan.gx)], [piece[tail, :] for piece in pieces], side_ref)
    skip = lead % lanes

    def chunk(index, carry):
        row = pl.multiple_of(index * step_rows, step_rows)
        real, imag = radix_forward([line_ref[n, pl.ds(row, step_rows), :] for n in range(radix)])
        for g in range(groups):
            if g == 0:
                first, second = real[0], real[groups]
            else:
                cos, sin = twiddle_ref[0, g : g + 1, :], twiddle_ref[1, g : g + 1, :]
                first = real[g] * cos + imag[g - 1] * sin
                second = imag[g - 1] * cos - real[g] * sin
            high, low = halves(jnp.concatenate([first, second], 1))
            place = pl.ds(skip + g * cols + row, step_rows)
            high_ref[place, :] = high
            low_ref[place, :] = low
        return carry

    lax.fori_loop(0, cols // step_rows, chunk, 0)
    for edge in ((0, skip), (skip + total, high_ref.shape[0])):
        if edge[0] < edge[1]:
            high_ref[edge[0] : edge[1], :] = jnp.zeros((edge[1] - edge[0], 2 * lanes), jnp.bfloat16)
            low_ref[edge[0] : edge[1], :] = jnp.zeros((edge[1] - edge[0], 2 * lanes), jnp.bfloat16)
    general = (table_ref[0, 0], table_ref[0, 1])
    special = (table_ref[1, 0], table_ref[1, 1])
    before = lead - skip
    for start in range(0, before, lanes):
        out_ref[:, :, start : start + lanes] = other_ref[:, :, start : start + lanes]
    for start in range(0, high_ref.shape[0], lanes):
        rows = slice(start, start + lanes)
        data = (high_ref[rows, :], low_ref[rows, :])
        end = skip + cols
        lane = lax.broadcasted_iota(jnp.int32, (2 * lanes, lanes), 1)
        if start + lanes <= end:
            out = product(special, data, True)
        else:
            out = product(general, data, True)
            if start < end:
                out = jnp.where(lane < end - start, product(special, data, True), out)
        out = out.reshape(plan.devices, plan.rows, lanes)
        at = before + start
        if start < skip:
            lane = lax.broadcasted_iota(jnp.int32, out.shape, 2)
            out = jnp.where(lane < skip - start, other_ref[:, :, at : at + lanes], out)
        out_ref[:, :, at : at + lanes] = out
    if lead:
        one, two = out_ref[0, :, :lanes], out_ref[0, :, before : before + 2 * lanes]
        row = lax.broadcasted_iota(jnp.int32, two.shape, 0)
        lane = lax.broadcasted_iota(jnp.int32, two.shape, 1)
        wide = pltpu.roll(jnp.concatenate([one, one], 1), plan.deep, 0)
        to_right = pltpu.roll(wide, skip, 1) if skip else wide
        swapped = pltpu.roll(two, plan.deep, 0)
        to_left = pltpu.roll(swapped, 2 * lanes - skip, 1) if skip else swapped
        take = (row == plan.deep) & (lane < cols)
        out_ref[0, :, :lanes] = jnp.where(take, to_left, jnp.concatenate([one, one], 1))[:, :lanes]
        take = (row == 0) & (lane >= skip) & (lane < skip + cols)
        out_ref[0, :, before : before + 2 * lanes] = jnp.where(take, to_right, two)


def middle_kernel(plan, position_ref, in_ref, t1_ref, t2_ref, t2i_ref, t1i_ref, twiddle_ref, out_ref, high_ref, low_ref, back_high, back_low, turn_ref):
    position = position_ref[0]
    cols, groups, deep, count = plan.cols, plan.groups, plan.deep, plan.devices
    width, size = lanes, 2 * lanes
    for start in range(0, 2 * groups * cols, lanes):
        block = in_ref[:, :, start : start + lanes].reshape(size, lanes).T
        high_ref[start : start + lanes, :], low_ref[start : start + lanes, :] = halves(block)
    t1 = (t1_ref[0], t1_ref[1])
    t2 = (t2_ref[0], t2_ref[1])
    t2i = (t2i_ref[0], t2i_ref[1])
    t1i = (t1i_ref[0], t1i_ref[1])
    cos, sin = twiddle_ref[0], twiddle_ref[1]
    lane = lax.broadcasted_iota(jnp.int32, (1, width), 1)
    q, t = lane % deep, lane // deep
    w = lax.broadcasted_iota(jnp.int32, (cols, width), 0)
    ky = wave_square(t + count * w, plan.length_y)
    m = position * deep + q
    special = jnp.broadcast_to((position == 0) & (q == 0), (cols, width))
    results = []
    mixed = []
    for g in range(groups):
        if g % 2 == 0:
            mixed = []
            for field in range(2):
                rows = slice((field * groups + g) * cols, (field * groups + min(g + 2, groups)) * cols)
                mixed.append(product((high_ref[rows, :], low_ref[rows, :]), t1))
        sides = []
        for field in range(2):
            part = mixed[field][(g % 2) * cols : (g % 2 + 1) * cols]
            re, im = part[:, :width], part[:, width:]
            sides.append(jnp.concatenate([re * cos + im * sin, im * cos - re * sin], 0))
        spectra = product(t2, halves(jnp.concatenate(sides, 1)))
        ur, vr = spectra[:cols, :width], spectra[:cols, width:]
        ui, vi = spectra[cols:, :width], spectra[cols:, width:]
        half = lanes // 2
        if g == 0:
            index = jnp.where(m < half, plan.radix * m, plan.radix // 2 + plan.radix * (m - half))
        else:
            index = g + plan.radix * m
        damping, across = spectral_kernels(wave_square(index, plan.length_x) + ky)
        out_r, out_i = across * (damping * ur - vr), across * (damping * ui - vi)
        if g == 0:
            out_r = jnp.where(special, across * (damping * ur - ui), out_r)
            out_i = jnp.where(special, across * (damping * ui + ur), out_i)
            damping, across = spectral_kernels(np.float32(math.pi) ** 2 + ky)
            extra = jnp.concatenate([across * (damping * vr - vi), across * (damping * vi + vr)], 0)
        results.append(jnp.concatenate([out_r, out_i], 0))
    results.append(extra)
    for g in range(0, groups + 1, 2):
        pair = results[g : g + 2]
        back = product(t2i, halves(jnp.concatenate(pair, 1)))
        for k in range(len(pair)):
            re, im = back[:cols, k * width : (k + 1) * width], back[cols:, k * width : (k + 1) * width]
            turned = jnp.concatenate([re * cos - im * sin, im * cos + re * sin], 1)
            place = slice((g + k) * cols, (g + k + 1) * cols)
            back_high[place, :], back_low[place, :] = halves(turned)
    last = slice(groups * cols, (groups + 1) * cols)
    extra = product((back_high[last, :], back_low[last, :]), t1i)
    place = lax.broadcasted_iota(jnp.int32, (cols, size), 1)
    moved = (position == 0) & (place % plan.rows == deep)
    for g in range(groups):
        rows = slice(g * cols, (g + 1) * cols)
        lines = product((back_high[rows, :], back_low[rows, :]), t1i)
        if g == 0:
            lines = jnp.where(moved, pltpu.roll(extra, deep, 1), lines)
        turn_ref[rows, :] = lines
    for start in range(0, groups * cols, lanes):
        block = turn_ref[start : start + lanes, :].T
        keep = min(lanes, groups * cols - start)
        out_ref[:, :, start : start + keep] = block.reshape(count, plan.rows, lanes)[:, :, :keep]


def inverse_kernel(plan, own_ref, in_ref, twiddle_ref, table_ref, *refs):
    out_refs, (line_ref, turn_ref, mid_ref) = refs[: plan.gx], refs[plan.gx :]
    own = own_ref[0]
    cols, groups, here = plan.cols, plan.groups, plan.here
    size = 2 * lanes
    total = groups * cols
    for start in range(0, total, lanes):
        keep = min(lanes, total - start)
        block = in_ref[:, :, start : start + keep].reshape(size, keep)
        turn_ref[start : start + keep, :] = block.T
    for g in range(groups):
        rows = slice(g * cols, (g + 1) * cols)
        kind = 1 if g == 0 else 0
        mid_ref[rows, :] = product(halves(turn_ref[rows, :]), (table_ref[kind, 0], table_ref[kind, 1]))
    step_rows = 16

    def chunk(index, carry):
        row = pl.multiple_of(index * step_rows, step_rows)
        real, imag = [], []
        for g in range(1, groups):
            place = pl.ds(g * cols + row, step_rows)
            re, im = mid_ref[place, :lanes], mid_ref[place, lanes:]
            cos, sin = twiddle_ref[0, g : g + 1, :], twiddle_ref[1, g : g + 1, :]
            real.append(re * cos - im * sin)
            imag.append(im * cos + re * sin)
        place = pl.ds(row, step_rows)
        values = radix_inverse(mid_ref[place, :lanes], mid_ref[place, lanes:], real, imag)
        for n, value in enumerate(values):
            line_ref[n, place, :] = value
        return carry

    lax.fori_loop(0, cols // step_rows, chunk, 0)
    for step in range(plan.gx):
        for a in range(here):
            out_refs[step][a] = line_ref[(own ^ step) * here + a]


def final_kernel(plan, own_ref, *refs):
    pieces, (out_ref, line_ref) = refs[:-2], refs[-2:]
    own = own_ref[0]
    for step in range(plan.gx):
        start = pl.multiple_of((own ^ step) * plan.cols, 8)
        for a in range(plan.here):
            line_ref[a, pl.ds(start, plan.cols), :] = pieces[step][a]
    for a in range(plan.here):
        out_ref[a * lanes : (a + 1) * lanes, :] = line_ref[a].T


def swap_gx(plan, pieces):
    got = [pieces[0]]
    for step in range(1, plan.gx):
        got.append(lax.ppermute(pieces[step], "gx", [(k, k ^ step) for k in range(plan.gx)]))
    return got


def build_kernels(plan):
    vmem, f32, bf16 = pltpu.VMEM, jnp.float32, jnp.bfloat16
    size, cols, groups = 2 * lanes, plan.cols, plan.groups
    half = groups * cols
    pieces = [real_array(plan.here, cols, lanes)] * plan.gx
    line = vmem((plan.radix, cols, lanes), f32)

    def forward(lead, own, *operands):
        skip = lead % lanes
        rounded = -(-(skip + half) // lanes) * lanes
        outs = [real_array(plan.devices, plan.rows, lead - skip + rounded)]
        if not lead:
            outs += [real_array(plan.gx, plan.tail, lanes), real_array(plan.radix, 1, lanes)]
        return call(
            lambda *refs: forward_kernel(plan, lead, *refs),
            outs,
            [line] + [vmem((rounded, size), bf16)] * 2,
            [own],
            *operands,
        )

    def local(thickness, bed_uplift, flux_x, flux_y, mass_balance, ice_mask):
        own = lax.axis_index("gx").reshape(1)
        position = (lax.axis_index("gy") * plan.gx + lax.axis_index("gx")).reshape(1)
        fields = (thickness, flux_x, flux_y, mass_balance, ice_mask)
        uplift = send_uplift(plan, own, bed_uplift, flux_x, flux_y)
        lines_u = swap_gx(plan, uplift)
        load = make_load(plan, own, fields)
        lines_v = swap_gx(plan, load)
        twiddle = plan.slot_twiddle()
        tables = np.stack([table_halves(table) for table in plan.slot_matrix()])
        spectrum_u, tails_u, edge = forward(0, own, *(lines_u + [twiddle, tables]))
        side = passed_along(edge, "gy", 1)
        (spectrum,) = forward(half, own, *(lines_v + [tails_u, side, spectrum_u, twiddle, tables]))
        thickness_new = make_thickness(plan, own, fields, (tails_u, side))
        received = exchange_all(spectrum)
        source, across = plan.source_matrix(), plan.line_matrix()
        scale = np.float32(1.0 / plan.length_y)
        tables = [table_halves(table) for table in (source, across, across.T * scale, source.T)]
        (middle,) = call(
            lambda *refs: middle_kernel(plan, *refs),
            [real_array(plan.devices, plan.rows, half)],
            [vmem((2 * half, size), bf16)] * 2 + [vmem((half + cols, size), bf16)] * 2 + [vmem((half + cols, size), f32)],
            [position],
            *([received] + tables + [plan.line_twiddle()]),
        )
        back = exchange_all(middle)
        inverse = np.stack([table_halves(table) for table in plan.slot_inverse()])
        bed = call(
            lambda *refs: inverse_kernel(plan, *refs),
            pieces,
            [line] + [vmem((half, size), f32)] * 2,
            [own],
            *(back, twiddle, inverse),
        )
        lines_b = swap_gx(plan, bed)
        (bed_new,) = call(
            lambda *refs: final_kernel(plan, *refs),
            [real_array(*thickness.shape)],
            [vmem((plan.here, plan.gx * cols, lanes), f32)],
            [own],
            *lines_b,
        )
        return thickness_new, bed_new

    return local


def build(plan):
    if plan.devices * plan.rows == 2 * lanes and plan.cols % 16 == 0 and plan.radix <= 16 and plan.gx in (2, 4, 8):
        return build_kernels(plan)

    def local(thickness, bed_uplift, flux_x, flux_y, mass_balance, ice_mask):
        lower_face = passed_along(flux_x[-1:, :], "gx", 1)
        left_face = passed_along(flux_y[:, -1:], "gy", 1)
        flux_below = jnp.concatenate([lower_face, flux_x[:-1, :]], axis=0)
        flux_left = jnp.concatenate([left_face, flux_y[:, :-1]], axis=1)
        divergence = flux_x - flux_below + flux_y - flux_left
        trial = thickness + time_step * (mass_balance - divergence)
        thickness_new = jnp.where(ice_mask == 2, 0.0, jnp.maximum(trial, 0.0))
        load = jnp.where(ice_mask == 0, thickness_new - thickness, 0.0)
        fields = jnp.stack([to_lines(plan, bed_uplift), to_lines(plan, load)], 1)
        lines = exchange_gx(fields)
        lines = lines.transpose(1, 0, 2, 3, 4).reshape(2, plan.radix, plan.cols, lanes)
        received = exchange_all(forward_x(plan, lines))
        position = lax.axis_index("gy") * plan.gx + lax.axis_index("gx")
        back = exchange_all(middle_y(plan, received, position))
        bed = inverse_x(plan, back)
        bed = jnp.stack(bed).reshape(plan.gx, plan.here, plan.cols, lanes)
        bed = exchange_gx(bed)
        bed_new = bed.transpose(1, 3, 0, 2).reshape(plan.here * lanes, plan.gx * plan.cols)
        return thickness_new, bed_new

    return local


def solution(mesh):
    spec = P("gx", "gy")

    def step(*args):
        length_x, length_y = args[0].shape
        plan = Plan(mesh, length_x, length_y)
        body = jax.shard_map(build(plan), mesh=mesh, in_specs=(spec,) * 6, out_specs=(spec, spec), check_vma=False)
        return body(*args)

    return step
```

```python
import math

import jax
import jax.numpy as jnp
import numpy as np
from jax import lax
from jax.experimental import pallas as pl
from jax.experimental.pallas import tpu as pltpu
from jax.sharding import PartitionSpec as P

time_step = 0.5
viscous = 4.0
buoyant = 0.01
flexural = 50.0
lanes = 128
highest = lax.Precision.HIGHEST


class Plan:
    def __init__(self, mesh, length_x, length_y):
        self.gx, self.gy = mesh.shape["gx"], mesh.shape["gy"]
        self.devices = self.gx * self.gy
        self.length_x, self.length_y = length_x, length_y
        self.radix = length_x // lanes
        self.here = self.radix // self.gx
        self.groups = self.radix // 2
        self.cols = length_y // self.devices
        self.m_parts = min(self.devices, lanes)
        self.g_parts = self.devices // self.m_parts
        self.deep = lanes // self.m_parts
        self.own_groups = self.groups // self.g_parts
        self.rows = 2 * self.deep
        self.tail = -(-(2 + 2 * self.here) // 8) * 8
        self.piece_rows = self.here * self.cols + self.tail

    def slot_matrix(self):
        n2 = np.arange(lanes)[None, :]
        m = np.arange(lanes)[:, None]
        theta = 2 * np.pi * (m * n2 % lanes) / lanes
        cos, sin = np.cos(theta), np.sin(theta)
        general = np.stack([np.concatenate([cos, sin], 1), np.concatenate([-sin, cos], 1)])
        half = lanes // 2
        turned = 2 * np.pi * ((2 * (m - half) + 1) * n2 % (2 * lanes)) / (2 * lanes)
        low = np.arange(lanes)[:, None] < half
        real = np.concatenate([np.where(low, cos, 0), np.where(low, 0, np.cos(turned))], 1)
        imag = np.concatenate([np.where(low, -sin, 0), np.where(low, 0, -np.sin(turned))], 1)
        imag[0, :lanes] = np.where(np.arange(lanes) % 2 == 0, 1.0, -1.0)
        first = np.stack([real, imag])
        return np.stack([self._by_part(general), self._by_part(first)]).astype(np.float32)

    def _by_part(self, table):
        split = table.reshape(2, self.m_parts, self.deep, 2 * lanes)
        return split.transpose(1, 0, 2, 3).reshape(2 * lanes, 2 * lanes)

    def slot_inverse(self):
        m = np.arange(lanes)[:, None]
        n2 = np.arange(lanes)[None, :]
        theta = 2 * np.pi * (m * n2 % lanes) / lanes
        cos, sin = np.cos(theta), np.sin(theta)
        general = 2 * np.stack([np.concatenate([cos, sin], 1), np.concatenate([-sin, cos], 1)])
        half = lanes // 2
        turned = 2 * np.pi * ((2 * (m - half) + 1) * n2 % (2 * lanes)) / (2 * lanes)
        low = m < half
        real = 2 * np.concatenate([np.where(low, cos, 0), np.where(low, 0, np.cos(turned))], 1)
        imag = 2 * np.concatenate([np.where(low, -sin, 0), np.where(low, 0, -np.sin(turned))], 1)
        real[0, :lanes] = 1.0
        imag[0, :lanes] = np.where(np.arange(lanes) % 2 == 0, 1.0, -1.0)
        first = np.stack([real, imag])
        return (np.stack([self._by_part(general), self._by_part(first)]) / self.length_x).astype(np.float32)

    def slot_twiddle(self):
        angle = 2 * np.pi * np.arange(self.groups)[:, None] * np.arange(lanes)[None, :] / self.length_x
        return np.stack([np.cos(angle), np.sin(angle)]).astype(np.float32)

    def source_matrix(self):
        count, deep = self.devices, self.deep
        index = np.arange(count)
        theta = 2 * np.pi * (index[:, None] * index[None, :] % count) / count
        cos, sin = np.cos(theta), np.sin(theta)
        out = np.zeros((count, 2, deep, 2, count, deep))
        for q in range(deep):
            out[:, 0, q, 0, :, q] = cos
            out[:, 1, q, 0, :, q] = sin
            out[:, 0, q, 1, :, q] = -sin
            out[:, 1, q, 1, :, q] = cos
        return out.reshape(count * 2 * deep, 2 * count * deep).astype(np.float32)

    def line_matrix(self):
        index = np.arange(self.cols)
        theta = 2 * np.pi * (index[:, None] * index[None, :] % self.cols) / self.cols
        cos, sin = np.cos(theta), np.sin(theta)
        return np.block([[cos, sin], [-sin, cos]]).astype(np.float32)

    def line_twiddle(self):
        angle = 2 * np.pi * np.arange(self.cols)[:, None] * np.arange(self.devices)[None, :] / self.length_y
        angle = np.repeat(angle, self.deep, axis=1)
        return np.stack([np.cos(angle), np.sin(angle)]).astype(np.float32)


def weighted(terms):
    groups = {}
    for coefficient, value in terms:
        size = round(abs(coefficient), 12)
        if size == 0.0:
            continue
        groups.setdefault(size, []).append((coefficient > 0, value))
    total = None
    for size, members in groups.items():
        members.sort(key=lambda member: not member[0])
        positive, part = members[0]
        for sign, value in members[1:]:
            part = part + value if sign == positive else part - value
        if size != 1.0:
            part = part * np.float32(size)
        if total is None:
            total = part if positive else -part
        else:
            total = total + part if positive else total - part
    return total


def radix_forward(values):
    count = len(values)
    half = count // 2
    even = [values[j] + values[count - j] for j in range(1, half)]
    odd = [values[j] - values[count - j] for j in range(1, half)]
    real, imag = [], []
    for g in range(half + 1):
        terms = [(1.0, values[0]), ((-1.0) ** g, values[half])]
        terms += [(math.cos(2 * math.pi * g * (j + 1) / count), even[j]) for j in range(half - 1)]
        real.append(weighted(terms))
        if 0 < g < half:
            imag.append(weighted([(-math.sin(2 * math.pi * g * (j + 1) / count), odd[j]) for j in range(half - 1)]))
    return real, imag


def radix_inverse(first, middle, real, imag):
    half = len(real) + 1
    count = 2 * half
    out = [None] * count
    for j in range(half + 1):
        terms = [(1.0, first), ((-1.0) ** j, middle)]
        terms += [(math.cos(2 * math.pi * g * j / count), real[g - 1]) for g in range(1, half)]
        together = weighted(terms)
        if j in (0, half):
            out[j] = together
            continue
        apart = weighted([(math.sin(2 * math.pi * g * j / count), imag[g - 1]) for g in range(1, half)])
        out[j] = together - apart
        out[count - j] = together + apart
    return out


def mul(a, b):
    return jnp.matmul(a, b, precision=highest)


def exchange_gx(value):
    count = lax.axis_size("gx")
    own = lax.axis_index("gx")
    if count > 8:
        return lax.all_to_all(value, "gx", split_axis=0, concat_axis=0, tiled=True)
    pieces = [lax.dynamic_index_in_dim(value, own, 0, False)]
    for step in range(1, count):
        piece = lax.dynamic_index_in_dim(value, own ^ step, 0, False)
        pieces.append(lax.ppermute(piece, "gx", [(k, k ^ step) for k in range(count)]))
    stacked = jnp.stack(pieces)
    return jnp.stack([lax.dynamic_index_in_dim(stacked, own ^ k, 0, False) for k in range(count)])


def exchange_all(value):
    return lax.all_to_all(value, ("gy", "gx"), split_axis=0, concat_axis=0, tiled=True)


def passed_along(value, axis, steps):
    count = lax.axis_size(axis)
    leading, last = (max(0, -steps), min(count, count - steps))
    return lax.ppermute(value, axis, [(source, source + steps) for source in range(leading, last)])


def forward_x(plan, lines):
    table = plan.slot_matrix()
    cos, sin = plan.slot_twiddle()
    real, imag = radix_forward([lines[:, n] for n in range(plan.radix)])
    blocks = [jnp.concatenate([real[0], real[plan.groups]], -1)]
    for g in range(1, plan.groups):
        re, im = real[g], imag[g - 1]
        blocks.append(jnp.concatenate([re * cos[g] + im * sin[g], im * cos[g] - re * sin[g]], -1))
    first = jnp.einsum("ok,fck->ofc", table[1], blocks[0], precision=highest)
    row = first[plan.deep, 0]
    first = first.at[plan.deep, 0].set(first[0, 1]).at[0, 1].set(row)
    rest = jnp.einsum("ok,gfck->ogfc", table[0], jnp.stack(blocks[1:]), precision=highest)
    spectrum = jnp.concatenate([first[:, None], rest], 1)
    spectrum = spectrum.reshape(plan.m_parts, plan.rows, plan.g_parts, -1)
    return spectrum.transpose(2, 0, 1, 3).reshape(plan.devices, plan.rows, -1)


def spectral_kernels(square):
    kappa = jnp.sqrt(square)
    damping = viscous * kappa
    across = 1.0 / (damping + buoyant + flexural * kappa**4)
    return damping, across


def wave_square(index, length):
    signed = jnp.where(2 * index >= length, index - length, index)
    wave = signed.astype(jnp.float32) * (2.0 * math.pi / length)
    return wave * wave


def middle_y(plan, received, position):
    deep, count, cols = plan.deep, plan.devices, plan.cols
    width = count * deep
    flat = received.reshape(count * plan.rows, -1).T
    mixed = mul(flat, plan.source_matrix())
    mixed = mixed.reshape(plan.own_groups, 2, cols, 2, width)
    cos, sin = plan.line_twiddle()
    re, im = mixed[:, :, :, 0], mixed[:, :, :, 1]
    turned = jnp.concatenate([re * cos + im * sin, im * cos - re * sin], 2)
    spectra = jnp.einsum("wk,gfkl->gfwl", plan.line_matrix(), turned, precision=highest)
    lane = lax.broadcasted_iota(jnp.int32, (1, width), 1)
    q, t = lane % deep, lane // deep
    w = lax.broadcasted_iota(jnp.int32, (cols, 1), 0)
    ky = wave_square(t + count * w, plan.length_y)
    m = (position % plan.m_parts) * deep + q
    base = (position // plan.m_parts) * plan.own_groups
    special = (position == 0) & (q == 0)
    results = []
    for group in range(plan.own_groups):
        g = base + group
        half = lanes // 2
        first = jnp.where(m < half, plan.radix * m, plan.radix // 2 + plan.radix * (m - half))
        index = jnp.where(g == 0, first, g + plan.radix * m)
        damping, across = spectral_kernels(wave_square(index, plan.length_x) + ky)
        u, v = spectra[group, 0], spectra[group, 1]
        ur, ui, vr, vi = u[:cols], u[cols:], v[:cols], v[cols:]
        out_r, out_i = across * (damping * ur - vr), across * (damping * ui - vi)
        if group == 0:
            out_r = jnp.where(special, across * (damping * ur - ui), out_r)
            out_i = jnp.where(special, across * (damping * ui + ur), out_i)
            damping, across = spectral_kernels(np.float32(math.pi) ** 2 + ky)
            extra = jnp.concatenate([across * (damping * vr - vi), across * (damping * vi + vr)], 0)
        results.append(jnp.concatenate([out_r, out_i], 0))
    results.append(extra)
    back = jnp.einsum("kw,gkl->gwl", plan.line_matrix() * np.float32(1.0 / plan.length_y), jnp.stack(results), precision=highest)
    re, im = back[:, :cols], back[:, cols:]
    turned = jnp.concatenate([re * cos - im * sin, im * cos + re * sin], 2)
    lines = jnp.einsum("gcl,sl->gcs", turned, plan.source_matrix(), precision=highest)
    place = lax.broadcasted_iota(jnp.int32, (1, count * plan.rows), 1)
    moved = (position == 0) & (place % plan.rows == deep)
    fixed = jnp.where(moved, jnp.roll(lines[-1], deep, axis=1), lines[0])
    lines = jnp.concatenate([fixed[None], lines[1:-1]], 0)
    return lines.reshape(plan.own_groups * cols, count * plan.rows).T.reshape(count, plan.rows, -1)


def inverse_x(plan, received):
    cols = plan.cols
    table = plan.slot_inverse()
    cos, sin = plan.slot_twiddle()
    split = received.reshape(plan.g_parts, 2 * lanes, plan.own_groups, cols)
    split = split.transpose(0, 2, 3, 1).reshape(plan.groups, cols, 2 * lanes)
    first = mul(split[0], table[1])
    rest = mul(split[1:], table[0])
    real, imag = [], []
    for g in range(1, plan.groups):
        re, im = rest[g - 1, :, :lanes], rest[g - 1, :, lanes:]
        real.append(re * cos[g] - im * sin[g])
        imag.append(im * cos[g] + re * sin[g])
    return radix_inverse(first[:, :lanes], first[:, lanes:], real, imag)


def to_lines(plan, field):
    split = field.reshape(plan.here, lanes, plan.gx, plan.cols)
    return split.transpose(2, 0, 3, 1)


def halves(value):
    high = value.astype(jnp.bfloat16)
    return high, (value - high.astype(jnp.float32)).astype(jnp.bfloat16)


def table_halves(table):
    high = table.astype(jnp.bfloat16)
    return np.stack([high, (table - high.astype(np.float32)).astype(jnp.bfloat16)])


def product(left, right, turned=False):
    dims = (((1,), (1 if turned else 0,)), ((), ()))

    def one(a, b):
        return lax.dot_general(a, b, dims, preferred_element_type=jnp.float32)

    return one(left[0], right[0]) + (one(left[0], right[1]) + one(left[1], right[0]))


def call(body, outs, scratch, scalars, *operands):
    scalar = pl.BlockSpec(memory_space=pltpu.SMEM)
    whole = pl.BlockSpec(memory_space=pltpu.VMEM)
    run = pl.pallas_call(
        body,
        out_shape=outs,
        in_specs=[scalar] * len(scalars) + [whole] * len(operands),
        out_specs=[whole] * len(outs),
        scratch_shapes=scratch,
        compiler_params=pltpu.CompilerParams(vmem_limit_bytes=16 << 20),
    )
    return run(*scalars, *operands)


def real_array(*shape):
    return jax.ShapeDtypeStruct(shape, jnp.float32)


def lines_out(plan, own, block, here, turned_ref, out_refs):
    turned_ref[here] = block.T
    for step in range(plan.gx):
        start = pl.multiple_of((own ^ step) * plan.cols, 8)
        out_refs[step][here * plan.cols : (here + 1) * plan.cols, :] = turned_ref[here, pl.ds(start, plan.cols), :]


def own_part(plan, part, row):
    wide = jnp.concatenate([row, row[:, :lanes]], 1)
    wide = jnp.broadcast_to(wide, (8, wide.shape[1]))
    out = wide[:, :lanes]
    for k in range(1, plan.gx):
        start = k * plan.cols
        low = start // lanes * lanes
        block = wide[:, low : low + 2 * lanes]
        if start % lanes:
            block = pltpu.roll(block, 2 * lanes - start % lanes, 1)
        out = jnp.where(part == k, block[:, :lanes], out)
    return out[:1]


def kernel_call(body, outs, scratch, scalars, inputs, faces=()):
    whole = pl.BlockSpec(memory_space=pltpu.VMEM)
    run = pl.pallas_call(
        body,
        out_shape=outs,
        in_specs=[pl.BlockSpec(memory_space=pltpu.SMEM)] * len(scalars) + [pl.BlockSpec(memory_space=pl.ANY)] * len(inputs) + [whole] * len(faces),
        out_specs=[whole] * len(outs),
        scratch_shapes=scratch,
    )
    return run(*scalars, *inputs, *faces)


def uplift_kernel(plan, own_ref, uplift_hbm, flux_x_hbm, flux_y_hbm, *refs):
    own = own_ref[0]
    out_refs = refs[: plan.gx]
    field_ref, turned_ref, tail_ref, last_x_ref, last_y_ref, sems, out_sems = refs[plan.gx :]
    rows, cols = uplift_hbm.shape
    copies = [
        pltpu.make_async_copy(flux_x_hbm.at[pl.ds(rows - 8, 8), :], last_x_ref, sems.at[0]),
        pltpu.make_async_copy(flux_y_hbm.at[:, pl.ds(cols - lanes, lanes)], last_y_ref, sems.at[1]),
    ]
    half = lanes // 2
    for part in range(2 * plan.here):
        source = uplift_hbm.at[pl.ds(part * half, half), :]
        copies.append(pltpu.make_async_copy(source, field_ref.at[pl.ds(part * half, half), :], sems.at[2 + part]))
    for copy in copies[2:] + copies[:2]:
        copy.start()
    sent = []
    for here in range(plan.here):
        copies[2 + 2 * here].wait()
        copies[3 + 2 * here].wait()
        turned_ref[here] = field_ref[here * lanes : (here + 1) * lanes, :].T
        for step in range(plan.gx):
            source = turned_ref.at[here, pl.ds(pl.multiple_of((own ^ step) * plan.cols, 8), plan.cols), :]
            target = out_refs[step].at[pl.ds(here * plan.cols, plan.cols), :]
            sent.append(pltpu.make_async_copy(source, target, out_sems.at[here, step]))
            sent[-1].start()
    copies[0].wait()
    copies[1].wait()
    last_x = last_x_ref[7:8, :]
    last_y = last_y_ref[...].T[lanes - 1 : lanes, :]
    parts = [last[:, a * lanes : (a + 1) * lanes] for last in (last_x, last_y) for a in range(plan.here)]
    parts.append(jnp.zeros((plan.tail - 2 * plan.here, lanes), jnp.float32))
    tail_ref[...] = jnp.concatenate(parts, 0)
    for step in range(plan.gx):
        target = out_refs[step].at[pl.ds(plan.here * plan.cols, plan.tail), :]
        sent.append(pltpu.make_async_copy(tail_ref, target, out_sems.at[plan.here, step]))
        sent[-1].start()
    for copy in sent:
        copy.wait()


def send_uplift(plan, own, bed_uplift, flux_x, flux_y):
    rows, cols = bed_uplift.shape
    run = pl.pallas_call(
        lambda *refs: uplift_kernel(plan, *refs),
        out_shape=[real_array(plan.piece_rows, lanes)] * plan.gx,
        in_specs=[pl.BlockSpec(memory_space=pltpu.SMEM)] + [pl.BlockSpec(memory_space=pl.ANY)] * 3,
        out_specs=[pl.BlockSpec(memory_space=pl.ANY)] * plan.gx,
        scratch_shapes=[
            pltpu.VMEM((rows, cols), jnp.float32),
            pltpu.VMEM((plan.here, cols, lanes), jnp.float32),
            pltpu.VMEM((plan.tail, lanes), jnp.float32),
            pltpu.VMEM((8, cols), jnp.float32),
            pltpu.VMEM((rows, lanes), jnp.float32),
            pltpu.SemaphoreType.DMA((2 + 2 * plan.here,)),
            pltpu.SemaphoreType.DMA((plan.here + 1, plan.gx)),
        ],
    )
    return run(own, bed_uplift, flux_x, flux_y)


def fetch_fields(plan, sources, mask_ref, floats_ref, sems):
    targets = [floats_ref.at[k] for k in range(4)] + [mask_ref]
    copies = []
    for here in range(plan.here):
        rows = pl.ds(here * lanes, lanes)
        group = [
            pltpu.make_async_copy(source.at[rows, :], target.at[rows, :], sems.at[here, k])
            for k, (source, target) in enumerate(zip(sources, targets))
        ]
        for copy in group:
            copy.start()
        copies.append(group)
    return copies


def trial_block(floats_ref, here, above, left_edge):
    rows = slice(here * lanes, (here + 1) * lanes)
    fx, fy = floats_ref[1, rows, :], floats_ref[2, rows, :]
    row = lax.broadcasted_iota(jnp.int32, fx.shape, 0)
    col = lax.broadcasted_iota(jnp.int32, fx.shape, 1)
    if here:
        above = floats_ref[1, here * lanes - 1 : here * lanes, :]
    below = jnp.where(row == 0, jnp.broadcast_to(above, fx.shape) if here or above.ndim else above, pltpu.roll(fx, 1, 0))
    left = jnp.where(col == 0, left_edge, pltpu.roll(fy, 1, 1))
    divergence = fx - below + fy - left
    return floats_ref[0, rows, :] + time_step * (floats_ref[3, rows, :] - divergence)


hidden = np.float32(-1e30)


def load_kernel(plan, own_ref, *refs):
    own = own_ref[0]
    sources, refs = refs[:5], refs[5:]
    line_refs, (mask_ref, floats_ref, turned_ref, sems) = refs[: plan.gx], refs[plan.gx :]
    copies = fetch_fields(plan, sources, mask_ref, floats_ref, sems)
    columns_trial, columns_thick = [], []
    for here in range(plan.here):
        for copy in copies[here]:
            copy.wait()
        rows = slice(here * lanes, (here + 1) * lanes)
        trial = trial_block(floats_ref, here, jnp.float32(0.0), 0.0)
        free = mask_ref[rows, :] == 0
        thick = jnp.where(free, floats_ref[0, rows, :], 0.0)
        trial = jnp.where(free, trial, hidden)
        lines_out(plan, own, jnp.maximum(trial, 0.0) - thick, here, turned_ref, line_refs)
        lane = lax.broadcasted_iota(jnp.int32, (lanes, lanes), 1)
        packed = jnp.where(lane == 0, trial[:, :lanes], pltpu.roll(thick[:, :lanes], 1, 1)).T
        columns_trial.append(packed[0:1])
        columns_thick.append(packed[1:2])
        if here == 0:
            row_trial, row_thick = trial[0:1], thick[0:1]
    tail = plan.here * plan.cols
    rest = plan.tail - 2 - 2 * plan.here
    for step in range(plan.gx):
        parts = [own_part(plan, own ^ step, row_trial), own_part(plan, own ^ step, row_thick)] + columns_trial + columns_thick
        if rest:
            parts.append(jnp.zeros((rest, lanes), jnp.float32))
        line_refs[step][tail : tail + plan.tail, :] = jnp.concatenate(parts, 0)


def field_scratch(shape):
    return [
        pltpu.VMEM(shape, jnp.int32),
        pltpu.VMEM((4,) + shape, jnp.float32),
    ]


def make_load(plan, own, fields):
    shape = fields[0].shape
    scratch = field_scratch(shape) + [
        pltpu.VMEM((plan.here, shape[1], lanes), jnp.float32),
        pltpu.SemaphoreType.DMA((plan.here, 5)),
    ]
    outs = [real_array(plan.piece_rows, lanes)] * plan.gx
    return kernel_call(lambda *refs: load_kernel(plan, *refs), outs, scratch, [own], fields)


def row_above(plan, own, block, tails):
    above = [jnp.zeros((1, lanes), jnp.float32)] * plan.here
    for step in range(plan.gx):
        match = (own ^ step) + 1 == block
        above = [jnp.where(match, tails[step][a : a + 1, :], above[a]) for a in range(plan.here)]
    return jnp.concatenate(above, 1)


def thickness_kernel(plan, own_ref, *refs):
    own = own_ref[0]
    sources, (tails_ref, side_ref, out_ref, mask_ref, floats_ref, sems) = refs[:5], refs[5:]
    copies = fetch_fields(plan, sources, mask_ref, floats_ref, sems)
    above = row_above(plan, own, own, [tails_ref[step] for step in range(plan.gx)])
    for here in range(plan.here):
        for copy in copies[here]:
            copy.wait()
        rows = slice(here * lanes, (here + 1) * lanes)
        side = jnp.broadcast_to(side_ref[0, plan.here + here : plan.here + here + 1, :], (lanes, lanes)).T
        side = jnp.concatenate([side] * (out_ref.shape[1] // lanes), 1)
        trial = trial_block(floats_ref, here, above, side)
        out_ref[rows, :] = jnp.where(mask_ref[rows, :] == 2, 0.0, jnp.maximum(trial, 0.0))


def make_thickness(plan, own, fields, faces):
    shape = fields[0].shape
    scratch = field_scratch(shape) + [pltpu.SemaphoreType.DMA((plan.here, 5))]
    return kernel_call(lambda *refs: thickness_kernel(plan, *refs), [real_array(*shape)], scratch, [own], fields, faces)[0]


def finish_load(plan, own, line_ref, uplift_tails, load_tails, side_ref):
    cols, here = plan.cols, plan.here
    lane = lax.broadcasted_iota(jnp.int32, (1, lanes), 1)
    wide_lane = lax.broadcasted_iota(jnp.int32, (cols, lanes), 1)
    above, new = [], []
    for step in range(plan.gx):
        above.append(own_part(plan, own, row_above(plan, own, own ^ step, uplift_tails)))
        tail = load_tails[step]
        new.append(jnp.maximum(tail[0:1, :] + time_step * above[step], 0.0) - tail[1:2, :])
    turned = jnp.concatenate(new + [jnp.zeros((lanes - plan.gx, lanes), jnp.float32)], 0).T[:cols]
    for step in range(plan.gx):
        place = (own ^ step) * here
        first = pltpu.roll(turned, lanes - step, 1) if step else turned
        line_ref[place] = jnp.where(wide_lane == 0, first, line_ref[place])

    @pl.when(own == 0)
    def _():
        for step in range(plan.gx):
            tail = load_tails[step]
            for a in range(here):
                corner = jnp.where(lane == 0, jnp.broadcast_to(above[step][:, :1], (1, lanes)), 0.0) if a == 0 else 0.0
                trial = tail[2 + a : 3 + a, :] + time_step * (side_ref[step, here + a : here + a + 1, :] + corner)
                line_ref[step * here + a, 0:1, :] = jnp.maximum(trial, 0.0) - tail[2 + here + a : 3 + here + a, :]


def tails_kernel(plan, *refs):
    pieces, tails_ref = refs[: plan.gx], refs[plan.gx]
    start = plan.here * plan.cols
    for step in range(plan.gx):
        tails_ref[step] = pieces[step][start : start + plan.tail, :]


def forward_kernel(plan, lead, own_ref, *refs):
    pieces, refs = refs[: plan.gx], refs[plan.gx :]
    cols, radix, groups, here = plan.cols, plan.radix, plan.groups, plan.here
    own = own_ref[0]
    tail = slice(here * cols, here * cols + plan.tail)
    if lead:
        uplift_tails, side_ref, edge_ref, head_ref, _, twiddle_ref, table_ref, *refs = refs
        out_hbm, line_ref, high_ref, low_ref, block_ref, sems = refs
    else:
        twiddle_ref, table_ref, out_hbm, edge_ref, head_ref, line_ref, high_ref, low_ref, block_ref, sems = refs
    step_rows = 16
    total = groups * cols
    for step in range(plan.gx):
        for a in range(here):
            line_ref[(own ^ step) * here + a] = pieces[step][a * cols : (a + 1) * cols, :]
    if lead:
        tails = [uplift_tails[step] for step in range(plan.gx)]
        finish_load(plan, own, line_ref, tails, [piece[tail, :] for piece in pieces], side_ref)
    skip = lead % lanes

    def chunk(index, carry):
        row = pl.multiple_of(index * step_rows, step_rows)
        real, imag = radix_forward([line_ref[n, pl.ds(row, step_rows), :] for n in range(radix)])
        for g in range(groups):
            if g == 0:
                first, second = real[0], real[groups]
            else:
                cos, sin = twiddle_ref[0, g : g + 1, :], twiddle_ref[1, g : g + 1, :]
                first = real[g] * cos + imag[g - 1] * sin
                second = imag[g - 1] * cos - real[g] * sin
            high, low = halves(jnp.concatenate([first, second], 1))
            place = pl.ds(skip + g * cols + row, step_rows)
            high_ref[place, :] = high
            low_ref[place, :] = low
        return carry

    lax.fori_loop(0, cols // step_rows, chunk, 0)
    for edge in ((0, skip), (skip + total, high_ref.shape[0])):
        if edge[0] < edge[1]:
            high_ref[edge[0] : edge[1], :] = jnp.zeros((edge[1] - edge[0], 2 * lanes), jnp.bfloat16)
            low_ref[edge[0] : edge[1], :] = jnp.zeros((edge[1] - edge[0], 2 * lanes), jnp.bfloat16)
    general = (table_ref[0, 0], table_ref[0, 1])
    special = (table_ref[1, 0], table_ref[1, 1])
    before = (lead - skip) // lanes
    blocks = high_ref.shape[0] // lanes
    sent = []

    def send(block):
        lane = pl.ds((before + block) * lanes, lanes)
        sent.append(pltpu.make_async_copy(block_ref.at[block], out_hbm.at[:, :, lane], sems.at[block]))
        sent[-1].start()

    held = -(-(skip + cols) // lanes) if lead else 0
    for block in range(blocks):
        start = block * lanes
        rows = slice(start, start + lanes)
        data = (high_ref[rows, :], low_ref[rows, :])
        end = skip + cols
        lane = lax.broadcasted_iota(jnp.int32, (2 * lanes, lanes), 1)
        if start + lanes <= end:
            out = product(special, data, True)
        else:
            out = product(general, data, True)
            if start < end:
                out = jnp.where(lane < end - start, product(special, data, True), out)
        out = out.reshape(plan.devices, plan.rows, lanes)
        if start < skip:
            lane = lax.broadcasted_iota(jnp.int32, out.shape, 2)
            out = jnp.where(lane < skip - start, edge_ref[...], out)
        if not lead and (block + 1) * lanes > total:
            edge_ref[...] = out
            continue
        block_ref[block] = out
        if not lead and block == 0:
            head_ref[...] = out[0]
        if block + 1 == held:
            two = jnp.concatenate([block_ref[k, 0] for k in range(held)], 1)
            width = held * lanes
            row = lax.broadcasted_iota(jnp.int32, two.shape, 0)
            lane = lax.broadcasted_iota(jnp.int32, two.shape, 1)
            head = head_ref[...]
            wide = pltpu.roll(jnp.concatenate([head] * held, 1), plan.deep, 0)
            to_right = pltpu.roll(wide, skip, 1) if skip else wide
            swapped = pltpu.roll(two, plan.deep, 0)
            to_left = pltpu.roll(swapped, width - skip, 1) if skip else swapped
            take = (row[:, :lanes] == plan.deep) & (lane[:, :lanes] < cols)
            head_out = block_ref.at[blocks, 0]
            head_out[...] = jnp.where(take, to_left[:, :lanes], head)
            take = (row == 0) & (lane >= skip) & (lane < skip + cols)
            fixed = jnp.where(take, to_right, two)
            for k in range(held):
                block_ref[k, 0] = fixed[:, k * lanes : (k + 1) * lanes]
                send(k)
            sent.append(pltpu.make_async_copy(head_out, out_hbm.at[0, :, pl.ds(0, lanes)], sems.at[blocks]))
            sent[-1].start()
        elif block >= held:
            send(block)
    for copy in sent:
        copy.wait()


def make_forward(plan, own, pieces, tables, before=None):
    half = plan.groups * plan.cols
    lead = half if before else 0
    skip = lead % lanes
    blocks = -(-(skip + half) // lanes)
    any_space, whole = pl.BlockSpec(memory_space=pl.ANY), pl.BlockSpec(memory_space=pltpu.VMEM)
    outs, out_specs, operands, alias = [real_array(plan.devices, plan.rows, 2 * half)], [any_space], list(pieces), {}
    in_specs = [pl.BlockSpec(memory_space=pltpu.SMEM)] + [whole] * len(pieces)
    if before:
        tails, side, spectrum, edge, head = before
        operands += [tails, side, edge, head, spectrum]
        in_specs += [whole] * 4 + [any_space]
        alias = {len(operands): 0}
    else:
        outs += [real_array(plan.devices, plan.rows, lanes), real_array(plan.rows, lanes)]
        out_specs += [whole] * 2
    run = pl.pallas_call(
        lambda *refs: forward_kernel(plan, lead, *refs),
        out_shape=outs,
        in_specs=in_specs + [whole] * 2,
        out_specs=out_specs,
        scratch_shapes=[
            pltpu.VMEM((plan.radix, plan.cols, lanes), jnp.float32),
            pltpu.VMEM((blocks * lanes, 2 * lanes), jnp.bfloat16),
            pltpu.VMEM((blocks * lanes, 2 * lanes), jnp.bfloat16),
            pltpu.VMEM((blocks + 1, plan.devices, plan.rows, lanes), jnp.float32),
            pltpu.SemaphoreType.DMA((blocks + 1,)),
        ],
        input_output_aliases=alias,
        compiler_params=pltpu.CompilerParams(vmem_limit_bytes=16 << 20),
    )
    return run(own, *operands, *tables)


def middle_kernel(plan, position_ref, in_ref, t1_ref, t2_ref, t2i_ref, t1i_ref, twiddle_ref, out_ref, high_ref, low_ref, back_high, back_low, turn_ref):
    position = position_ref[0]
    cols, groups, deep, count = plan.cols, plan.groups, plan.deep, plan.devices
    width, size = lanes, 2 * lanes
    for start in range(0, 2 * groups * cols, lanes):
        block = in_ref[:, :, start : start + lanes].reshape(size, lanes).T
        high_ref[start : start + lanes, :], low_ref[start : start + lanes, :] = halves(block)
    t1 = (t1_ref[0], t1_ref[1])
    t2 = (t2_ref[0], t2_ref[1])
    t2i = (t2i_ref[0], t2i_ref[1])
    t1i = (t1i_ref[0], t1i_ref[1])
    cos, sin = twiddle_ref[0], twiddle_ref[1]
    lane = lax.broadcasted_iota(jnp.int32, (1, width), 1)
    q, t = lane % deep, lane // deep
    w = lax.broadcasted_iota(jnp.int32, (cols, width), 0)
    ky = wave_square(t + count * w, plan.length_y)
    m = position * deep + q
    special = jnp.broadcast_to((position == 0) & (q == 0), (cols, width))
    results = []
    mixed = []
    for g in range(groups):
        if g % 2 == 0:
            mixed = []
            for field in range(2):
                rows = slice((field * groups + g) * cols, (field * groups + min(g + 2, groups)) * cols)
                mixed.append(product((high_ref[rows, :], low_ref[rows, :]), t1))
        sides = []
        for field in range(2):
            part = mixed[field][(g % 2) * cols : (g % 2 + 1) * cols]
            re, im = part[:, :width], part[:, width:]
            sides.append(jnp.concatenate([re * cos + im * sin, im * cos - re * sin], 0))
        spectra = product(t2, halves(jnp.concatenate(sides, 1)))
        ur, vr = spectra[:cols, :width], spectra[:cols, width:]
        ui, vi = spectra[cols:, :width], spectra[cols:, width:]
        half = lanes // 2
        if g == 0:
            index = jnp.where(m < half, plan.radix * m, plan.radix // 2 + plan.radix * (m - half))
        else:
            index = g + plan.radix * m
        damping, across = spectral_kernels(wave_square(index, plan.length_x) + ky)
        out_r, out_i = across * (damping * ur - vr), across * (damping * ui - vi)
        if g == 0:
            out_r = jnp.where(special, across * (damping * ur - ui), out_r)
            out_i = jnp.where(special, across * (damping * ui + ur), out_i)
            damping, across = spectral_kernels(np.float32(math.pi) ** 2 + ky)
            extra = jnp.concatenate([across * (damping * vr - vi), across * (damping * vi + vr)], 0)
        results.append(jnp.concatenate([out_r, out_i], 0))
    results.append(extra)
    for g in range(0, groups + 1, 2):
        pair = results[g : g + 2]
        back = product(t2i, halves(jnp.concatenate(pair, 1)))
        for k in range(len(pair)):
            re, im = back[:cols, k * width : (k + 1) * width], back[cols:, k * width : (k + 1) * width]
            turned = jnp.concatenate([re * cos - im * sin, im * cos + re * sin], 1)
            place = slice((g + k) * cols, (g + k + 1) * cols)
            back_high[place, :], back_low[place, :] = halves(turned)
    last = slice(groups * cols, (groups + 1) * cols)
    extra = product((back_high[last, :], back_low[last, :]), t1i)
    place = lax.broadcasted_iota(jnp.int32, (cols, size), 1)
    moved = (position == 0) & (place % plan.rows == deep)
    for g in range(groups):
        rows = slice(g * cols, (g + 1) * cols)
        lines = product((back_high[rows, :], back_low[rows, :]), t1i)
        if g == 0:
            lines = jnp.where(moved, pltpu.roll(extra, deep, 1), lines)
        turn_ref[rows, :] = lines
    for start in range(0, groups * cols, lanes):
        block = turn_ref[start : start + lanes, :].T.reshape(count, plan.rows, lanes)
        keep = min(lanes, groups * cols - start)
        real, imag = block[:, :deep], block[:, deep:]
        if keep < lanes:
            place = lax.broadcasted_iota(jnp.int32, real.shape, 2)
            out_ref[:, :, 2 * start : 2 * start + 2 * keep] = jnp.where(place < keep, real, pltpu.roll(imag, keep, 2))[:, :, : 2 * keep]
        else:
            out_ref[:, :, 2 * start : 2 * start + lanes] = real
            out_ref[:, :, 2 * start + lanes : 2 * start + 2 * lanes] = imag


def inverse_kernel(plan, own_ref, in_ref, twiddle_ref, table_ref, *refs):
    out_refs, (line_ref, turn_ref, mid_ref) = refs[: plan.gx], refs[plan.gx :]
    own = own_ref[0]
    cols, groups, here = plan.cols, plan.groups, plan.here
    size = 2 * lanes
    total = groups * cols
    for start in range(0, total, lanes):
        keep = min(lanes, total - start)
        real = in_ref[:, :, 2 * start : 2 * start + lanes]
        imag = pltpu.roll(real, keep, 2) if keep < lanes else in_ref[:, :, 2 * start + lanes : 2 * start + 2 * lanes]
        block = jnp.concatenate([real, imag], 1).reshape(size, lanes)
        turn_ref[start : start + keep, :] = block.T[:keep]
    for g in range(groups):
        rows = slice(g * cols, (g + 1) * cols)
        kind = 1 if g == 0 else 0
        mid_ref[rows, :] = product(halves(turn_ref[rows, :]), (table_ref[kind, 0], table_ref[kind, 1]))
    step_rows = 16

    def chunk(index, carry):
        row = pl.multiple_of(index * step_rows, step_rows)
        real, imag = [], []
        for g in range(1, groups):
            place = pl.ds(g * cols + row, step_rows)
            re, im = mid_ref[place, :lanes], mid_ref[place, lanes:]
            cos, sin = twiddle_ref[0, g : g + 1, :], twiddle_ref[1, g : g + 1, :]
            real.append(re * cos - im * sin)
            imag.append(im * cos + re * sin)
        place = pl.ds(row, step_rows)
        values = radix_inverse(mid_ref[place, :lanes], mid_ref[place, lanes:], real, imag)
        for n, value in enumerate(values):
            line_ref[n, place, :] = value
        return carry

    lax.fori_loop(0, cols // step_rows, chunk, 0)
    for step in range(plan.gx):
        for a in range(here):
            out_refs[step][a] = line_ref[(own ^ step) * here + a]


def final_kernel(plan, own_ref, *refs):
    pieces, (out_hbm, line_ref, block_ref, sems) = refs[: plan.gx], refs[plan.gx :]
    own = own_ref[0]
    sent = []
    for a in range(plan.here):
        for step in range(plan.gx):
            start = pl.multiple_of((own ^ step) * plan.cols, 8)
            line_ref[a, pl.ds(start, plan.cols), :] = pieces[step][a]
        block_ref[a] = line_ref[a].T
        sent.append(pltpu.make_async_copy(block_ref.at[a], out_hbm.at[pl.ds(a * lanes, lanes), :], sems.at[a]))
        sent[-1].start()
    for copy in sent:
        copy.wait()


def make_final(plan, own, pieces, shape):
    whole = pl.BlockSpec(memory_space=pltpu.VMEM)
    run = pl.pallas_call(
        lambda *refs: final_kernel(plan, *refs),
        out_shape=real_array(*shape),
        in_specs=[pl.BlockSpec(memory_space=pltpu.SMEM)] + [whole] * plan.gx,
        out_specs=pl.BlockSpec(memory_space=pl.ANY),
        scratch_shapes=[
            pltpu.VMEM((plan.here, shape[1], lanes), jnp.float32),
            pltpu.VMEM((plan.here, lanes, shape[1]), jnp.float32),
            pltpu.SemaphoreType.DMA((plan.here,)),
        ],
        compiler_params=pltpu.CompilerParams(vmem_limit_bytes=16 << 20),
    )
    return run(own, *pieces)


def swap_gx(plan, pieces):
    got = [pieces[0]]
    for step in range(1, plan.gx):
        got.append(lax.ppermute(pieces[step], "gx", [(k, k ^ step) for k in range(plan.gx)]))
    return got


def build_kernels(plan):
    vmem, f32, bf16 = pltpu.VMEM, jnp.float32, jnp.bfloat16
    size, cols, groups = 2 * lanes, plan.cols, plan.groups
    half = groups * cols
    pieces = [real_array(plan.here, cols, lanes)] * plan.gx
    line = vmem((plan.radix, cols, lanes), f32)

    def local(thickness, bed_uplift, flux_x, flux_y, mass_balance, ice_mask):
        own = lax.axis_index("gx").reshape(1)
        position = (lax.axis_index("gy") * plan.gx + lax.axis_index("gx")).reshape(1)
        fields = (thickness, flux_x, flux_y, mass_balance, ice_mask)
        uplift = send_uplift(plan, own, bed_uplift, flux_x, flux_y)
        lines_u = swap_gx(plan, uplift)
        load = make_load(plan, own, fields)
        lines_v = swap_gx(plan, load)
        twiddle = plan.slot_twiddle()
        tables = np.stack([table_halves(table) for table in plan.slot_matrix()])
        (tails_u,) = call(lambda *refs: tails_kernel(plan, *refs), [real_array(plan.gx, plan.tail, lanes)], [], [], *lines_u)
        side = passed_along(tails_u, "gy", 1)
        partial = make_forward(plan, own, lines_u, (twiddle, tables))
        (spectrum,) = make_forward(plan, own, lines_v, (twiddle, tables), (tails_u, side, *partial))
        thickness_new = make_thickness(plan, own, fields, (tails_u, side))
        received = exchange_all(spectrum)
        source, across = plan.source_matrix(), plan.line_matrix()
        scale = np.float32(1.0 / plan.length_y)
        tables = [table_halves(table) for table in (source, across, across.T * scale, source.T)]
        (middle,) = call(
            lambda *refs: middle_kernel(plan, *refs),
            [real_array(plan.devices, plan.deep, 2 * half)],
            [vmem((2 * half, size), bf16)] * 2 + [vmem((half + cols, size), bf16)] * 2 + [vmem((half + cols, size), f32)],
            [position],
            *([received] + tables + [plan.line_twiddle()]),
        )
        back = exchange_all(middle)
        inverse = np.stack([table_halves(table) for table in plan.slot_inverse()])
        bed = call(
            lambda *refs: inverse_kernel(plan, *refs),
            pieces,
            [line] + [vmem((half, size), f32)] * 2,
            [own],
            *(back, twiddle, inverse),
        )
        lines_b = swap_gx(plan, bed)
        bed_new = make_final(plan, own, lines_b, thickness.shape)
        return thickness_new, bed_new

    return local


def build(plan):
    if plan.devices * plan.rows == 2 * lanes and plan.cols % 16 == 0 and plan.radix <= 16 and plan.gx in (2, 4, 8) and plan.groups * plan.cols % lanes in (0, lanes // 2):
        return build_kernels(plan)

    def local(thickness, bed_uplift, flux_x, flux_y, mass_balance, ice_mask):
        lower_face = passed_along(flux_x[-1:, :], "gx", 1)
        left_face = passed_along(flux_y[:, -1:], "gy", 1)
        flux_below = jnp.concatenate([lower_face, flux_x[:-1, :]], axis=0)
        flux_left = jnp.concatenate([left_face, flux_y[:, :-1]], axis=1)
        divergence = flux_x - flux_below + flux_y - flux_left
        trial = thickness + time_step * (mass_balance - divergence)
        thickness_new = jnp.where(ice_mask == 2, 0.0, jnp.maximum(trial, 0.0))
        load = jnp.where(ice_mask == 0, thickness_new - thickness, 0.0)
        fields = jnp.stack([to_lines(plan, bed_uplift), to_lines(plan, load)], 1)
        lines = exchange_gx(fields)
        lines = lines.transpose(1, 0, 2, 3, 4).reshape(2, plan.radix, plan.cols, lanes)
        received = exchange_all(forward_x(plan, lines))
        position = lax.axis_index("gy") * plan.gx + lax.axis_index("gx")
        back = exchange_all(middle_y(plan, received, position))
        bed = inverse_x(plan, back)
        bed = jnp.stack(bed).reshape(plan.gx, plan.here, plan.cols, lanes)
        bed = exchange_gx(bed)
        bed_new = bed.transpose(1, 3, 0, 2).reshape(plan.here * lanes, plan.gx * plan.cols)
        return thickness_new, bed_new

    return local


def solution(mesh):
    spec = P("gx", "gy")

    def step(*args):
        length_x, length_y = args[0].shape
        plan = Plan(mesh, length_x, length_y)
        body = jax.shard_map(build(plan), mesh=mesh, in_specs=(spec,) * 6, out_specs=(spec, spec), check_vma=False)
        return body(*args)

    return step
```

```python
import math

import jax
import jax.numpy as jnp
import numpy as np
from jax import lax
from jax.experimental import pallas as pl
from jax.experimental.pallas import tpu as pltpu
from jax.sharding import PartitionSpec as P

time_step = 0.5
viscous = 4.0
buoyant = 0.01
flexural = 50.0
lanes = 128
highest = lax.Precision.HIGHEST


class Plan:
    def __init__(self, mesh, length_x, length_y):
        self.gx, self.gy = mesh.shape["gx"], mesh.shape["gy"]
        self.devices = self.gx * self.gy
        self.length_x, self.length_y = length_x, length_y
        self.radix = length_x // lanes
        self.here = self.radix // self.gx
        self.groups = self.radix // 2
        self.cols = length_y // self.devices
        self.m_parts = min(self.devices, lanes)
        self.g_parts = self.devices // self.m_parts
        self.deep = lanes // self.m_parts
        self.own_groups = self.groups // self.g_parts
        self.rows = 2 * self.deep
        self.tail = -(-(2 + 2 * self.here) // 8) * 8
        self.piece_rows = self.here * self.cols + self.tail

    def slot_matrix(self):
        n2 = np.arange(lanes)[None, :]
        m = np.arange(lanes)[:, None]
        theta = 2 * np.pi * (m * n2 % lanes) / lanes
        cos, sin = np.cos(theta), np.sin(theta)
        general = np.stack([np.concatenate([cos, sin], 1), np.concatenate([-sin, cos], 1)])
        half = lanes // 2
        turned = 2 * np.pi * ((2 * (m - half) + 1) * n2 % (2 * lanes)) / (2 * lanes)
        low = np.arange(lanes)[:, None] < half
        real = np.concatenate([np.where(low, cos, 0), np.where(low, 0, np.cos(turned))], 1)
        imag = np.concatenate([np.where(low, -sin, 0), np.where(low, 0, -np.sin(turned))], 1)
        imag[0, :lanes] = np.where(np.arange(lanes) % 2 == 0, 1.0, -1.0)
        first = np.stack([real, imag])
        return np.stack([self._by_part(general), self._by_part(first)]).astype(np.float32)

    def _by_part(self, table):
        split = table.reshape(2, self.m_parts, self.deep, 2 * lanes)
        return split.transpose(1, 0, 2, 3).reshape(2 * lanes, 2 * lanes)

    def slot_inverse(self):
        m = np.arange(lanes)[:, None]
        n2 = np.arange(lanes)[None, :]
        theta = 2 * np.pi * (m * n2 % lanes) / lanes
        cos, sin = np.cos(theta), np.sin(theta)
        general = 2 * np.stack([np.concatenate([cos, sin], 1), np.concatenate([-sin, cos], 1)])
        half = lanes // 2
        turned = 2 * np.pi * ((2 * (m - half) + 1) * n2 % (2 * lanes)) / (2 * lanes)
        low = m < half
        real = 2 * np.concatenate([np.where(low, cos, 0), np.where(low, 0, np.cos(turned))], 1)
        imag = 2 * np.concatenate([np.where(low, -sin, 0), np.where(low, 0, -np.sin(turned))], 1)
        real[0, :lanes] = 1.0
        imag[0, :lanes] = np.where(np.arange(lanes) % 2 == 0, 1.0, -1.0)
        first = np.stack([real, imag])
        return (np.stack([self._by_part(general), self._by_part(first)]) / self.length_x).astype(np.float32)

    def slot_twiddle(self):
        angle = 2 * np.pi * np.arange(self.groups)[:, None] * np.arange(lanes)[None, :] / self.length_x
        return np.stack([np.cos(angle), np.sin(angle)]).astype(np.float32)

    def source_matrix(self):
        count, deep = self.devices, self.deep
        index = np.arange(count)
        theta = 2 * np.pi * (index[:, None] * index[None, :] % count) / count
        cos, sin = np.cos(theta), np.sin(theta)
        out = np.zeros((count, 2, deep, 2, count, deep))
        for q in range(deep):
            out[:, 0, q, 0, :, q] = cos
            out[:, 1, q, 0, :, q] = sin
            out[:, 0, q, 1, :, q] = -sin
            out[:, 1, q, 1, :, q] = cos
        return out.reshape(count * 2 * deep, 2 * count * deep).astype(np.float32)

    def line_matrix(self):
        index = np.arange(self.cols)
        theta = 2 * np.pi * (index[:, None] * index[None, :] % self.cols) / self.cols
        cos, sin = np.cos(theta), np.sin(theta)
        return np.block([[cos, sin], [-sin, cos]]).astype(np.float32)

    def line_twiddle(self):
        angle = 2 * np.pi * np.arange(self.cols)[:, None] * np.arange(self.devices)[None, :] / self.length_y
        angle = np.repeat(angle, self.deep, axis=1)
        return np.stack([np.cos(angle), np.sin(angle)]).astype(np.float32)


def weighted(terms):
    groups = {}
    for coefficient, value in terms:
        size = round(abs(coefficient), 12)
        if size == 0.0:
            continue
        groups.setdefault(size, []).append((coefficient > 0, value))
    total = None
    for size, members in groups.items():
        members.sort(key=lambda member: not member[0])
        positive, part = members[0]
        for sign, value in members[1:]:
            part = part + value if sign == positive else part - value
        if size != 1.0:
            part = part * np.float32(size)
        if total is None:
            total = part if positive else -part
        else:
            total = total + part if positive else total - part
    return total


def radix_forward(values):
    count = len(values)
    half = count // 2
    even = [values[j] + values[count - j] for j in range(1, half)]
    odd = [values[j] - values[count - j] for j in range(1, half)]
    real, imag = [], []
    for g in range(half + 1):
        terms = [(1.0, values[0]), ((-1.0) ** g, values[half])]
        terms += [(math.cos(2 * math.pi * g * (j + 1) / count), even[j]) for j in range(half - 1)]
        real.append(weighted(terms))
        if 0 < g < half:
            imag.append(weighted([(-math.sin(2 * math.pi * g * (j + 1) / count), odd[j]) for j in range(half - 1)]))
    return real, imag


def radix_inverse(first, middle, real, imag):
    half = len(real) + 1
    count = 2 * half
    out = [None] * count
    for j in range(half + 1):
        terms = [(1.0, first), ((-1.0) ** j, middle)]
        terms += [(math.cos(2 * math.pi * g * j / count), real[g - 1]) for g in range(1, half)]
        together = weighted(terms)
        if j in (0, half):
            out[j] = together
            continue
        apart = weighted([(math.sin(2 * math.pi * g * j / count), imag[g - 1]) for g in range(1, half)])
        out[j] = together - apart
        out[count - j] = together + apart
    return out


def mul(a, b):
    return jnp.matmul(a, b, precision=highest)


def exchange_gx(value):
    count = lax.axis_size("gx")
    own = lax.axis_index("gx")
    if count > 8:
        return lax.all_to_all(value, "gx", split_axis=0, concat_axis=0, tiled=True)
    pieces = [lax.dynamic_index_in_dim(value, own, 0, False)]
    for step in range(1, count):
        piece = lax.dynamic_index_in_dim(value, own ^ step, 0, False)
        pieces.append(lax.ppermute(piece, "gx", [(k, k ^ step) for k in range(count)]))
    stacked = jnp.stack(pieces)
    return jnp.stack([lax.dynamic_index_in_dim(stacked, own ^ k, 0, False) for k in range(count)])


def exchange_all(value):
    return lax.all_to_all(value, ("gy", "gx"), split_axis=0, concat_axis=0, tiled=True)


def passed_along(value, axis, steps):
    count = lax.axis_size(axis)
    leading, last = (max(0, -steps), min(count, count - steps))
    return lax.ppermute(value, axis, [(source, source + steps) for source in range(leading, last)])


def forward_x(plan, lines):
    table = plan.slot_matrix()
    cos, sin = plan.slot_twiddle()
    real, imag = radix_forward([lines[:, n] for n in range(plan.radix)])
    blocks = [jnp.concatenate([real[0], real[plan.groups]], -1)]
    for g in range(1, plan.groups):
        re, im = real[g], imag[g - 1]
        blocks.append(jnp.concatenate([re * cos[g] + im * sin[g], im * cos[g] - re * sin[g]], -1))
    first = jnp.einsum("ok,fck->ofc", table[1], blocks[0], precision=highest)
    row = first[plan.deep, 0]
    first = first.at[plan.deep, 0].set(first[0, 1]).at[0, 1].set(row)
    rest = jnp.einsum("ok,gfck->ogfc", table[0], jnp.stack(blocks[1:]), precision=highest)
    spectrum = jnp.concatenate([first[:, None], rest], 1)
    spectrum = spectrum.reshape(plan.m_parts, plan.rows, plan.g_parts, -1)
    return spectrum.transpose(2, 0, 1, 3).reshape(plan.devices, plan.rows, -1)


def spectral_kernels(square):
    kappa = jnp.sqrt(square)
    damping = viscous * kappa
    across = 1.0 / (damping + buoyant + flexural * kappa**4)
    return damping, across


def wave_square(index, length):
    signed = jnp.where(2 * index >= length, index - length, index)
    wave = signed.astype(jnp.float32) * (2.0 * math.pi / length)
    return wave * wave


def middle_y(plan, received, position):
    deep, count, cols = plan.deep, plan.devices, plan.cols
    width = count * deep
    flat = received.reshape(count * plan.rows, -1).T
    mixed = mul(flat, plan.source_matrix())
    mixed = mixed.reshape(plan.own_groups, 2, cols, 2, width)
    cos, sin = plan.line_twiddle()
    re, im = mixed[:, :, :, 0], mixed[:, :, :, 1]
    turned = jnp.concatenate([re * cos + im * sin, im * cos - re * sin], 2)
    spectra = jnp.einsum("wk,gfkl->gfwl", plan.line_matrix(), turned, precision=highest)
    lane = lax.broadcasted_iota(jnp.int32, (1, width), 1)
    q, t = lane % deep, lane // deep
    w = lax.broadcasted_iota(jnp.int32, (cols, 1), 0)
    ky = wave_square(t + count * w, plan.length_y)
    m = (position % plan.m_parts) * deep + q
    base = (position // plan.m_parts) * plan.own_groups
    special = (position == 0) & (q == 0)
    results = []
    for group in range(plan.own_groups):
        g = base + group
        half = lanes // 2
        first = jnp.where(m < half, plan.radix * m, plan.radix // 2 + plan.radix * (m - half))
        index = jnp.where(g == 0, first, g + plan.radix * m)
        damping, across = spectral_kernels(wave_square(index, plan.length_x) + ky)
        u, v = spectra[group, 0], spectra[group, 1]
        ur, ui, vr, vi = u[:cols], u[cols:], v[:cols], v[cols:]
        out_r, out_i = across * (damping * ur - vr), across * (damping * ui - vi)
        if group == 0:
            out_r = jnp.where(special, across * (damping * ur - ui), out_r)
            out_i = jnp.where(special, across * (damping * ui + ur), out_i)
            damping, across = spectral_kernels(np.float32(math.pi) ** 2 + ky)
            extra = jnp.concatenate([across * (damping * vr - vi), across * (damping * vi + vr)], 0)
        results.append(jnp.concatenate([out_r, out_i], 0))
    results.append(extra)
    back = jnp.einsum("kw,gkl->gwl", plan.line_matrix() * np.float32(1.0 / plan.length_y), jnp.stack(results), precision=highest)
    re, im = back[:, :cols], back[:, cols:]
    turned = jnp.concatenate([re * cos - im * sin, im * cos + re * sin], 2)
    lines = jnp.einsum("gcl,sl->gcs", turned, plan.source_matrix(), precision=highest)
    place = lax.broadcasted_iota(jnp.int32, (1, count * plan.rows), 1)
    moved = (position == 0) & (place % plan.rows == deep)
    fixed = jnp.where(moved, jnp.roll(lines[-1], deep, axis=1), lines[0])
    lines = jnp.concatenate([fixed[None], lines[1:-1]], 0)
    return lines.reshape(plan.own_groups * cols, count * plan.rows).T.reshape(count, plan.rows, -1)


def inverse_x(plan, received):
    cols = plan.cols
    table = plan.slot_inverse()
    cos, sin = plan.slot_twiddle()
    split = received.reshape(plan.g_parts, 2 * lanes, plan.own_groups, cols)
    split = split.transpose(0, 2, 3, 1).reshape(plan.groups, cols, 2 * lanes)
    first = mul(split[0], table[1])
    rest = mul(split[1:], table[0])
    real, imag = [], []
    for g in range(1, plan.groups):
        re, im = rest[g - 1, :, :lanes], rest[g - 1, :, lanes:]
        real.append(re * cos[g] - im * sin[g])
        imag.append(im * cos[g] + re * sin[g])
    return radix_inverse(first[:, :lanes], first[:, lanes:], real, imag)


def to_lines(plan, field):
    split = field.reshape(plan.here, lanes, plan.gx, plan.cols)
    return split.transpose(2, 0, 3, 1)


def halves(value):
    high = value.astype(jnp.bfloat16)
    return high, (value - high.astype(jnp.float32)).astype(jnp.bfloat16)


def table_halves(table):
    high = table.astype(jnp.bfloat16)
    return np.concatenate([high, (table - high.astype(np.float32)).astype(jnp.bfloat16)], 0)


def dot(left, right, turned=False):
    dims = (((1,), (1 if turned else 0,)), ((), ()))
    return lax.dot_general(left, right, dims, preferred_element_type=jnp.float32)


def table_times(table, data, turned=False):
    rows = table.shape[0] // 2
    both = dot(table, data[0], turned)
    return both[:rows] + (both[rows:] + dot(table[:rows], data[1], turned))


def times_table(data, table):
    rows, inner = data[0].shape[0], table.shape[0] // 2
    both = dot(jnp.concatenate(data, 0), table[:inner])
    return both[:rows] + (both[rows:] + dot(data[0], table[inner:]))


def call(body, outs, scratch, scalars, *operands):
    scalar = pl.BlockSpec(memory_space=pltpu.SMEM)
    whole = pl.BlockSpec(memory_space=pltpu.VMEM)
    run = pl.pallas_call(
        body,
        out_shape=outs,
        in_specs=[scalar] * len(scalars) + [whole] * len(operands),
        out_specs=[whole] * len(outs),
        scratch_shapes=scratch,
        compiler_params=pltpu.CompilerParams(vmem_limit_bytes=16 << 20),
    )
    return run(*scalars, *operands)


def real_array(*shape):
    return jax.ShapeDtypeStruct(shape, jnp.float32)


def lines_out(plan, own, block, here, turned_ref, out_refs):
    turned_ref[here] = block.T
    for step in range(plan.gx):
        start = pl.multiple_of((own ^ step) * plan.cols, 8)
        out_refs[step][here * plan.cols : (here + 1) * plan.cols, :] = turned_ref[here, pl.ds(start, plan.cols), :]


def own_part(plan, part, row):
    wide = jnp.concatenate([row, row[:, :lanes]], 1)
    wide = jnp.broadcast_to(wide, (8, wide.shape[1]))
    out = wide[:, :lanes]
    for k in range(1, plan.gx):
        start = k * plan.cols
        low = start // lanes * lanes
        block = wide[:, low : low + 2 * lanes]
        if start % lanes:
            block = pltpu.roll(block, 2 * lanes - start % lanes, 1)
        out = jnp.where(part == k, block[:, :lanes], out)
    return out[:1]


def kernel_call(body, outs, scratch, scalars, inputs, faces=()):
    whole = pl.BlockSpec(memory_space=pltpu.VMEM)
    run = pl.pallas_call(
        body,
        out_shape=outs,
        in_specs=[pl.BlockSpec(memory_space=pltpu.SMEM)] * len(scalars) + [pl.BlockSpec(memory_space=pl.ANY)] * len(inputs) + [whole] * len(faces),
        out_specs=[whole] * len(outs),
        scratch_shapes=scratch,
    )
    return run(*scalars, *inputs, *faces)


def uplift_kernel(plan, own_ref, _, uplift_hbm, flux_x_hbm, flux_y_hbm, *refs):
    own = own_ref[0]
    out_refs = refs[: plan.gx]
    field_ref, turned_ref, tail_ref, last_x_ref, last_y_ref, sems, out_sems = refs[plan.gx :]
    rows, cols = uplift_hbm.shape
    copies = [
        pltpu.make_async_copy(flux_x_hbm.at[pl.ds(rows - 8, 8), :], last_x_ref, sems.at[0]),
        pltpu.make_async_copy(flux_y_hbm.at[:, pl.ds(cols - lanes, lanes)], last_y_ref, sems.at[1]),
    ]
    half = lanes // 2
    for part in range(2 * plan.here):
        source = uplift_hbm.at[pl.ds(part * half, half), :]
        copies.append(pltpu.make_async_copy(source, field_ref.at[pl.ds(part * half, half), :], sems.at[2 + part]))
    for copy in copies[2:] + copies[:2]:
        copy.start()
    sent = []
    for here in range(plan.here):
        copies[2 + 2 * here].wait()
        copies[3 + 2 * here].wait()
        turned_ref[here] = field_ref[here * lanes : (here + 1) * lanes, :].T
        for step in range(plan.gx):
            source = turned_ref.at[here, pl.ds(pl.multiple_of((own ^ step) * plan.cols, 8), plan.cols), :]
            target = out_refs[step].at[pl.ds(here * plan.cols, plan.cols), :]
            sent.append(pltpu.make_async_copy(source, target, out_sems.at[here, step]))
            sent[-1].start()
    copies[0].wait()
    copies[1].wait()
    last_x = last_x_ref[7:8, :]
    last_y = last_y_ref[...].T[lanes - 1 : lanes, :]
    parts = [last[:, a * lanes : (a + 1) * lanes] for last in (last_x, last_y) for a in range(plan.here)]
    parts.append(jnp.zeros((plan.tail - 2 * plan.here, lanes), jnp.float32))
    tail_ref[...] = jnp.concatenate(parts, 0)
    for step in range(plan.gx):
        target = out_refs[step].at[pl.ds(plan.here * plan.cols, plan.tail), :]
        sent.append(pltpu.make_async_copy(tail_ref, target, out_sems.at[plan.here, step]))
        sent[-1].start()
    for copy in sent:
        copy.wait()


def send_uplift(plan, own, across_y, bed_uplift, flux_x, flux_y):
    rows, cols = bed_uplift.shape
    run = pl.pallas_call(
        lambda *refs: uplift_kernel(plan, *refs),
        out_shape=[real_array(plan.piece_rows, lanes)] * plan.gx,
        in_specs=[pl.BlockSpec(memory_space=pltpu.SMEM)] * 2 + [pl.BlockSpec(memory_space=pl.ANY)] * 3,
        out_specs=[pl.BlockSpec(memory_space=pl.ANY)] * plan.gx,
        scratch_shapes=[
            pltpu.VMEM((rows, cols), jnp.float32),
            pltpu.VMEM((plan.here, cols, lanes), jnp.float32),
            pltpu.VMEM((plan.tail, lanes), jnp.float32),
            pltpu.VMEM((8, cols), jnp.float32),
            pltpu.VMEM((rows, lanes), jnp.float32),
            pltpu.SemaphoreType.DMA((2 + 2 * plan.here,)),
            pltpu.SemaphoreType.DMA((plan.here + 1, plan.gx)),
        ],
    )
    return run(own, across_y, bed_uplift, flux_x, flux_y)


def fetch_fields(plan, sources, mask_ref, floats_ref, sems):
    targets = [floats_ref.at[k] for k in range(4)] + [mask_ref]
    copies = []
    for here in range(plan.here):
        rows = pl.ds(here * lanes, lanes)
        group = [
            pltpu.make_async_copy(source.at[rows, :], target.at[rows, :], sems.at[here, k])
            for k, (source, target) in enumerate(zip(sources, targets))
        ]
        for copy in group:
            copy.start()
        copies.append(group)
    return copies


def trial_block(floats_ref, here, above, left_edge):
    rows = slice(here * lanes, (here + 1) * lanes)
    fx, fy = floats_ref[1, rows, :], floats_ref[2, rows, :]
    row = lax.broadcasted_iota(jnp.int32, fx.shape, 0)
    col = lax.broadcasted_iota(jnp.int32, fx.shape, 1)
    if here:
        above = floats_ref[1, here * lanes - 1 : here * lanes, :]
    below = jnp.where(row == 0, jnp.broadcast_to(above, fx.shape) if here or above.ndim else above, pltpu.roll(fx, 1, 0))
    left = jnp.where(col == 0, left_edge, pltpu.roll(fy, 1, 1))
    divergence = fx - below + fy - left
    return floats_ref[0, rows, :] + time_step * (floats_ref[3, rows, :] - divergence)


hidden = np.float32(-1e30)


def load_kernel(plan, own_ref, *refs):
    own = own_ref[0]
    sources, refs = refs[:5], refs[5:]
    line_refs, (mask_ref, floats_ref, turned_ref, sems) = refs[: plan.gx], refs[plan.gx :]
    copies = fetch_fields(plan, sources, mask_ref, floats_ref, sems)
    columns_trial, columns_thick = [], []
    for here in range(plan.here):
        for copy in copies[here]:
            copy.wait()
        rows = slice(here * lanes, (here + 1) * lanes)
        trial = trial_block(floats_ref, here, jnp.float32(0.0), 0.0)
        free = mask_ref[rows, :] == 0
        thick = jnp.where(free, floats_ref[0, rows, :], 0.0)
        trial = jnp.where(free, trial, hidden)
        lines_out(plan, own, jnp.maximum(trial, 0.0) - thick, here, turned_ref, line_refs)
        lane = lax.broadcasted_iota(jnp.int32, (lanes, lanes), 1)
        packed = jnp.where(lane == 0, trial[:, :lanes], pltpu.roll(thick[:, :lanes], 1, 1)).T
        columns_trial.append(packed[0:1])
        columns_thick.append(packed[1:2])
        if here == 0:
            row_trial, row_thick = trial[0:1], thick[0:1]
    tail = plan.here * plan.cols
    rest = plan.tail - 2 - 2 * plan.here
    for step in range(plan.gx):
        parts = [own_part(plan, own ^ step, row_trial), own_part(plan, own ^ step, row_thick)] + columns_trial + columns_thick
        if rest:
            parts.append(jnp.zeros((rest, lanes), jnp.float32))
        line_refs[step][tail : tail + plan.tail, :] = jnp.concatenate(parts, 0)


def field_scratch(shape):
    return [
        pltpu.VMEM(shape, jnp.int32),
        pltpu.VMEM((4,) + shape, jnp.float32),
    ]


def make_load(plan, own, fields):
    shape = fields[0].shape
    scratch = field_scratch(shape) + [
        pltpu.VMEM((plan.here, shape[1], lanes), jnp.float32),
        pltpu.SemaphoreType.DMA((plan.here, 5)),
    ]
    outs = [real_array(plan.piece_rows, lanes)] * plan.gx
    return kernel_call(lambda *refs: load_kernel(plan, *refs), outs, scratch, [own], fields)


def row_above(plan, own, block, tails):
    above = [jnp.zeros((1, lanes), jnp.float32)] * plan.here
    for step in range(plan.gx):
        match = (own ^ step) + 1 == block
        above = [jnp.where(match, tails[step][a : a + 1, :], above[a]) for a in range(plan.here)]
    return jnp.concatenate(above, 1)


def thickness_kernel(plan, own_ref, *refs):
    own = own_ref[0]
    sources, (tails_ref, side_ref, out_ref, mask_ref, floats_ref, sems) = refs[:5], refs[5:]
    copies = fetch_fields(plan, sources, mask_ref, floats_ref, sems)
    above = row_above(plan, own, own, [tails_ref[step] for step in range(plan.gx)])
    for here in range(plan.here):
        for copy in copies[here]:
            copy.wait()
        rows = slice(here * lanes, (here + 1) * lanes)
        side = jnp.broadcast_to(side_ref[0, plan.here + here : plan.here + here + 1, :], (lanes, lanes)).T
        side = jnp.concatenate([side] * (out_ref.shape[1] // lanes), 1)
        trial = trial_block(floats_ref, here, above, side)
        out_ref[rows, :] = jnp.where(mask_ref[rows, :] == 2, 0.0, jnp.maximum(trial, 0.0))


def make_thickness(plan, own, fields, faces):
    shape = fields[0].shape
    scratch = field_scratch(shape) + [pltpu.SemaphoreType.DMA((plan.here, 5))]
    return kernel_call(lambda *refs: thickness_kernel(plan, *refs), [real_array(*shape)], scratch, [own], fields, faces)[0]


def finish_load(plan, own, line_ref, uplift_tails, load_tails, side_ref):
    cols, here = plan.cols, plan.here
    lane = lax.broadcasted_iota(jnp.int32, (1, lanes), 1)
    wide_lane = lax.broadcasted_iota(jnp.int32, (cols, lanes), 1)
    above, new = [], []
    for step in range(plan.gx):
        above.append(own_part(plan, own, row_above(plan, own, own ^ step, uplift_tails)))
        tail = load_tails[step]
        new.append(jnp.maximum(tail[0:1, :] + time_step * above[step], 0.0) - tail[1:2, :])
    turned = jnp.concatenate(new + [jnp.zeros((lanes - plan.gx, lanes), jnp.float32)], 0).T[:cols]
    for step in range(plan.gx):
        place = (own ^ step) * here
        first = pltpu.roll(turned, lanes - step, 1) if step else turned
        line_ref[place] = jnp.where(wide_lane == 0, first, line_ref[place])

    @pl.when(own == 0)
    def _():
        for step in range(plan.gx):
            tail = load_tails[step]
            for a in range(here):
                corner = jnp.where(lane == 0, jnp.broadcast_to(above[step][:, :1], (1, lanes)), 0.0) if a == 0 else 0.0
                trial = tail[2 + a : 3 + a, :] + time_step * (side_ref[step, here + a : here + a + 1, :] + corner)
                line_ref[step * here + a, 0:1, :] = jnp.maximum(trial, 0.0) - tail[2 + here + a : 3 + here + a, :]


def tails_kernel(plan, *refs):
    pieces, tails_ref = refs[: plan.gx], refs[plan.gx]
    start = plan.here * plan.cols
    for step in range(plan.gx):
        tails_ref[step] = pieces[step][start : start + plan.tail, :]


def forward_kernel(plan, lead, own_ref, *refs):
    pieces, refs = refs[: plan.gx], refs[plan.gx :]
    cols, radix, groups, here = plan.cols, plan.radix, plan.groups, plan.here
    own = own_ref[0]
    tail = slice(here * cols, here * cols + plan.tail)
    if lead:
        uplift_tails, side_ref, edge_ref, head_ref, _, twiddle_ref, table_ref, *refs = refs
        out_hbm, line_ref, high_ref, low_ref, block_ref, sems = refs
    else:
        twiddle_ref, table_ref, out_hbm, edge_ref, head_ref, line_ref, high_ref, low_ref, block_ref, sems = refs
    step_rows = 16
    total = groups * cols
    for step in range(plan.gx):
        for a in range(here):
            line_ref[(own ^ step) * here + a] = pieces[step][a * cols : (a + 1) * cols, :]
    if lead:
        tails = [uplift_tails[step] for step in range(plan.gx)]
        finish_load(plan, own, line_ref, tails, [piece[tail, :] for piece in pieces], side_ref)
    skip = lead % lanes

    def chunk(index, carry):
        row = pl.multiple_of(index * step_rows, step_rows)
        real, imag = radix_forward([line_ref[n, pl.ds(row, step_rows), :] for n in range(radix)])
        for g in range(groups):
            if g == 0:
                first, second = real[0], real[groups]
            else:
                cos, sin = twiddle_ref[0, g : g + 1, :], twiddle_ref[1, g : g + 1, :]
                first = real[g] * cos + imag[g - 1] * sin
                second = imag[g - 1] * cos - real[g] * sin
            high, low = halves(jnp.concatenate([first, second], 1))
            place = pl.ds(skip + g * cols + row, step_rows)
            high_ref[place, :] = high
            low_ref[place, :] = low
        return carry

    lax.fori_loop(0, cols // step_rows, chunk, 0)
    for edge in ((0, skip), (skip + total, high_ref.shape[0])):
        if edge[0] < edge[1]:
            high_ref[edge[0] : edge[1], :] = jnp.zeros((edge[1] - edge[0], 2 * lanes), jnp.bfloat16)
            low_ref[edge[0] : edge[1], :] = jnp.zeros((edge[1] - edge[0], 2 * lanes), jnp.bfloat16)
    before = (lead - skip) // lanes
    blocks = high_ref.shape[0] // lanes
    sent = []

    def send(block):
        lane = pl.ds((before + block) * lanes, lanes)
        sent.append(pltpu.make_async_copy(block_ref.at[block], out_hbm.at[:, :, lane], sems.at[block]))
        sent[-1].start()

    held = -(-(skip + cols) // lanes) if lead else 0
    end = skip + cols
    special = -(-end // lanes) * lanes
    first = table_times(table_ref[1], (high_ref[:special, :], low_ref[:special, :]), True)
    for block in range(blocks):
        start = block * lanes
        if block % 2 == 0:
            rows = slice(start, min(start + 2 * lanes, blocks * lanes))
            pair = table_times(table_ref[0], (high_ref[rows, :], low_ref[rows, :]), True)
        out = pair[:, (block % 2) * lanes : (block % 2 + 1) * lanes]
        if start < end:
            lane = lax.broadcasted_iota(jnp.int32, (2 * lanes, lanes), 1)
            out = jnp.where(lane < end - start, first[:, start : start + lanes], out)
        out = out.reshape(plan.devices, plan.rows, lanes)
        if start < skip:
            lane = lax.broadcasted_iota(jnp.int32, out.shape, 2)
            out = jnp.where(lane < skip - start, edge_ref[...], out)
        if not lead and (block + 1) * lanes > total:
            edge_ref[...] = out
            continue
        block_ref[block] = out
        if not lead and block == 0:
            head_ref[...] = out[0]
        if block + 1 == held:
            two = jnp.concatenate([block_ref[k, 0] for k in range(held)], 1)
            width = held * lanes
            row = lax.broadcasted_iota(jnp.int32, two.shape, 0)
            lane = lax.broadcasted_iota(jnp.int32, two.shape, 1)
            head = head_ref[...]
            wide = pltpu.roll(jnp.concatenate([head] * held, 1), plan.deep, 0)
            to_right = pltpu.roll(wide, skip, 1) if skip else wide
            swapped = pltpu.roll(two, plan.deep, 0)
            to_left = pltpu.roll(swapped, width - skip, 1) if skip else swapped
            take = (row[:, :lanes] == plan.deep) & (lane[:, :lanes] < cols)
            head_out = block_ref.at[blocks, 0]
            head_out[...] = jnp.where(take, to_left[:, :lanes], head)
            take = (row == 0) & (lane >= skip) & (lane < skip + cols)
            fixed = jnp.where(take, to_right, two)
            for k in range(held):
                block_ref[k, 0] = fixed[:, k * lanes : (k + 1) * lanes]
                send(k)
            sent.append(pltpu.make_async_copy(head_out, out_hbm.at[0, :, pl.ds(0, lanes)], sems.at[blocks]))
            sent[-1].start()
        elif block >= held:
            send(block)
    for copy in sent:
        copy.wait()


def make_forward(plan, own, pieces, tables, before=None):
    half = plan.groups * plan.cols
    lead = half if before else 0
    skip = lead % lanes
    blocks = -(-(skip + half) // lanes)
    any_space, whole = pl.BlockSpec(memory_space=pl.ANY), pl.BlockSpec(memory_space=pltpu.VMEM)
    outs, out_specs, operands, alias = [real_array(plan.devices, plan.rows, 2 * half)], [any_space], list(pieces), {}
    in_specs = [pl.BlockSpec(memory_space=pltpu.SMEM)] + [whole] * len(pieces)
    if before:
        tails, side, spectrum, edge, head = before
        operands += [tails, side, edge, head, spectrum]
        in_specs += [whole] * 4 + [any_space]
        alias = {len(operands): 0}
    else:
        outs += [real_array(plan.devices, plan.rows, lanes), real_array(plan.rows, lanes)]
        out_specs += [whole] * 2
    run = pl.pallas_call(
        lambda *refs: forward_kernel(plan, lead, *refs),
        out_shape=outs,
        in_specs=in_specs + [whole] * 2,
        out_specs=out_specs,
        scratch_shapes=[
            pltpu.VMEM((plan.radix, plan.cols, lanes), jnp.float32),
            pltpu.VMEM((blocks * lanes, 2 * lanes), jnp.bfloat16),
            pltpu.VMEM((blocks * lanes, 2 * lanes), jnp.bfloat16),
            pltpu.VMEM((blocks + 1, plan.devices, plan.rows, lanes), jnp.float32),
            pltpu.SemaphoreType.DMA((blocks + 1,)),
        ],
        input_output_aliases=alias,
        compiler_params=pltpu.CompilerParams(vmem_limit_bytes=16 << 20),
    )
    return run(own, *operands, *tables)


def middle_kernel(plan, own_ref, across_ref, in_ref, t1_ref, t2_ref, t2i_ref, t1i_ref, twiddle_ref, out_ref, high_ref, low_ref, back_high, back_low, turn_ref, mixed_ref):
    position = across_ref[0] * plan.gx + own_ref[0]
    cols, groups, deep, count = plan.cols, plan.groups, plan.deep, plan.devices
    width, size = lanes, 2 * lanes
    for start in range(0, 2 * groups * cols, lanes):
        block = in_ref[:, :, start : start + lanes].reshape(size, lanes).T
        high_ref[start : start + lanes, :], low_ref[start : start + lanes, :] = halves(block)
    step = 2 * groups * cols // 4
    for start in range(0, 2 * groups * cols, step):
        rows = slice(start, start + step)
        mixed_ref[rows, :] = times_table((high_ref[rows, :], low_ref[rows, :]), t1_ref[...])
    cos, sin = twiddle_ref[0], twiddle_ref[1]
    lane = lax.broadcasted_iota(jnp.int32, (1, width), 1)
    q, t = lane % deep, lane // deep
    w = lax.broadcasted_iota(jnp.int32, (cols, width), 0)
    ky = wave_square(t + count * w, plan.length_y)
    m = position * deep + q
    special = jnp.broadcast_to((position == 0) & (q == 0), (cols, width))
    results = []
    for g in range(groups):
        sides = []
        for field in range(2):
            part = mixed_ref[(field * groups + g) * cols : (field * groups + g + 1) * cols, :]
            re, im = part[:, :width], part[:, width:]
            sides.append(jnp.concatenate([re * cos + im * sin, im * cos - re * sin], 0))
        spectra = table_times(t2_ref[...], halves(jnp.concatenate(sides, 1)))
        ur, vr = spectra[:cols, :width], spectra[:cols, width:]
        ui, vi = spectra[cols:, :width], spectra[cols:, width:]
        half = lanes // 2
        if g == 0:
            index = jnp.where(m < half, plan.radix * m, plan.radix // 2 + plan.radix * (m - half))
        else:
            index = g + plan.radix * m
        damping, across = spectral_kernels(wave_square(index, plan.length_x) + ky)
        out_r, out_i = across * (damping * ur - vr), across * (damping * ui - vi)
        if g == 0:
            out_r = jnp.where(special, across * (damping * ur - ui), out_r)
            out_i = jnp.where(special, across * (damping * ui + ur), out_i)
            damping, across = spectral_kernels(np.float32(math.pi) ** 2 + ky)
            extra = jnp.concatenate([across * (damping * vr - vi), across * (damping * vi + vr)], 0)
        results.append(jnp.concatenate([out_r, out_i], 0))
    results.append(extra)
    for g in range(0, groups + 1, 2):
        pair = results[g : g + 2]
        back = table_times(t2i_ref[...], halves(jnp.concatenate(pair, 1)))
        for k in range(len(pair)):
            re, im = back[:cols, k * width : (k + 1) * width], back[cols:, k * width : (k + 1) * width]
            turned = jnp.concatenate([re * cos - im * sin, im * cos + re * sin], 1)
            place = slice((g + k) * cols, (g + k + 1) * cols)
            back_high[place, :], back_low[place, :] = halves(turned)
    total = (groups + 1) * cols
    cuts = [total * k // 2 // 16 * 16 for k in range(2)] + [total]
    for start, stop in zip(cuts, cuts[1:]):
        rows = slice(start, stop)
        turn_ref[rows, :] = times_table((back_high[rows, :], back_low[rows, :]), t1i_ref[...])
    place = lax.broadcasted_iota(jnp.int32, (cols, size), 1)
    moved = (position == 0) & (place % plan.rows == deep)
    extra = turn_ref[groups * cols : (groups + 1) * cols, :]
    turn_ref[:cols, :] = jnp.where(moved, pltpu.roll(extra, deep, 1), turn_ref[:cols, :])
    for start in range(0, groups * cols, lanes):
        block = turn_ref[start : start + lanes, :].T.reshape(count, plan.rows, lanes)
        keep = min(lanes, groups * cols - start)
        real, imag = block[:, :deep], block[:, deep:]
        if keep < lanes:
            place = lax.broadcasted_iota(jnp.int32, real.shape, 2)
            out_ref[:, :, 2 * start : 2 * start + 2 * keep] = jnp.where(place < keep, real, pltpu.roll(imag, keep, 2))[:, :, : 2 * keep]
        else:
            out_ref[:, :, 2 * start : 2 * start + lanes] = real
            out_ref[:, :, 2 * start + lanes : 2 * start + 2 * lanes] = imag


def inverse_kernel(plan, own_ref, in_ref, twiddle_ref, table_ref, *refs):
    out_refs, (line_ref, turn_ref, mid_ref) = refs[: plan.gx], refs[plan.gx :]
    own = own_ref[0]
    cols, groups, here = plan.cols, plan.groups, plan.here
    size = 2 * lanes
    total = groups * cols
    for start in range(0, total, lanes):
        keep = min(lanes, total - start)
        real = in_ref[:, :, 2 * start : 2 * start + lanes]
        imag = pltpu.roll(real, keep, 2) if keep < lanes else in_ref[:, :, 2 * start + lanes : 2 * start + 2 * lanes]
        block = jnp.concatenate([real, imag], 1).reshape(size, lanes)
        turn_ref[start : start + keep, :] = block.T[:keep]
    mid_ref[:cols, :] = times_table(halves(turn_ref[:cols, :]), table_ref[1])
    mid_ref[cols:, :] = times_table(halves(turn_ref[cols:, :]), table_ref[0])
    step_rows = 16

    def chunk(index, carry):
        row = pl.multiple_of(index * step_rows, step_rows)
        real, imag = [], []
        for g in range(1, groups):
            place = pl.ds(g * cols + row, step_rows)
            re, im = mid_ref[place, :lanes], mid_ref[place, lanes:]
            cos, sin = twiddle_ref[0, g : g + 1, :], twiddle_ref[1, g : g + 1, :]
            real.append(re * cos - im * sin)
            imag.append(im * cos + re * sin)
        place = pl.ds(row, step_rows)
        values = radix_inverse(mid_ref[place, :lanes], mid_ref[place, lanes:], real, imag)
        for n, value in enumerate(values):
            line_ref[n, place, :] = value
        return carry

    lax.fori_loop(0, cols // step_rows, chunk, 0)
    for step in range(plan.gx):
        for a in range(here):
            out_refs[step][a] = line_ref[(own ^ step) * here + a]


def final_kernel(plan, own_ref, *refs):
    pieces, (out_hbm, line_ref, block_ref, sems) = refs[: plan.gx], refs[plan.gx :]
    own = own_ref[0]
    sent = []
    for a in range(plan.here):
        for step in range(plan.gx):
            start = pl.multiple_of((own ^ step) * plan.cols, 8)
            line_ref[a, pl.ds(start, plan.cols), :] = pieces[step][a]
        block_ref[a] = line_ref[a].T
        sent.append(pltpu.make_async_copy(block_ref.at[a], out_hbm.at[pl.ds(a * lanes, lanes), :], sems.at[a]))
        sent[-1].start()
    for copy in sent:
        copy.wait()


def make_final(plan, own, pieces, shape):
    whole = pl.BlockSpec(memory_space=pltpu.VMEM)
    run = pl.pallas_call(
        lambda *refs: final_kernel(plan, *refs),
        out_shape=real_array(*shape),
        in_specs=[pl.BlockSpec(memory_space=pltpu.SMEM)] + [whole] * plan.gx,
        out_specs=pl.BlockSpec(memory_space=pl.ANY),
        scratch_shapes=[
            pltpu.VMEM((plan.here, shape[1], lanes), jnp.float32),
            pltpu.VMEM((plan.here, lanes, shape[1]), jnp.float32),
            pltpu.SemaphoreType.DMA((plan.here,)),
        ],
        compiler_params=pltpu.CompilerParams(vmem_limit_bytes=16 << 20),
    )
    return run(own, *pieces)


def swap_gx(plan, pieces):
    got = [pieces[0]]
    for step in range(1, plan.gx):
        got.append(lax.ppermute(pieces[step], "gx", [(k, k ^ step) for k in range(plan.gx)]))
    return got


def build_kernels(plan):
    vmem, f32, bf16 = pltpu.VMEM, jnp.float32, jnp.bfloat16
    size, cols, groups = 2 * lanes, plan.cols, plan.groups
    half = groups * cols
    pieces = [real_array(plan.here, cols, lanes)] * plan.gx
    line = vmem((plan.radix, cols, lanes), f32)

    def local(thickness, bed_uplift, flux_x, flux_y, mass_balance, ice_mask):
        own, across_y = lax.axis_index("gx").reshape(1), lax.axis_index("gy").reshape(1)
        fields = (thickness, flux_x, flux_y, mass_balance, ice_mask)
        uplift = send_uplift(plan, own, across_y, bed_uplift, flux_x, flux_y)
        lines_u = swap_gx(plan, uplift)
        load = make_load(plan, own, fields)
        lines_v = swap_gx(plan, load)
        twiddle = plan.slot_twiddle()
        tables = np.stack([table_halves(table) for table in plan.slot_matrix()])
        (tails_u,) = call(lambda *refs: tails_kernel(plan, *refs), [real_array(plan.gx, plan.tail, lanes)], [], [], *lines_u)
        side = passed_along(tails_u, "gy", 1)
        partial = make_forward(plan, own, lines_u, (twiddle, tables))
        (spectrum,) = make_forward(plan, own, lines_v, (twiddle, tables), (tails_u, side, *partial))
        thickness_new = make_thickness(plan, own, fields, (tails_u, side))
        received = exchange_all(spectrum)
        source, across = plan.source_matrix(), plan.line_matrix()
        scale = np.float32(1.0 / plan.length_y)
        tables = [table_halves(table) for table in (source, across, across.T * scale, source.T)]
        (middle,) = call(
            lambda *refs: middle_kernel(plan, *refs),
            [real_array(plan.devices, plan.deep, 2 * half)],
            [vmem((2 * half, size), bf16)] * 2 + [vmem((half + cols, size), bf16)] * 2 + [vmem((half + cols, size), f32), vmem((2 * half, size), f32)],
            [own, across_y],
            *([received] + tables + [plan.line_twiddle()]),
        )
        back = exchange_all(middle)
        inverse = np.stack([table_halves(table) for table in plan.slot_inverse()])
        bed = call(
            lambda *refs: inverse_kernel(plan, *refs),
            pieces,
            [line] + [vmem((half, size), f32)] * 2,
            [own],
            *(back, twiddle, inverse),
        )
        lines_b = swap_gx(plan, bed)
        bed_new = make_final(plan, own, lines_b, thickness.shape)
        return thickness_new, bed_new

    return local


def build(plan):
    if plan.devices * plan.rows == 2 * lanes and plan.cols % 16 == 0 and plan.radix <= 16 and plan.gx in (2, 4, 8) and plan.groups * plan.cols % lanes in (0, lanes // 2):
        return build_kernels(plan)

    def local(thickness, bed_uplift, flux_x, flux_y, mass_balance, ice_mask):
        lower_face = passed_along(flux_x[-1:, :], "gx", 1)
        left_face = passed_along(flux_y[:, -1:], "gy", 1)
        flux_below = jnp.concatenate([lower_face, flux_x[:-1, :]], axis=0)
        flux_left = jnp.concatenate([left_face, flux_y[:, :-1]], axis=1)
        divergence = flux_x - flux_below + flux_y - flux_left
        trial = thickness + time_step * (mass_balance - divergence)
        thickness_new = jnp.where(ice_mask == 2, 0.0, jnp.maximum(trial, 0.0))
        load = jnp.where(ice_mask == 0, thickness_new - thickness, 0.0)
        fields = jnp.stack([to_lines(plan, bed_uplift), to_lines(plan, load)], 1)
        lines = exchange_gx(fields)
        lines = lines.transpose(1, 0, 2, 3, 4).reshape(2, plan.radix, plan.cols, lanes)
        received = exchange_all(forward_x(plan, lines))
        position = lax.axis_index("gy") * plan.gx + lax.axis_index("gx")
        back = exchange_all(middle_y(plan, received, position))
        bed = inverse_x(plan, back)
        bed = jnp.stack(bed).reshape(plan.gx, plan.here, plan.cols, lanes)
        bed = exchange_gx(bed)
        bed_new = bed.transpose(1, 3, 0, 2).reshape(plan.here * lanes, plan.gx * plan.cols)
        return thickness_new, bed_new

    return local


def solution(mesh):
    spec = P("gx", "gy")

    def step(*args):
        length_x, length_y = args[0].shape
        plan = Plan(mesh, length_x, length_y)
        body = jax.shard_map(build(plan), mesh=mesh, in_specs=(spec,) * 6, out_specs=(spec, spec), check_vma=False)
        return body(*args)

    return step
```

```python
import math

import jax
import jax.numpy as jnp
import numpy as np
from jax import lax
from jax.experimental import pallas as pl
from jax.experimental.pallas import tpu as pltpu
from jax.sharding import PartitionSpec as P

time_step = 0.5
viscous = 4.0
buoyant = 0.01
flexural = 50.0
lanes = 128
highest = lax.Precision.HIGHEST


class Plan:
    def __init__(self, mesh, length_x, length_y):
        self.gx, self.gy = mesh.shape["gx"], mesh.shape["gy"]
        self.devices = self.gx * self.gy
        self.length_x, self.length_y = length_x, length_y
        self.radix = length_x // lanes
        self.here = self.radix // self.gx
        self.groups = self.radix // 2
        self.cols = length_y // self.devices
        self.m_parts = min(self.devices, lanes)
        self.g_parts = self.devices // self.m_parts
        self.deep = lanes // self.m_parts
        self.own_groups = self.groups // self.g_parts
        self.rows = 2 * self.deep
        self.tail = -(-(2 + 2 * self.here) // 8) * 8
        self.piece_rows = self.here * self.cols + self.tail

    def slot_matrix(self):
        n2 = np.arange(lanes)[None, :]
        m = np.arange(lanes)[:, None]
        theta = 2 * np.pi * (m * n2 % lanes) / lanes
        cos, sin = np.cos(theta), np.sin(theta)
        general = np.stack([np.concatenate([cos, sin], 1), np.concatenate([-sin, cos], 1)])
        half = lanes // 2
        turned = 2 * np.pi * ((2 * (m - half) + 1) * n2 % (2 * lanes)) / (2 * lanes)
        low = np.arange(lanes)[:, None] < half
        real = np.concatenate([np.where(low, cos, 0), np.where(low, 0, np.cos(turned))], 1)
        imag = np.concatenate([np.where(low, -sin, 0), np.where(low, 0, -np.sin(turned))], 1)
        imag[0, :lanes] = np.where(np.arange(lanes) % 2 == 0, 1.0, -1.0)
        first = np.stack([real, imag])
        return np.stack([self._by_part(general), self._by_part(first)]).astype(np.float32)

    def _by_part(self, table):
        split = table.reshape(2, self.m_parts, self.deep, 2 * lanes)
        return split.transpose(1, 0, 2, 3).reshape(2 * lanes, 2 * lanes)

    def slot_inverse(self):
        m = np.arange(lanes)[:, None]
        n2 = np.arange(lanes)[None, :]
        theta = 2 * np.pi * (m * n2 % lanes) / lanes
        cos, sin = np.cos(theta), np.sin(theta)
        general = 2 * np.stack([np.concatenate([cos, sin], 1), np.concatenate([-sin, cos], 1)])
        half = lanes // 2
        turned = 2 * np.pi * ((2 * (m - half) + 1) * n2 % (2 * lanes)) / (2 * lanes)
        low = m < half
        real = 2 * np.concatenate([np.where(low, cos, 0), np.where(low, 0, np.cos(turned))], 1)
        imag = 2 * np.concatenate([np.where(low, -sin, 0), np.where(low, 0, -np.sin(turned))], 1)
        real[0, :lanes] = 1.0
        imag[0, :lanes] = np.where(np.arange(lanes) % 2 == 0, 1.0, -1.0)
        first = np.stack([real, imag])
        return (np.stack([self._by_part(general), self._by_part(first)]) / self.length_x).astype(np.float32)

    def slot_twiddle(self):
        angle = 2 * np.pi * np.arange(self.groups)[:, None] * np.arange(lanes)[None, :] / self.length_x
        return np.stack([np.cos(angle), np.sin(angle)]).astype(np.float32)

    def source_matrix(self):
        count, deep = self.devices, self.deep
        index = np.arange(count)
        theta = 2 * np.pi * (index[:, None] * index[None, :] % count) / count
        cos, sin = np.cos(theta), np.sin(theta)
        out = np.zeros((count, 2, deep, 2, count, deep))
        for q in range(deep):
            out[:, 0, q, 0, :, q] = cos
            out[:, 1, q, 0, :, q] = sin
            out[:, 0, q, 1, :, q] = -sin
            out[:, 1, q, 1, :, q] = cos
        return out.reshape(count * 2 * deep, 2 * count * deep).astype(np.float32)

    def line_matrix(self):
        index = np.arange(self.cols)
        theta = 2 * np.pi * (index[:, None] * index[None, :] % self.cols) / self.cols
        cos, sin = np.cos(theta), np.sin(theta)
        return np.block([[cos, sin], [-sin, cos]]).astype(np.float32)

    def line_twiddle(self):
        angle = 2 * np.pi * np.arange(self.cols)[:, None] * np.arange(self.devices)[None, :] / self.length_y
        angle = np.repeat(angle, self.deep, axis=1)
        return np.stack([np.cos(angle), np.sin(angle)]).astype(np.float32)


def weighted(terms):
    groups = {}
    for coefficient, value in terms:
        size = round(abs(coefficient), 12)
        if size == 0.0:
            continue
        groups.setdefault(size, []).append((coefficient > 0, value))
    total = None
    for size, members in groups.items():
        members.sort(key=lambda member: not member[0])
        positive, part = members[0]
        for sign, value in members[1:]:
            part = part + value if sign == positive else part - value
        if size != 1.0:
            part = part * np.float32(size)
        if total is None:
            total = part if positive else -part
        else:
            total = total + part if positive else total - part
    return total


def radix_forward(values):
    count = len(values)
    half = count // 2
    even = [values[j] + values[count - j] for j in range(1, half)]
    odd = [values[j] - values[count - j] for j in range(1, half)]
    real, imag = [], []
    for g in range(half + 1):
        terms = [(1.0, values[0]), ((-1.0) ** g, values[half])]
        terms += [(math.cos(2 * math.pi * g * (j + 1) / count), even[j]) for j in range(half - 1)]
        real.append(weighted(terms))
        if 0 < g < half:
            imag.append(weighted([(-math.sin(2 * math.pi * g * (j + 1) / count), odd[j]) for j in range(half - 1)]))
    return real, imag


def radix_inverse(first, middle, real, imag):
    half = len(real) + 1
    count = 2 * half
    out = [None] * count
    for j in range(half + 1):
        terms = [(1.0, first), ((-1.0) ** j, middle)]
        terms += [(math.cos(2 * math.pi * g * j / count), real[g - 1]) for g in range(1, half)]
        together = weighted(terms)
        if j in (0, half):
            out[j] = together
            continue
        apart = weighted([(math.sin(2 * math.pi * g * j / count), imag[g - 1]) for g in range(1, half)])
        out[j] = together - apart
        out[count - j] = together + apart
    return out


def mul(a, b):
    return jnp.matmul(a, b, precision=highest)


def exchange_gx(value):
    count = lax.axis_size("gx")
    own = lax.axis_index("gx")
    if count > 8:
        return lax.all_to_all(value, "gx", split_axis=0, concat_axis=0, tiled=True)
    pieces = [lax.dynamic_index_in_dim(value, own, 0, False)]
    for step in range(1, count):
        piece = lax.dynamic_index_in_dim(value, own ^ step, 0, False)
        pieces.append(lax.ppermute(piece, "gx", [(k, k ^ step) for k in range(count)]))
    stacked = jnp.stack(pieces)
    return jnp.stack([lax.dynamic_index_in_dim(stacked, own ^ k, 0, False) for k in range(count)])


def exchange_all(value):
    return lax.all_to_all(value, ("gy", "gx"), split_axis=0, concat_axis=0, tiled=True)


def passed_along(value, axis, steps):
    count = lax.axis_size(axis)
    leading, last = (max(0, -steps), min(count, count - steps))
    return lax.ppermute(value, axis, [(source, source + steps) for source in range(leading, last)])


def forward_x(plan, lines):
    table = plan.slot_matrix()
    cos, sin = plan.slot_twiddle()
    real, imag = radix_forward([lines[:, n] for n in range(plan.radix)])
    blocks = [jnp.concatenate([real[0], real[plan.groups]], -1)]
    for g in range(1, plan.groups):
        re, im = real[g], imag[g - 1]
        blocks.append(jnp.concatenate([re * cos[g] + im * sin[g], im * cos[g] - re * sin[g]], -1))
    first = jnp.einsum("ok,fck->ofc", table[1], blocks[0], precision=highest)
    row = first[plan.deep, 0]
    first = first.at[plan.deep, 0].set(first[0, 1]).at[0, 1].set(row)
    rest = jnp.einsum("ok,gfck->ogfc", table[0], jnp.stack(blocks[1:]), precision=highest)
    spectrum = jnp.concatenate([first[:, None], rest], 1)
    spectrum = spectrum.reshape(plan.m_parts, plan.rows, plan.g_parts, -1)
    return spectrum.transpose(2, 0, 1, 3).reshape(plan.devices, plan.rows, -1)


def spectral_kernels(square):
    kappa = jnp.sqrt(square)
    damping = viscous * kappa
    across = 1.0 / (damping + buoyant + flexural * kappa**4)
    return damping, across


def wave_square(index, length):
    signed = jnp.where(2 * index >= length, index - length, index)
    wave = signed.astype(jnp.float32) * (2.0 * math.pi / length)
    return wave * wave


def middle_y(plan, received, position):
    deep, count, cols = plan.deep, plan.devices, plan.cols
    width = count * deep
    flat = received.reshape(count * plan.rows, -1).T
    mixed = mul(flat, plan.source_matrix())
    mixed = mixed.reshape(plan.own_groups, 2, cols, 2, width)
    cos, sin = plan.line_twiddle()
    re, im = mixed[:, :, :, 0], mixed[:, :, :, 1]
    turned = jnp.concatenate([re * cos + im * sin, im * cos - re * sin], 2)
    spectra = jnp.einsum("wk,gfkl->gfwl", plan.line_matrix(), turned, precision=highest)
    lane = lax.broadcasted_iota(jnp.int32, (1, width), 1)
    q, t = lane % deep, lane // deep
    w = lax.broadcasted_iota(jnp.int32, (cols, 1), 0)
    ky = wave_square(t + count * w, plan.length_y)
    m = (position % plan.m_parts) * deep + q
    base = (position // plan.m_parts) * plan.own_groups
    special = (position == 0) & (q == 0)
    results = []
    for group in range(plan.own_groups):
        g = base + group
        half = lanes // 2
        first = jnp.where(m < half, plan.radix * m, plan.radix // 2 + plan.radix * (m - half))
        index = jnp.where(g == 0, first, g + plan.radix * m)
        damping, across = spectral_kernels(wave_square(index, plan.length_x) + ky)
        u, v = spectra[group, 0], spectra[group, 1]
        ur, ui, vr, vi = u[:cols], u[cols:], v[:cols], v[cols:]
        out_r, out_i = across * (damping * ur - vr), across * (damping * ui - vi)
        if group == 0:
            out_r = jnp.where(special, across * (damping * ur - ui), out_r)
            out_i = jnp.where(special, across * (damping * ui + ur), out_i)
            damping, across = spectral_kernels(np.float32(math.pi) ** 2 + ky)
            extra = jnp.concatenate([across * (damping * vr - vi), across * (damping * vi + vr)], 0)
        results.append(jnp.concatenate([out_r, out_i], 0))
    results.append(extra)
    back = jnp.einsum("kw,gkl->gwl", plan.line_matrix() * np.float32(1.0 / plan.length_y), jnp.stack(results), precision=highest)
    re, im = back[:, :cols], back[:, cols:]
    turned = jnp.concatenate([re * cos - im * sin, im * cos + re * sin], 2)
    lines = jnp.einsum("gcl,sl->gcs", turned, plan.source_matrix(), precision=highest)
    place = lax.broadcasted_iota(jnp.int32, (1, count * plan.rows), 1)
    moved = (position == 0) & (place % plan.rows == deep)
    fixed = jnp.where(moved, jnp.roll(lines[-1], deep, axis=1), lines[0])
    lines = jnp.concatenate([fixed[None], lines[1:-1]], 0)
    return lines.reshape(plan.own_groups * cols, count * plan.rows).T.reshape(count, plan.rows, -1)


def inverse_x(plan, received):
    cols = plan.cols
    table = plan.slot_inverse()
    cos, sin = plan.slot_twiddle()
    split = received.reshape(plan.g_parts, 2 * lanes, plan.own_groups, cols)
    split = split.transpose(0, 2, 3, 1).reshape(plan.groups, cols, 2 * lanes)
    first = mul(split[0], table[1])
    rest = mul(split[1:], table[0])
    real, imag = [], []
    for g in range(1, plan.groups):
        re, im = rest[g - 1, :, :lanes], rest[g - 1, :, lanes:]
        real.append(re * cos[g] - im * sin[g])
        imag.append(im * cos[g] + re * sin[g])
    return radix_inverse(first[:, :lanes], first[:, lanes:], real, imag)


def to_lines(plan, field):
    split = field.reshape(plan.here, lanes, plan.gx, plan.cols)
    return split.transpose(2, 0, 3, 1)


def halves(value):
    high = value.astype(jnp.bfloat16)
    return high, (value - high.astype(jnp.float32)).astype(jnp.bfloat16)


def table_halves(table):
    high = table.astype(jnp.bfloat16)
    return np.concatenate([high, (table - high.astype(np.float32)).astype(jnp.bfloat16)], 0)


def dot(left, right, turned=False):
    dims = (((1,), (1 if turned else 0,)), ((), ()))
    return lax.dot_general(left, right, dims, preferred_element_type=jnp.float32)


def table_times(table, data, turned=False):
    rows = table.shape[0] // 2
    both = dot(table, data[0], turned)
    return both[:rows] + (both[rows:] + dot(table[:rows], data[1], turned))


def times_table(data, table):
    rows, inner = data[0].shape[0], table.shape[0] // 2
    both = dot(jnp.concatenate(data, 0), table[:inner])
    return both[:rows] + (both[rows:] + dot(data[0], table[inner:]))


def call(body, outs, scratch, scalars, *operands):
    scalar = pl.BlockSpec(memory_space=pltpu.SMEM)
    whole = pl.BlockSpec(memory_space=pltpu.VMEM)
    run = pl.pallas_call(
        body,
        out_shape=outs,
        in_specs=[scalar] * len(scalars) + [whole] * len(operands),
        out_specs=[whole] * len(outs),
        scratch_shapes=scratch,
        compiler_params=pltpu.CompilerParams(vmem_limit_bytes=16 << 20),
    )
    return run(*scalars, *operands)


def real_array(*shape):
    return jax.ShapeDtypeStruct(shape, jnp.float32)


def lines_out(plan, own, block, here, turned_ref, out_refs):
    turned_ref[here] = block.T
    for step in range(plan.gx):
        start = pl.multiple_of((own ^ step) * plan.cols, 8)
        out_refs[step][here * plan.cols : (here + 1) * plan.cols, :] = turned_ref[here, pl.ds(start, plan.cols), :]


def own_part(plan, part, row):
    wide = jnp.concatenate([row, row[:, :lanes]], 1)
    wide = jnp.broadcast_to(wide, (8, wide.shape[1]))
    out = wide[:, :lanes]
    for k in range(1, plan.gx):
        start = k * plan.cols
        low = start // lanes * lanes
        block = wide[:, low : low + 2 * lanes]
        if start % lanes:
            block = pltpu.roll(block, 2 * lanes - start % lanes, 1)
        out = jnp.where(part == k, block[:, :lanes], out)
    return out[:1]


def kernel_call(body, outs, scratch, scalars, inputs, faces=()):
    whole = pl.BlockSpec(memory_space=pltpu.VMEM)
    run = pl.pallas_call(
        body,
        out_shape=outs,
        in_specs=[pl.BlockSpec(memory_space=pltpu.SMEM)] * len(scalars) + [pl.BlockSpec(memory_space=pl.ANY)] * len(inputs) + [whole] * len(faces),
        out_specs=[whole] * len(outs),
        scratch_shapes=scratch,
    )
    return run(*scalars, *inputs, *faces)


def uplift_kernel(plan, own_ref, _, uplift_hbm, flux_x_hbm, flux_y_hbm, *refs):
    own = own_ref[0]
    out_refs = refs[: plan.gx]
    field_ref, turned_ref, tail_ref, last_x_ref, last_y_ref, sems, out_sems = refs[plan.gx :]
    rows, cols = uplift_hbm.shape
    copies = [
        pltpu.make_async_copy(flux_x_hbm.at[pl.ds(rows - 8, 8), :], last_x_ref, sems.at[0]),
        pltpu.make_async_copy(flux_y_hbm.at[:, pl.ds(cols - lanes, lanes)], last_y_ref, sems.at[1]),
    ]
    half = lanes // 2
    for part in range(2 * plan.here):
        source = uplift_hbm.at[pl.ds(part * half, half), :]
        copies.append(pltpu.make_async_copy(source, field_ref.at[pl.ds(part * half, half), :], sems.at[2 + part]))
    for copy in copies[2:] + copies[:2]:
        copy.start()
    sent = []
    for here in range(plan.here):
        copies[2 + 2 * here].wait()
        copies[3 + 2 * here].wait()
        turned_ref[here] = field_ref[here * lanes : (here + 1) * lanes, :].T
        for step in range(plan.gx):
            source = turned_ref.at[here, pl.ds(pl.multiple_of((own ^ step) * plan.cols, 8), plan.cols), :]
            target = out_refs[step].at[pl.ds(here * plan.cols, plan.cols), :]
            sent.append(pltpu.make_async_copy(source, target, out_sems.at[here, step]))
            sent[-1].start()
    copies[0].wait()
    copies[1].wait()
    last_x = last_x_ref[7:8, :]
    last_y = last_y_ref[...].T[lanes - 1 : lanes, :]
    parts = [last[:, a * lanes : (a + 1) * lanes] for last in (last_x, last_y) for a in range(plan.here)]
    parts.append(jnp.zeros((plan.tail - 2 * plan.here, lanes), jnp.float32))
    tail_ref[...] = jnp.concatenate(parts, 0)
    for step in range(plan.gx):
        target = out_refs[step].at[pl.ds(plan.here * plan.cols, plan.tail), :]
        sent.append(pltpu.make_async_copy(tail_ref, target, out_sems.at[plan.here, step]))
        sent[-1].start()
    for copy in sent:
        copy.wait()


def send_uplift(plan, own, across_y, bed_uplift, flux_x, flux_y):
    rows, cols = bed_uplift.shape
    run = pl.pallas_call(
        lambda *refs: uplift_kernel(plan, *refs),
        out_shape=[real_array(plan.piece_rows, lanes)] * plan.gx,
        in_specs=[pl.BlockSpec(memory_space=pltpu.SMEM)] * 2 + [pl.BlockSpec(memory_space=pl.ANY)] * 3,
        out_specs=[pl.BlockSpec(memory_space=pl.ANY)] * plan.gx,
        scratch_shapes=[
            pltpu.VMEM((rows, cols), jnp.float32),
            pltpu.VMEM((plan.here, cols, lanes), jnp.float32),
            pltpu.VMEM((plan.tail, lanes), jnp.float32),
            pltpu.VMEM((8, cols), jnp.float32),
            pltpu.VMEM((rows, lanes), jnp.float32),
            pltpu.SemaphoreType.DMA((2 + 2 * plan.here,)),
            pltpu.SemaphoreType.DMA((plan.here + 1, plan.gx)),
        ],
    )
    return run(own, across_y, bed_uplift, flux_x, flux_y)


def fetch_fields(plan, sources, mask_ref, floats_ref, sems):
    targets = [floats_ref.at[k] for k in range(4)] + [mask_ref]
    copies = []
    for here in range(plan.here):
        rows = pl.ds(here * lanes, lanes)
        group = [
            pltpu.make_async_copy(source.at[rows, :], target.at[rows, :], sems.at[here, k])
            for k, (source, target) in enumerate(zip(sources, targets))
        ]
        for copy in group:
            copy.start()
        copies.append(group)
    return copies


def trial_block(floats_ref, here, above, left_edge):
    rows = slice(here * lanes, (here + 1) * lanes)
    fx, fy = floats_ref[1, rows, :], floats_ref[2, rows, :]
    row = lax.broadcasted_iota(jnp.int32, fx.shape, 0)
    col = lax.broadcasted_iota(jnp.int32, fx.shape, 1)
    if here:
        above = floats_ref[1, here * lanes - 1 : here * lanes, :]
    below = jnp.where(row == 0, jnp.broadcast_to(above, fx.shape) if here or above.ndim else above, pltpu.roll(fx, 1, 0))
    left = jnp.where(col == 0, left_edge, pltpu.roll(fy, 1, 1))
    divergence = fx - below + fy - left
    return floats_ref[0, rows, :] + time_step * (floats_ref[3, rows, :] - divergence)


hidden = np.float32(-1e30)


def load_kernel(plan, own_ref, *refs):
    own = own_ref[0]
    sources, refs = refs[:5], refs[5:]
    line_refs, (mask_ref, floats_ref, turned_ref, sems) = refs[: plan.gx], refs[plan.gx :]
    copies = fetch_fields(plan, sources, mask_ref, floats_ref, sems)
    columns_trial, columns_thick = [], []
    for here in range(plan.here):
        for copy in copies[here]:
            copy.wait()
        rows = slice(here * lanes, (here + 1) * lanes)
        trial = trial_block(floats_ref, here, jnp.float32(0.0), 0.0)
        free = mask_ref[rows, :] == 0
        thick = jnp.where(free, floats_ref[0, rows, :], 0.0)
        trial = jnp.where(free, trial, hidden)
        lines_out(plan, own, jnp.maximum(trial, 0.0) - thick, here, turned_ref, line_refs)
        lane = lax.broadcasted_iota(jnp.int32, (lanes, lanes), 1)
        packed = jnp.where(lane == 0, trial[:, :lanes], pltpu.roll(thick[:, :lanes], 1, 1)).T
        columns_trial.append(packed[0:1])
        columns_thick.append(packed[1:2])
        if here == 0:
            row_trial, row_thick = trial[0:1], thick[0:1]
    tail = plan.here * plan.cols
    rest = plan.tail - 2 - 2 * plan.here
    for step in range(plan.gx):
        parts = [own_part(plan, own ^ step, row_trial), own_part(plan, own ^ step, row_thick)] + columns_trial + columns_thick
        if rest:
            parts.append(jnp.zeros((rest, lanes), jnp.float32))
        line_refs[step][tail : tail + plan.tail, :] = jnp.concatenate(parts, 0)


def field_scratch(shape):
    return [
        pltpu.VMEM(shape, jnp.int32),
        pltpu.VMEM((4,) + shape, jnp.float32),
    ]


def make_load(plan, own, fields):
    shape = fields[0].shape
    scratch = field_scratch(shape) + [
        pltpu.VMEM((plan.here, shape[1], lanes), jnp.float32),
        pltpu.SemaphoreType.DMA((plan.here, 5)),
    ]
    outs = [real_array(plan.piece_rows, lanes)] * plan.gx
    return kernel_call(lambda *refs: load_kernel(plan, *refs), outs, scratch, [own], fields)


def row_above(plan, own, block, tails):
    above = [jnp.zeros((1, lanes), jnp.float32)] * plan.here
    for step in range(plan.gx):
        match = (own ^ step) + 1 == block
        above = [jnp.where(match, tails[step][a : a + 1, :], above[a]) for a in range(plan.here)]
    return jnp.concatenate(above, 1)


def thickness_kernel(plan, own_ref, *refs):
    own = own_ref[0]
    sources, (tails_ref, side_ref, out_ref, mask_ref, floats_ref, sems) = refs[:5], refs[5:]
    copies = fetch_fields(plan, sources, mask_ref, floats_ref, sems)
    above = row_above(plan, own, own, [tails_ref[step] for step in range(plan.gx)])
    for here in range(plan.here):
        for copy in copies[here]:
            copy.wait()
        rows = slice(here * lanes, (here + 1) * lanes)
        side = jnp.broadcast_to(side_ref[0, plan.here + here : plan.here + here + 1, :], (lanes, lanes)).T
        side = jnp.concatenate([side] * (out_ref.shape[1] // lanes), 1)
        trial = trial_block(floats_ref, here, above, side)
        out_ref[rows, :] = jnp.where(mask_ref[rows, :] == 2, 0.0, jnp.maximum(trial, 0.0))


def make_thickness(plan, own, fields, faces):
    shape = fields[0].shape
    scratch = field_scratch(shape) + [pltpu.SemaphoreType.DMA((plan.here, 5))]
    return kernel_call(lambda *refs: thickness_kernel(plan, *refs), [real_array(*shape)], scratch, [own], fields, faces)[0]


def finish_load(plan, own, line_ref, uplift_tails, load_tails, side_ref):
    cols, here = plan.cols, plan.here
    lane = lax.broadcasted_iota(jnp.int32, (1, lanes), 1)
    wide_lane = lax.broadcasted_iota(jnp.int32, (cols, lanes), 1)
    above, new = [], []
    for step in range(plan.gx):
        above.append(own_part(plan, own, row_above(plan, own, own ^ step, uplift_tails)))
        tail = load_tails[step]
        new.append(jnp.maximum(tail[0:1, :] + time_step * above[step], 0.0) - tail[1:2, :])
    turned = jnp.concatenate(new + [jnp.zeros((lanes - plan.gx, lanes), jnp.float32)], 0).T[:cols]
    for step in range(plan.gx):
        place = (own ^ step) * here
        first = pltpu.roll(turned, lanes - step, 1) if step else turned
        line_ref[place] = jnp.where(wide_lane == 0, first, line_ref[place])

    @pl.when(own == 0)
    def _():
        for step in range(plan.gx):
            tail = load_tails[step]
            for a in range(here):
                corner = jnp.where(lane == 0, jnp.broadcast_to(above[step][:, :1], (1, lanes)), 0.0) if a == 0 else 0.0
                trial = tail[2 + a : 3 + a, :] + time_step * (side_ref[step, here + a : here + a + 1, :] + corner)
                line_ref[step * here + a, 0:1, :] = jnp.maximum(trial, 0.0) - tail[2 + here + a : 3 + here + a, :]


def tails_kernel(plan, *refs):
    pieces, tails_ref = refs[: plan.gx], refs[plan.gx]
    start = plan.here * plan.cols
    for step in range(plan.gx):
        tails_ref[step] = pieces[step][start : start + plan.tail, :]


def forward_kernel(plan, lead, own_ref, *refs):
    pieces, refs = refs[: plan.gx], refs[plan.gx :]
    cols, radix, groups, here = plan.cols, plan.radix, plan.groups, plan.here
    own = own_ref[0]
    tail = slice(here * cols, here * cols + plan.tail)
    if lead:
        uplift_tails, side_ref, edge_ref, head_ref, _, twiddle_ref, table_ref, *refs = refs
        out_ref, line_ref, high_ref, low_ref = refs
    else:
        twiddle_ref, table_ref, out_ref, edge_ref, head_ref, line_ref, high_ref, low_ref = refs
    step_rows = 16
    total = groups * cols
    for step in range(plan.gx):
        for a in range(here):
            line_ref[(own ^ step) * here + a] = pieces[step][a * cols : (a + 1) * cols, :]
    if lead:
        tails = [uplift_tails[step] for step in range(plan.gx)]
        finish_load(plan, own, line_ref, tails, [piece[tail, :] for piece in pieces], side_ref)
    skip = lead % lanes

    def chunk(index, carry):
        row = pl.multiple_of(index * step_rows, step_rows)
        real, imag = radix_forward([line_ref[n, pl.ds(row, step_rows), :] for n in range(radix)])
        for g in range(groups):
            if g == 0:
                first, second = real[0], real[groups]
            else:
                cos, sin = twiddle_ref[0, g : g + 1, :], twiddle_ref[1, g : g + 1, :]
                first = real[g] * cos + imag[g - 1] * sin
                second = imag[g - 1] * cos - real[g] * sin
            high, low = halves(jnp.concatenate([first, second], 1))
            target = pl.ds(skip + g * cols + row, step_rows)
            high_ref[target, :] = high
            low_ref[target, :] = low
        return carry

    lax.fori_loop(0, cols // step_rows, chunk, 0)
    for edge in ((0, skip), (skip + total, high_ref.shape[0])):
        if edge[0] < edge[1]:
            high_ref[edge[0] : edge[1], :] = jnp.zeros((edge[1] - edge[0], 2 * lanes), jnp.bfloat16)
            low_ref[edge[0] : edge[1], :] = jnp.zeros((edge[1] - edge[0], 2 * lanes), jnp.bfloat16)
    before = (lead - skip) // lanes
    blocks = high_ref.shape[0] // lanes

    def place(block):
        return slice((before + block) * lanes, (before + block + 1) * lanes)

    held = -(-(skip + cols) // lanes) if lead else 0
    end = skip + cols
    special = -(-end // lanes) * lanes
    first = table_times(table_ref[1], (high_ref[:special, :], low_ref[:special, :]), True)
    for block in range(blocks):
        start = block * lanes
        if block % 2 == 0:
            rows = slice(start, min(start + 2 * lanes, blocks * lanes))
            pair = table_times(table_ref[0], (high_ref[rows, :], low_ref[rows, :]), True)
        out = pair[:, (block % 2) * lanes : (block % 2 + 1) * lanes]
        if start < end:
            lane = lax.broadcasted_iota(jnp.int32, (2 * lanes, lanes), 1)
            out = jnp.where(lane < end - start, first[:, start : start + lanes], out)
        out = out.reshape(plan.devices, plan.rows, lanes)
        if start < skip:
            lane = lax.broadcasted_iota(jnp.int32, out.shape, 2)
            out = jnp.where(lane < skip - start, edge_ref[...], out)
        if not lead and (block + 1) * lanes > total:
            edge_ref[...] = out
            continue
        out_ref[:, :, place(block)] = out
        if not lead and block == 0:
            head_ref[...] = out[0]
        if block + 1 == held:
            two = jnp.concatenate([out_ref[0, :, place(k)] for k in range(held)], 1)
            width = held * lanes
            row = lax.broadcasted_iota(jnp.int32, two.shape, 0)
            lane = lax.broadcasted_iota(jnp.int32, two.shape, 1)
            head = head_ref[...]
            wide = pltpu.roll(jnp.concatenate([head] * held, 1), plan.deep, 0)
            to_right = pltpu.roll(wide, skip, 1) if skip else wide
            swapped = pltpu.roll(two, plan.deep, 0)
            to_left = pltpu.roll(swapped, width - skip, 1) if skip else swapped
            take = (row[:, :lanes] == plan.deep) & (lane[:, :lanes] < cols)
            out_ref[0, :, :lanes] = jnp.where(take, to_left[:, :lanes], head)
            take = (row == 0) & (lane >= skip) & (lane < skip + cols)
            fixed = jnp.where(take, to_right, two)
            for k in range(held):
                out_ref[0, :, place(k)] = fixed[:, k * lanes : (k + 1) * lanes]


def make_forward(plan, own, pieces, tables, before=None):
    half = plan.groups * plan.cols
    lead = half if before else 0
    skip = lead % lanes
    blocks = -(-(skip + half) // lanes)
    whole = pl.BlockSpec(memory_space=pltpu.VMEM)
    outs, operands, alias = [real_array(plan.devices, plan.rows, 2 * half)], list(pieces), {}
    if before:
        tails, side, spectrum, edge, head = before
        operands += [tails, side, edge, head, spectrum]
        alias = {len(operands): 0}
    else:
        outs += [real_array(plan.devices, plan.rows, lanes), real_array(plan.rows, lanes)]
    operands += tables
    run = pl.pallas_call(
        lambda *refs: forward_kernel(plan, lead, *refs),
        out_shape=outs,
        in_specs=[pl.BlockSpec(memory_space=pltpu.SMEM)] + [whole] * len(operands),
        out_specs=[whole] * len(outs),
        scratch_shapes=[
            pltpu.VMEM((plan.radix, plan.cols, lanes), jnp.float32),
            pltpu.VMEM((blocks * lanes, 2 * lanes), jnp.bfloat16),
            pltpu.VMEM((blocks * lanes, 2 * lanes), jnp.bfloat16),
        ],
        input_output_aliases=alias,
        compiler_params=pltpu.CompilerParams(vmem_limit_bytes=16 << 20),
    )
    return run(own, *operands)


def middle_kernel(plan, own_ref, across_ref, in_ref, t1_ref, t2_ref, t2i_ref, t1i_ref, twiddle_ref, out_ref, high_ref, low_ref, back_high, back_low, turn_ref, mixed_ref):
    position = across_ref[0] * plan.gx + own_ref[0]
    cols, groups, deep, count = plan.cols, plan.groups, plan.deep, plan.devices
    width, size = lanes, 2 * lanes
    for start in range(0, 2 * groups * cols, lanes):
        block = in_ref[:, :, start : start + lanes].reshape(size, lanes).T
        high_ref[start : start + lanes, :], low_ref[start : start + lanes, :] = halves(block)
    step = 2 * groups * cols // 4
    for start in range(0, 2 * groups * cols, step):
        rows = slice(start, start + step)
        mixed_ref[rows, :] = times_table((high_ref[rows, :], low_ref[rows, :]), t1_ref[...])
    cos, sin = twiddle_ref[0], twiddle_ref[1]
    lane = lax.broadcasted_iota(jnp.int32, (1, width), 1)
    q, t = lane % deep, lane // deep
    w = lax.broadcasted_iota(jnp.int32, (cols, width), 0)
    ky = wave_square(t + count * w, plan.length_y)
    m = position * deep + q
    special = jnp.broadcast_to((position == 0) & (q == 0), (cols, width))
    results = []
    for g in range(groups):
        sides = []
        for field in range(2):
            part = mixed_ref[(field * groups + g) * cols : (field * groups + g + 1) * cols, :]
            re, im = part[:, :width], part[:, width:]
            sides.append(jnp.concatenate([re * cos + im * sin, im * cos - re * sin], 0))
        spectra = table_times(t2_ref[...], halves(jnp.concatenate(sides, 1)))
        ur, vr = spectra[:cols, :width], spectra[:cols, width:]
        ui, vi = spectra[cols:, :width], spectra[cols:, width:]
        half = lanes // 2
        if g == 0:
            index = jnp.where(m < half, plan.radix * m, plan.radix // 2 + plan.radix * (m - half))
        else:
            index = g + plan.radix * m
        damping, across = spectral_kernels(wave_square(index, plan.length_x) + ky)
        out_r, out_i = across * (damping * ur - vr), across * (damping * ui - vi)
        if g == 0:
            out_r = jnp.where(special, across * (damping * ur - ui), out_r)
            out_i = jnp.where(special, across * (damping * ui + ur), out_i)
            damping, across = spectral_kernels(np.float32(math.pi) ** 2 + ky)
            extra = jnp.concatenate([across * (damping * vr - vi), across * (damping * vi + vr)], 0)
        results.append(jnp.concatenate([out_r, out_i], 0))
    results.append(extra)
    for g in range(0, groups + 1, 2):
        pair = results[g : g + 2]
        back = table_times(t2i_ref[...], halves(jnp.concatenate(pair, 1)))
        for k in range(len(pair)):
            re, im = back[:cols, k * width : (k + 1) * width], back[cols:, k * width : (k + 1) * width]
            turned = jnp.concatenate([re * cos - im * sin, im * cos + re * sin], 1)
            place = slice((g + k) * cols, (g + k + 1) * cols)
            back_high[place, :], back_low[place, :] = halves(turned)
    total = (groups + 1) * cols
    cuts = [total * k // 2 // 16 * 16 for k in range(2)] + [total]
    for start, stop in zip(cuts, cuts[1:]):
        rows = slice(start, stop)
        turn_ref[rows, :] = times_table((back_high[rows, :], back_low[rows, :]), t1i_ref[...])
    place = lax.broadcasted_iota(jnp.int32, (cols, size), 1)
    moved = (position == 0) & (place % plan.rows == deep)
    extra = turn_ref[groups * cols : (groups + 1) * cols, :]
    turn_ref[:cols, :] = jnp.where(moved, pltpu.roll(extra, deep, 1), turn_ref[:cols, :])
    for start in range(0, groups * cols, lanes):
        block = turn_ref[start : start + lanes, :].T.reshape(count, plan.rows, lanes)
        keep = min(lanes, groups * cols - start)
        real, imag = block[:, :deep], block[:, deep:]
        if keep < lanes:
            place = lax.broadcasted_iota(jnp.int32, real.shape, 2)
            out_ref[:, :, 2 * start : 2 * start + 2 * keep] = jnp.where(place < keep, real, pltpu.roll(imag, keep, 2))[:, :, : 2 * keep]
        else:
            out_ref[:, :, 2 * start : 2 * start + lanes] = real
            out_ref[:, :, 2 * start + lanes : 2 * start + 2 * lanes] = imag


def inverse_kernel(plan, own_ref, in_ref, twiddle_ref, table_ref, *refs):
    out_refs, (line_ref, turn_ref, mid_ref) = refs[: plan.gx], refs[plan.gx :]
    own = own_ref[0]
    cols, groups, here = plan.cols, plan.groups, plan.here
    size = 2 * lanes
    total = groups * cols
    for start in range(0, total, lanes):
        keep = min(lanes, total - start)
        real = in_ref[:, :, 2 * start : 2 * start + lanes]
        imag = pltpu.roll(real, keep, 2) if keep < lanes else in_ref[:, :, 2 * start + lanes : 2 * start + 2 * lanes]
        block = jnp.concatenate([real, imag], 1).reshape(size, lanes)
        turn_ref[start : start + keep, :] = block.T[:keep]
    mid_ref[:cols, :] = times_table(halves(turn_ref[:cols, :]), table_ref[1])
    mid_ref[cols:, :] = times_table(halves(turn_ref[cols:, :]), table_ref[0])
    step_rows = 16

    def chunk(index, carry):
        row = pl.multiple_of(index * step_rows, step_rows)
        real, imag = [], []
        for g in range(1, groups):
            place = pl.ds(g * cols + row, step_rows)
            re, im = mid_ref[place, :lanes], mid_ref[place, lanes:]
            cos, sin = twiddle_ref[0, g : g + 1, :], twiddle_ref[1, g : g + 1, :]
            real.append(re * cos - im * sin)
            imag.append(im * cos + re * sin)
        place = pl.ds(row, step_rows)
        values = radix_inverse(mid_ref[place, :lanes], mid_ref[place, lanes:], real, imag)
        for n, value in enumerate(values):
            line_ref[n, place, :] = value
        return carry

    lax.fori_loop(0, cols // step_rows, chunk, 0)
    for step in range(plan.gx):
        for a in range(here):
            out_refs[step][a] = line_ref[(own ^ step) * here + a]


def final_kernel(plan, own_ref, *refs):
    pieces, (out_hbm, line_ref, block_ref, sems) = refs[: plan.gx], refs[plan.gx :]
    own = own_ref[0]
    sent = []
    for a in range(plan.here):
        for step in range(plan.gx):
            start = pl.multiple_of((own ^ step) * plan.cols, 8)
            line_ref[a, pl.ds(start, plan.cols), :] = pieces[step][a]
        block_ref[a] = line_ref[a].T
        sent.append(pltpu.make_async_copy(block_ref.at[a], out_hbm.at[pl.ds(a * lanes, lanes), :], sems.at[a]))
        sent[-1].start()
    for copy in sent:
        copy.wait()


def make_final(plan, own, pieces, shape):
    whole = pl.BlockSpec(memory_space=pltpu.VMEM)
    run = pl.pallas_call(
        lambda *refs: final_kernel(plan, *refs),
        out_shape=real_array(*shape),
        in_specs=[pl.BlockSpec(memory_space=pltpu.SMEM)] + [whole] * plan.gx,
        out_specs=pl.BlockSpec(memory_space=pl.ANY),
        scratch_shapes=[
            pltpu.VMEM((plan.here, shape[1], lanes), jnp.float32),
            pltpu.VMEM((plan.here, lanes, shape[1]), jnp.float32),
            pltpu.SemaphoreType.DMA((plan.here,)),
        ],
        compiler_params=pltpu.CompilerParams(vmem_limit_bytes=16 << 20),
    )
    return run(own, *pieces)


def swap_gx(plan, pieces):
    got = [pieces[0]]
    for step in range(1, plan.gx):
        got.append(lax.ppermute(pieces[step], "gx", [(k, k ^ step) for k in range(plan.gx)]))
    return got


def build_kernels(plan):
    vmem, f32, bf16 = pltpu.VMEM, jnp.float32, jnp.bfloat16
    size, cols, groups = 2 * lanes, plan.cols, plan.groups
    half = groups * cols
    pieces = [real_array(plan.here, cols, lanes)] * plan.gx
    line = vmem((plan.radix, cols, lanes), f32)

    def local(thickness, bed_uplift, flux_x, flux_y, mass_balance, ice_mask):
        own, across_y = lax.axis_index("gx").reshape(1), lax.axis_index("gy").reshape(1)
        fields = (thickness, flux_x, flux_y, mass_balance, ice_mask)
        uplift = send_uplift(plan, own, across_y, bed_uplift, flux_x, flux_y)
        lines_u = swap_gx(plan, uplift)
        load = make_load(plan, own, fields)
        lines_v = swap_gx(plan, load)
        twiddle = plan.slot_twiddle()
        tables = np.stack([table_halves(table) for table in plan.slot_matrix()])
        (tails_u,) = call(lambda *refs: tails_kernel(plan, *refs), [real_array(plan.gx, plan.tail, lanes)], [], [], *lines_u)
        side = passed_along(tails_u, "gy", 1)
        partial = make_forward(plan, own, lines_u, (twiddle, tables))
        (spectrum,) = make_forward(plan, own, lines_v, (twiddle, tables), (tails_u, side, *partial))
        thickness_new = make_thickness(plan, own, fields, (tails_u, side))
        received = exchange_all(spectrum)
        source, across = plan.source_matrix(), plan.line_matrix()
        scale = np.float32(1.0 / plan.length_y)
        tables = [table_halves(table) for table in (source, across, across.T * scale, source.T)]
        (middle,) = call(
            lambda *refs: middle_kernel(plan, *refs),
            [real_array(plan.devices, plan.deep, 2 * half)],
            [vmem((2 * half, size), bf16)] * 2 + [vmem((half + cols, size), bf16)] * 2 + [vmem((half + cols, size), f32), vmem((2 * half, size), f32)],
            [own, across_y],
            *([received] + tables + [plan.line_twiddle()]),
        )
        back = exchange_all(middle)
        inverse = np.stack([table_halves(table) for table in plan.slot_inverse()])
        bed = call(
            lambda *refs: inverse_kernel(plan, *refs),
            pieces,
            [line] + [vmem((half, size), f32)] * 2,
            [own],
            *(back, twiddle, inverse),
        )
        lines_b = swap_gx(plan, bed)
        bed_new = make_final(plan, own, lines_b, thickness.shape)
        return thickness_new, bed_new

    return local


def build(plan):
    if plan.devices * plan.rows == 2 * lanes and plan.cols % 16 == 0 and plan.radix <= 16 and plan.gx in (2, 4, 8) and plan.groups * plan.cols % lanes in (0, lanes // 2):
        return build_kernels(plan)

    def local(thickness, bed_uplift, flux_x, flux_y, mass_balance, ice_mask):
        lower_face = passed_along(flux_x[-1:, :], "gx", 1)
        left_face = passed_along(flux_y[:, -1:], "gy", 1)
        flux_below = jnp.concatenate([lower_face, flux_x[:-1, :]], axis=0)
        flux_left = jnp.concatenate([left_face, flux_y[:, :-1]], axis=1)
        divergence = flux_x - flux_below + flux_y - flux_left
        trial = thickness + time_step * (mass_balance - divergence)
        thickness_new = jnp.where(ice_mask == 2, 0.0, jnp.maximum(trial, 0.0))
        load = jnp.where(ice_mask == 0, thickness_new - thickness, 0.0)
        fields = jnp.stack([to_lines(plan, bed_uplift), to_lines(plan, load)], 1)
        lines = exchange_gx(fields)
        lines = lines.transpose(1, 0, 2, 3, 4).reshape(2, plan.radix, plan.cols, lanes)
        received = exchange_all(forward_x(plan, lines))
        position = lax.axis_index("gy") * plan.gx + lax.axis_index("gx")
        back = exchange_all(middle_y(plan, received, position))
        bed = inverse_x(plan, back)
        bed = jnp.stack(bed).reshape(plan.gx, plan.here, plan.cols, lanes)
        bed = exchange_gx(bed)
        bed_new = bed.transpose(1, 3, 0, 2).reshape(plan.here * lanes, plan.gx * plan.cols)
        return thickness_new, bed_new

    return local


def solution(mesh):
    spec = P("gx", "gy")

    def step(*args):
        length_x, length_y = args[0].shape
        plan = Plan(mesh, length_x, length_y)
        body = jax.shard_map(build(plan), mesh=mesh, in_specs=(spec,) * 6, out_specs=(spec, spec), check_vma=False)
        return body(*args)

    return step
```

```python
import math

import jax
import jax.numpy as jnp
import numpy as np
from jax import lax
from jax.experimental import pallas as pl
from jax.experimental.pallas import tpu as pltpu
from jax.sharding import PartitionSpec as P

time_step = 0.5
viscous = 4.0
buoyant = 0.01
flexural = 50.0
lanes = 128
highest = lax.Precision.HIGHEST


class Plan:
    def __init__(self, mesh, length_x, length_y):
        self.gx, self.gy = mesh.shape["gx"], mesh.shape["gy"]
        self.devices = self.gx * self.gy
        self.length_x, self.length_y = length_x, length_y
        self.radix = length_x // lanes
        self.here = self.radix // self.gx
        self.groups = self.radix // 2
        self.cols = length_y // self.devices
        self.m_parts = min(self.devices, lanes)
        self.g_parts = self.devices // self.m_parts
        self.deep = lanes // self.m_parts
        self.own_groups = self.groups // self.g_parts
        self.rows = 2 * self.deep
        self.tail = -(-(2 + 2 * self.here) // 8) * 8
        self.piece_rows = self.here * self.cols + self.tail

    def slot_matrix(self):
        n2 = np.arange(lanes)[None, :]
        m = np.arange(lanes)[:, None]
        theta = 2 * np.pi * (m * n2 % lanes) / lanes
        cos, sin = np.cos(theta), np.sin(theta)
        general = np.stack([np.concatenate([cos, sin], 1), np.concatenate([-sin, cos], 1)])
        half = lanes // 2
        turned = 2 * np.pi * ((2 * (m - half) + 1) * n2 % (2 * lanes)) / (2 * lanes)
        low = np.arange(lanes)[:, None] < half
        real = np.concatenate([np.where(low, cos, 0), np.where(low, 0, np.cos(turned))], 1)
        imag = np.concatenate([np.where(low, -sin, 0), np.where(low, 0, -np.sin(turned))], 1)
        imag[0, :lanes] = np.where(np.arange(lanes) % 2 == 0, 1.0, -1.0)
        first = np.stack([real, imag])
        return np.stack([self._by_part(general), self._by_part(first)]).astype(np.float32)

    def _by_part(self, table):
        split = table.reshape(2, self.m_parts, self.deep, 2 * lanes)
        return split.transpose(1, 0, 2, 3).reshape(2 * lanes, 2 * lanes)

    def slot_inverse(self):
        m = np.arange(lanes)[:, None]
        n2 = np.arange(lanes)[None, :]
        theta = 2 * np.pi * (m * n2 % lanes) / lanes
        cos, sin = np.cos(theta), np.sin(theta)
        general = 2 * np.stack([np.concatenate([cos, sin], 1), np.concatenate([-sin, cos], 1)])
        half = lanes // 2
        turned = 2 * np.pi * ((2 * (m - half) + 1) * n2 % (2 * lanes)) / (2 * lanes)
        low = m < half
        real = 2 * np.concatenate([np.where(low, cos, 0), np.where(low, 0, np.cos(turned))], 1)
        imag = 2 * np.concatenate([np.where(low, -sin, 0), np.where(low, 0, -np.sin(turned))], 1)
        real[0, :lanes] = 1.0
        imag[0, :lanes] = np.where(np.arange(lanes) % 2 == 0, 1.0, -1.0)
        first = np.stack([real, imag])
        return (np.stack([self._by_part(general), self._by_part(first)]) / self.length_x).astype(np.float32)

    def slot_twiddle(self):
        angle = 2 * np.pi * np.arange(self.groups)[:, None] * np.arange(lanes)[None, :] / self.length_x
        return np.stack([np.cos(angle), np.sin(angle)]).astype(np.float32)

    def source_matrix(self):
        count, deep = self.devices, self.deep
        index = np.arange(count)
        theta = 2 * np.pi * (index[:, None] * index[None, :] % count) / count
        cos, sin = np.cos(theta), np.sin(theta)
        out = np.zeros((count, 2, deep, 2, count, deep))
        for q in range(deep):
            out[:, 0, q, 0, :, q] = cos
            out[:, 1, q, 0, :, q] = sin
            out[:, 0, q, 1, :, q] = -sin
            out[:, 1, q, 1, :, q] = cos
        return out.reshape(count * 2 * deep, 2 * count * deep).astype(np.float32)

    def line_matrix(self):
        index = np.arange(self.cols)
        theta = 2 * np.pi * (index[:, None] * index[None, :] % self.cols) / self.cols
        cos, sin = np.cos(theta), np.sin(theta)
        return np.block([[cos, sin], [-sin, cos]]).astype(np.float32)

    def line_twiddle(self):
        angle = 2 * np.pi * np.arange(self.cols)[:, None] * np.arange(self.devices)[None, :] / self.length_y
        angle = np.repeat(angle, self.deep, axis=1)
        return np.stack([np.cos(angle), np.sin(angle)]).astype(np.float32)


def weighted(terms):
    groups = {}
    for coefficient, value in terms:
        size = round(abs(coefficient), 12)
        if size == 0.0:
            continue
        groups.setdefault(size, []).append((coefficient > 0, value))
    total = None
    for size, members in groups.items():
        members.sort(key=lambda member: not member[0])
        positive, part = members[0]
        for sign, value in members[1:]:
            part = part + value if sign == positive else part - value
        if size != 1.0:
            part = part * np.float32(size)
        if total is None:
            total = part if positive else -part
        else:
            total = total + part if positive else total - part
    return total


def radix_forward(values):
    count = len(values)
    half = count // 2
    even = [values[j] + values[count - j] for j in range(1, half)]
    odd = [values[j] - values[count - j] for j in range(1, half)]
    real, imag = [], []
    for g in range(half + 1):
        terms = [(1.0, values[0]), ((-1.0) ** g, values[half])]
        terms += [(math.cos(2 * math.pi * g * (j + 1) / count), even[j]) for j in range(half - 1)]
        real.append(weighted(terms))
        if 0 < g < half:
            imag.append(weighted([(-math.sin(2 * math.pi * g * (j + 1) / count), odd[j]) for j in range(half - 1)]))
    return real, imag


def radix_inverse(first, middle, real, imag):
    half = len(real) + 1
    count = 2 * half
    out = [None] * count
    for j in range(half + 1):
        terms = [(1.0, first), ((-1.0) ** j, middle)]
        terms += [(math.cos(2 * math.pi * g * j / count), real[g - 1]) for g in range(1, half)]
        together = weighted(terms)
        if j in (0, half):
            out[j] = together
            continue
        apart = weighted([(math.sin(2 * math.pi * g * j / count), imag[g - 1]) for g in range(1, half)])
        out[j] = together - apart
        out[count - j] = together + apart
    return out


def mul(a, b):
    return jnp.matmul(a, b, precision=highest)


def exchange_gx(value):
    count = lax.axis_size("gx")
    own = lax.axis_index("gx")
    if count > 8:
        return lax.all_to_all(value, "gx", split_axis=0, concat_axis=0, tiled=True)
    pieces = [lax.dynamic_index_in_dim(value, own, 0, False)]
    for step in range(1, count):
        piece = lax.dynamic_index_in_dim(value, own ^ step, 0, False)
        pieces.append(lax.ppermute(piece, "gx", [(k, k ^ step) for k in range(count)]))
    stacked = jnp.stack(pieces)
    return jnp.stack([lax.dynamic_index_in_dim(stacked, own ^ k, 0, False) for k in range(count)])


def exchange_all(value):
    return lax.all_to_all(value, ("gy", "gx"), split_axis=0, concat_axis=0, tiled=True)


def passed_along(value, axis, steps):
    count = lax.axis_size(axis)
    leading, last = (max(0, -steps), min(count, count - steps))
    return lax.ppermute(value, axis, [(source, source + steps) for source in range(leading, last)])


def forward_x(plan, lines):
    table = plan.slot_matrix()
    cos, sin = plan.slot_twiddle()
    real, imag = radix_forward([lines[:, n] for n in range(plan.radix)])
    blocks = [jnp.concatenate([real[0], real[plan.groups]], -1)]
    for g in range(1, plan.groups):
        re, im = real[g], imag[g - 1]
        blocks.append(jnp.concatenate([re * cos[g] + im * sin[g], im * cos[g] - re * sin[g]], -1))
    first = jnp.einsum("ok,fck->ofc", table[1], blocks[0], precision=highest)
    row = first[plan.deep, 0]
    first = first.at[plan.deep, 0].set(first[0, 1]).at[0, 1].set(row)
    rest = jnp.einsum("ok,gfck->ogfc", table[0], jnp.stack(blocks[1:]), precision=highest)
    spectrum = jnp.concatenate([first[:, None], rest], 1)
    spectrum = spectrum.reshape(plan.m_parts, plan.rows, plan.g_parts, -1)
    return spectrum.transpose(2, 0, 1, 3).reshape(plan.devices, plan.rows, -1)


def spectral_kernels(square):
    kappa = jnp.sqrt(square)
    damping = viscous * kappa
    across = 1.0 / (damping + buoyant + flexural * kappa**4)
    return damping, across


def wave_square(index, length):
    signed = jnp.where(2 * index >= length, index - length, index)
    wave = signed.astype(jnp.float32) * (2.0 * math.pi / length)
    return wave * wave


def middle_y(plan, received, position):
    deep, count, cols = plan.deep, plan.devices, plan.cols
    width = count * deep
    flat = received.reshape(count * plan.rows, -1).T
    mixed = mul(flat, plan.source_matrix())
    mixed = mixed.reshape(plan.own_groups, 2, cols, 2, width)
    cos, sin = plan.line_twiddle()
    re, im = mixed[:, :, :, 0], mixed[:, :, :, 1]
    turned = jnp.concatenate([re * cos + im * sin, im * cos - re * sin], 2)
    spectra = jnp.einsum("wk,gfkl->gfwl", plan.line_matrix(), turned, precision=highest)
    lane = lax.broadcasted_iota(jnp.int32, (1, width), 1)
    q, t = lane % deep, lane // deep
    w = lax.broadcasted_iota(jnp.int32, (cols, 1), 0)
    ky = wave_square(t + count * w, plan.length_y)
    m = (position % plan.m_parts) * deep + q
    base = (position // plan.m_parts) * plan.own_groups
    special = (position == 0) & (q == 0)
    results = []
    for group in range(plan.own_groups):
        g = base + group
        half = lanes // 2
        first = jnp.where(m < half, plan.radix * m, plan.radix // 2 + plan.radix * (m - half))
        index = jnp.where(g == 0, first, g + plan.radix * m)
        damping, across = spectral_kernels(wave_square(index, plan.length_x) + ky)
        u, v = spectra[group, 0], spectra[group, 1]
        ur, ui, vr, vi = u[:cols], u[cols:], v[:cols], v[cols:]
        out_r, out_i = across * (damping * ur - vr), across * (damping * ui - vi)
        if group == 0:
            out_r = jnp.where(special, across * (damping * ur - ui), out_r)
            out_i = jnp.where(special, across * (damping * ui + ur), out_i)
            damping, across = spectral_kernels(np.float32(math.pi) ** 2 + ky)
            extra = jnp.concatenate([across * (damping * vr - vi), across * (damping * vi + vr)], 0)
        results.append(jnp.concatenate([out_r, out_i], 0))
    results.append(extra)
    back = jnp.einsum("kw,gkl->gwl", plan.line_matrix() * np.float32(1.0 / plan.length_y), jnp.stack(results), precision=highest)
    re, im = back[:, :cols], back[:, cols:]
    turned = jnp.concatenate([re * cos - im * sin, im * cos + re * sin], 2)
    lines = jnp.einsum("gcl,sl->gcs", turned, plan.source_matrix(), precision=highest)
    place = lax.broadcasted_iota(jnp.int32, (1, count * plan.rows), 1)
    moved = (position == 0) & (place % plan.rows == deep)
    fixed = jnp.where(moved, jnp.roll(lines[-1], deep, axis=1), lines[0])
    lines = jnp.concatenate([fixed[None], lines[1:-1]], 0)
    return lines.reshape(plan.own_groups * cols, count * plan.rows).T.reshape(count, plan.rows, -1)


def inverse_x(plan, received):
    cols = plan.cols
    table = plan.slot_inverse()
    cos, sin = plan.slot_twiddle()
    split = received.reshape(plan.g_parts, 2 * lanes, plan.own_groups, cols)
    split = split.transpose(0, 2, 3, 1).reshape(plan.groups, cols, 2 * lanes)
    first = mul(split[0], table[1])
    rest = mul(split[1:], table[0])
    real, imag = [], []
    for g in range(1, plan.groups):
        re, im = rest[g - 1, :, :lanes], rest[g - 1, :, lanes:]
        real.append(re * cos[g] - im * sin[g])
        imag.append(im * cos[g] + re * sin[g])
    return radix_inverse(first[:, :lanes], first[:, lanes:], real, imag)


def to_lines(plan, field):
    split = field.reshape(plan.here, lanes, plan.gx, plan.cols)
    return split.transpose(2, 0, 3, 1)


def halves(value):
    high = value.astype(jnp.bfloat16)
    return high, (value - high.astype(jnp.float32)).astype(jnp.bfloat16)


def table_halves(table):
    high = table.astype(jnp.bfloat16)
    return np.concatenate([high, (table - high.astype(np.float32)).astype(jnp.bfloat16)], 0)


def dot(left, right, turned=False):
    dims = (((1,), (1 if turned else 0,)), ((), ()))
    return lax.dot_general(left, right, dims, preferred_element_type=jnp.float32)


def table_times(table, data, turned=False):
    rows = table.shape[0] // 2
    both = dot(table, data[0], turned)
    return both[:rows] + (both[rows:] + dot(table[:rows], data[1], turned))


def times_table(data, table):
    rows, inner = data[0].shape[0], table.shape[0] // 2
    both = dot(jnp.concatenate(data, 0), table[:inner])
    return both[:rows] + (both[rows:] + dot(data[0], table[inner:]))


def call(body, outs, scratch, scalars, *operands):
    scalar = pl.BlockSpec(memory_space=pltpu.SMEM)
    whole = pl.BlockSpec(memory_space=pltpu.VMEM)
    run = pl.pallas_call(
        body,
        out_shape=outs,
        in_specs=[scalar] * len(scalars) + [whole] * len(operands),
        out_specs=[whole] * len(outs),
        scratch_shapes=scratch,
        compiler_params=pltpu.CompilerParams(vmem_limit_bytes=16 << 20),
    )
    return run(*scalars, *operands)


def real_array(*shape):
    return jax.ShapeDtypeStruct(shape, jnp.float32)


def lines_out(plan, own, block, here, turned_ref, out_refs):
    turned_ref[here] = block.T
    for step in range(plan.gx):
        start = pl.multiple_of((own ^ step) * plan.cols, 8)
        out_refs[step][here * plan.cols : (here + 1) * plan.cols, :] = turned_ref[here, pl.ds(start, plan.cols), :]


def own_part(plan, part, row):
    wide = jnp.concatenate([row, row[:, :lanes]], 1)
    wide = jnp.broadcast_to(wide, (8, wide.shape[1]))
    out = wide[:, :lanes]
    for k in range(1, plan.gx):
        start = k * plan.cols
        low = start // lanes * lanes
        block = wide[:, low : low + 2 * lanes]
        if start % lanes:
            block = pltpu.roll(block, 2 * lanes - start % lanes, 1)
        out = jnp.where(part == k, block[:, :lanes], out)
    return out[:1]


def kernel_call(body, outs, scratch, scalars, inputs, faces=()):
    whole = pl.BlockSpec(memory_space=pltpu.VMEM)
    run = pl.pallas_call(
        body,
        out_shape=outs,
        in_specs=[pl.BlockSpec(memory_space=pltpu.SMEM)] * len(scalars) + [pl.BlockSpec(memory_space=pltpu.HBM)] * len(inputs) + [whole] * len(faces),
        out_specs=[whole] * len(outs),
        scratch_shapes=scratch,
        compiler_params=pltpu.CompilerParams(vmem_limit_bytes=16 << 20),
    )
    inputs = [pltpu.with_memory_space_constraint(x, pltpu.HBM) for x in inputs]
    return run(*scalars, *inputs, *faces)


def uplift_kernel(plan, own_ref, _, uplift_hbm, flux_x_hbm, flux_y_hbm, *refs):
    own = own_ref[0]
    out_refs = refs[: plan.gx]
    field_ref, turned_ref, last_x_ref, last_y_ref, sems = refs[plan.gx :]
    rows, cols = uplift_hbm.shape
    copies = [
        pltpu.make_async_copy(flux_x_hbm.at[pl.ds(rows - 8, 8), :], last_x_ref, sems.at[0]),
        pltpu.make_async_copy(flux_y_hbm.at[:, pl.ds(cols - lanes, lanes)], last_y_ref, sems.at[1]),
    ]
    half = lanes // 2
    for part in range(2 * plan.here):
        source = uplift_hbm.at[pl.ds(part * half, half), :]
        copies.append(pltpu.make_async_copy(source, field_ref.at[pl.ds(part * half, half), :], sems.at[2 + part]))
    for copy in copies[2:] + copies[:2]:
        copy.start()
    for here in range(plan.here):
        copies[2 + 2 * here].wait()
        copies[3 + 2 * here].wait()
        turned_ref[here] = field_ref[here * lanes : (here + 1) * lanes, :].T
        for step in range(plan.gx):
            start = pl.multiple_of((own ^ step) * plan.cols, 8)
            out_refs[step][here * plan.cols : (here + 1) * plan.cols, :] = turned_ref[here, pl.ds(start, plan.cols), :]
    copies[0].wait()
    copies[1].wait()
    last_x = last_x_ref[7:8, :]
    last_y = last_y_ref[...].T[lanes - 1 : lanes, :]
    parts = [last[:, a * lanes : (a + 1) * lanes] for last in (last_x, last_y) for a in range(plan.here)]
    parts.append(jnp.zeros((plan.tail - 2 * plan.here, lanes), jnp.float32))
    parts = jnp.concatenate(parts, 0)
    for step in range(plan.gx):
        out_refs[step][plan.here * plan.cols :, :] = parts


def send_uplift(plan, own, across_y, bed_uplift, flux_x, flux_y):
    rows, cols = bed_uplift.shape
    run = pl.pallas_call(
        lambda *refs: uplift_kernel(plan, *refs),
        out_shape=[real_array(plan.piece_rows, lanes)] * plan.gx,
        in_specs=[pl.BlockSpec(memory_space=pltpu.SMEM)] * 2 + [pl.BlockSpec(memory_space=pltpu.HBM)] * 3,
        out_specs=[pl.BlockSpec(memory_space=pltpu.VMEM)] * plan.gx,
        compiler_params=pltpu.CompilerParams(vmem_limit_bytes=16 << 20),
        scratch_shapes=[
            pltpu.VMEM((rows, cols), jnp.float32),
            pltpu.VMEM((plan.here, cols, lanes), jnp.float32),
            pltpu.VMEM((8, cols), jnp.float32),
            pltpu.VMEM((rows, lanes), jnp.float32),
            pltpu.SemaphoreType.DMA((2 + 2 * plan.here,)),
        ],
    )
    fields = [pltpu.with_memory_space_constraint(x, pltpu.HBM) for x in (bed_uplift, flux_x, flux_y)]
    return run(own, across_y, *fields)


def fetch_fields(plan, sources, mask_ref, floats_ref, sems):
    targets = [floats_ref.at[k] for k in range(4)] + [mask_ref]
    copies = []
    for here in range(plan.here):
        rows = pl.ds(here * lanes, lanes)
        group = [
            pltpu.make_async_copy(source.at[rows, :], target.at[rows, :], sems.at[here, k])
            for k, (source, target) in enumerate(zip(sources, targets))
        ]
        for copy in group:
            copy.start()
        copies.append(group)
    return copies


def trial_block(floats_ref, here, above, left_edge):
    rows = slice(here * lanes, (here + 1) * lanes)
    fx, fy = floats_ref[1, rows, :], floats_ref[2, rows, :]
    row = lax.broadcasted_iota(jnp.int32, fx.shape, 0)
    col = lax.broadcasted_iota(jnp.int32, fx.shape, 1)
    if here:
        above = floats_ref[1, here * lanes - 1 : here * lanes, :]
    below = jnp.where(row == 0, jnp.broadcast_to(above, fx.shape) if here or above.ndim else above, pltpu.roll(fx, 1, 0))
    left = jnp.where(col == 0, left_edge, pltpu.roll(fy, 1, 1))
    divergence = fx - below + fy - left
    return floats_ref[0, rows, :] + time_step * (floats_ref[3, rows, :] - divergence)


hidden = np.float32(-1e30)


def load_kernel(plan, own_ref, *refs):
    own = own_ref[0]
    sources, refs = refs[:5], refs[5:]
    line_refs, (mask_ref, floats_ref, turned_ref, sems) = refs[: plan.gx], refs[plan.gx :]
    copies = fetch_fields(plan, sources, mask_ref, floats_ref, sems)
    columns_trial, columns_thick = [], []
    for here in range(plan.here):
        for copy in copies[here]:
            copy.wait()
        rows = slice(here * lanes, (here + 1) * lanes)
        trial = trial_block(floats_ref, here, jnp.float32(0.0), 0.0)
        free = mask_ref[rows, :] == 0
        thick = jnp.where(free, floats_ref[0, rows, :], 0.0)
        trial = jnp.where(free, trial, hidden)
        lines_out(plan, own, jnp.maximum(trial, 0.0) - thick, here, turned_ref, line_refs)
        lane = lax.broadcasted_iota(jnp.int32, (lanes, lanes), 1)
        packed = jnp.where(lane == 0, trial[:, :lanes], pltpu.roll(thick[:, :lanes], 1, 1)).T
        columns_trial.append(packed[0:1])
        columns_thick.append(packed[1:2])
        if here == 0:
            row_trial, row_thick = trial[0:1], thick[0:1]
    tail = plan.here * plan.cols
    rest = plan.tail - 2 - 2 * plan.here
    for step in range(plan.gx):
        parts = [own_part(plan, own ^ step, row_trial), own_part(plan, own ^ step, row_thick)] + columns_trial + columns_thick
        if rest:
            parts.append(jnp.zeros((rest, lanes), jnp.float32))
        line_refs[step][tail : tail + plan.tail, :] = jnp.concatenate(parts, 0)


def field_scratch(shape):
    return [
        pltpu.VMEM(shape, jnp.int32),
        pltpu.VMEM((4,) + shape, jnp.float32),
    ]


def make_load(plan, own, fields):
    shape = fields[0].shape
    scratch = field_scratch(shape) + [
        pltpu.VMEM((plan.here, shape[1], lanes), jnp.float32),
        pltpu.SemaphoreType.DMA((plan.here, 5)),
    ]
    outs = [real_array(plan.piece_rows, lanes)] * plan.gx
    return kernel_call(lambda *refs: load_kernel(plan, *refs), outs, scratch, [own], fields)


def row_above(plan, own, block, tails):
    above = [jnp.zeros((1, lanes), jnp.float32)] * plan.here
    for step in range(plan.gx):
        match = (own ^ step) + 1 == block
        above = [jnp.where(match, tails[step][a : a + 1, :], above[a]) for a in range(plan.here)]
    return jnp.concatenate(above, 1)


def thickness_kernel(plan, own_ref, *refs):
    own = own_ref[0]
    sources, (tails_ref, side_ref, out_ref, mask_ref, floats_ref, sems) = refs[:5], refs[5:]
    copies = fetch_fields(plan, sources, mask_ref, floats_ref, sems)
    above = row_above(plan, own, own, [tails_ref[step] for step in range(plan.gx)])
    for here in range(plan.here):
        for copy in copies[here]:
            copy.wait()
        rows = slice(here * lanes, (here + 1) * lanes)
        side = jnp.broadcast_to(side_ref[0, plan.here + here : plan.here + here + 1, :], (lanes, lanes)).T
        side = jnp.concatenate([side] * (out_ref.shape[1] // lanes), 1)
        trial = trial_block(floats_ref, here, above, side)
        out_ref[rows, :] = jnp.where(mask_ref[rows, :] == 2, 0.0, jnp.maximum(trial, 0.0))


def make_thickness(plan, own, fields, faces):
    shape = fields[0].shape
    scratch = field_scratch(shape) + [pltpu.SemaphoreType.DMA((plan.here, 5))]
    return kernel_call(lambda *refs: thickness_kernel(plan, *refs), [real_array(*shape)], scratch, [own], fields, faces)[0]


def finish_load(plan, own, line_ref, uplift_tails, load_tails, side_ref):
    cols, here = plan.cols, plan.here
    lane = lax.broadcasted_iota(jnp.int32, (1, lanes), 1)
    wide_lane = lax.broadcasted_iota(jnp.int32, (cols, lanes), 1)
    above, new = [], []
    for step in range(plan.gx):
        above.append(own_part(plan, own, row_above(plan, own, own ^ step, uplift_tails)))
        tail = load_tails[step]
        new.append(jnp.maximum(tail[0:1, :] + time_step * above[step], 0.0) - tail[1:2, :])
    turned = jnp.concatenate(new + [jnp.zeros((lanes - plan.gx, lanes), jnp.float32)], 0).T[:cols]
    for step in range(plan.gx):
        place = (own ^ step) * here
        first = pltpu.roll(turned, lanes - step, 1) if step else turned
        line_ref[place] = jnp.where(wide_lane == 0, first, line_ref[place])

    @pl.when(own == 0)
    def _():
        for step in range(plan.gx):
            tail = load_tails[step]
            for a in range(here):
                corner = jnp.where(lane == 0, jnp.broadcast_to(above[step][:, :1], (1, lanes)), 0.0) if a == 0 else 0.0
                trial = tail[2 + a : 3 + a, :] + time_step * (side_ref[step, here + a : here + a + 1, :] + corner)
                line_ref[step * here + a, 0:1, :] = jnp.maximum(trial, 0.0) - tail[2 + here + a : 3 + here + a, :]


def tails_kernel(plan, *refs):
    pieces, tails_ref = refs[: plan.gx], refs[plan.gx]
    start = plan.here * plan.cols
    for step in range(plan.gx):
        tails_ref[step] = pieces[step][start : start + plan.tail, :]


def forward_kernel(plan, lead, own_ref, *refs):
    pieces, refs = refs[: plan.gx], refs[plan.gx :]
    cols, radix, groups, here = plan.cols, plan.radix, plan.groups, plan.here
    own = own_ref[0]
    tail = slice(here * cols, here * cols + plan.tail)
    if lead:
        uplift_tails, side_ref, edge_ref, head_ref, _, twiddle_ref, table_ref, *refs = refs
        out_ref, line_ref, high_ref, low_ref = refs
    else:
        twiddle_ref, table_ref, out_ref, edge_ref, head_ref, line_ref, high_ref, low_ref = refs
    step_rows = 16
    total = groups * cols
    for step in range(plan.gx):
        for a in range(here):
            line_ref[(own ^ step) * here + a] = pieces[step][a * cols : (a + 1) * cols, :]
    if lead:
        tails = [uplift_tails[step] for step in range(plan.gx)]
        finish_load(plan, own, line_ref, tails, [piece[tail, :] for piece in pieces], side_ref)
    skip = lead % lanes

    def chunk(index, carry):
        row = pl.multiple_of(index * step_rows, step_rows)
        real, imag = radix_forward([line_ref[n, pl.ds(row, step_rows), :] for n in range(radix)])
        for g in range(groups):
            if g == 0:
                first, second = real[0], real[groups]
            else:
                cos, sin = twiddle_ref[0, g : g + 1, :], twiddle_ref[1, g : g + 1, :]
                first = real[g] * cos + imag[g - 1] * sin
                second = imag[g - 1] * cos - real[g] * sin
            high, low = halves(jnp.concatenate([first, second], 1))
            target = pl.ds(skip + g * cols + row, step_rows)
            high_ref[target, :] = high
            low_ref[target, :] = low
        return carry

    lax.fori_loop(0, cols // step_rows, chunk, 0, unroll=True)
    for edge in ((0, skip), (skip + total, high_ref.shape[0])):
        if edge[0] < edge[1]:
            high_ref[edge[0] : edge[1], :] = jnp.zeros((edge[1] - edge[0], 2 * lanes), jnp.bfloat16)
            low_ref[edge[0] : edge[1], :] = jnp.zeros((edge[1] - edge[0], 2 * lanes), jnp.bfloat16)
    before = (lead - skip) // lanes
    blocks = high_ref.shape[0] // lanes

    def place(block):
        return slice((before + block) * lanes, (before + block + 1) * lanes)

    held = -(-(skip + cols) // lanes) if lead else 0
    end = skip + cols
    special = -(-end // lanes) * lanes
    first = table_times(table_ref[1], (high_ref[:special, :], low_ref[:special, :]), True)
    for block in range(blocks):
        start = block * lanes
        if block % 2 == 0:
            rows = slice(start, min(start + 2 * lanes, blocks * lanes))
            pair = table_times(table_ref[0], (high_ref[rows, :], low_ref[rows, :]), True)
        out = pair[:, (block % 2) * lanes : (block % 2 + 1) * lanes]
        if start < end:
            lane = lax.broadcasted_iota(jnp.int32, (2 * lanes, lanes), 1)
            out = jnp.where(lane < end - start, first[:, start : start + lanes], out)
        out = out.reshape(plan.devices, plan.rows, lanes)
        if start < skip:
            lane = lax.broadcasted_iota(jnp.int32, out.shape, 2)
            out = jnp.where(lane < skip - start, edge_ref[...], out)
        if not lead and (block + 1) * lanes > total:
            edge_ref[...] = out
            continue
        out_ref[:, :, place(block)] = out
        if not lead and block == 0:
            head_ref[...] = out[0]
        if block + 1 == held:
            two = jnp.concatenate([out_ref[0, :, place(k)] for k in range(held)], 1)
            width = held * lanes
            row = lax.broadcasted_iota(jnp.int32, two.shape, 0)
            lane = lax.broadcasted_iota(jnp.int32, two.shape, 1)
            head = head_ref[...]
            wide = pltpu.roll(jnp.concatenate([head] * held, 1), plan.deep, 0)
            to_right = pltpu.roll(wide, skip, 1) if skip else wide
            swapped = pltpu.roll(two, plan.deep, 0)
            to_left = pltpu.roll(swapped, width - skip, 1) if skip else swapped
            take = (row[:, :lanes] == plan.deep) & (lane[:, :lanes] < cols)
            out_ref[0, :, :lanes] = jnp.where(take, to_left[:, :lanes], head)
            take = (row == 0) & (lane >= skip) & (lane < skip + cols)
            fixed = jnp.where(take, to_right, two)
            for k in range(held):
                out_ref[0, :, place(k)] = fixed[:, k * lanes : (k + 1) * lanes]


def make_forward(plan, own, pieces, tables, before=None):
    half = plan.groups * plan.cols
    lead = half if before else 0
    skip = lead % lanes
    blocks = -(-(skip + half) // lanes)
    whole = pl.BlockSpec(memory_space=pltpu.VMEM)
    outs, operands, alias = [real_array(plan.devices, plan.rows, 2 * half)], list(pieces), {}
    if before:
        tails, side, spectrum, edge, head = before
        operands += [tails, side, edge, head, spectrum]
        alias = {len(operands): 0}
    else:
        outs += [real_array(plan.devices, plan.rows, lanes), real_array(plan.rows, lanes)]
    operands += tables
    run = pl.pallas_call(
        lambda *refs: forward_kernel(plan, lead, *refs),
        out_shape=outs,
        in_specs=[pl.BlockSpec(memory_space=pltpu.SMEM)] + [whole] * len(operands),
        out_specs=[whole] * len(outs),
        scratch_shapes=[
            pltpu.VMEM((plan.radix, plan.cols, lanes), jnp.float32),
            pltpu.VMEM((blocks * lanes, 2 * lanes), jnp.bfloat16),
            pltpu.VMEM((blocks * lanes, 2 * lanes), jnp.bfloat16),
        ],
        input_output_aliases=alias,
        compiler_params=pltpu.CompilerParams(vmem_limit_bytes=16 << 20),
    )
    return run(own, *operands)


def middle_kernel(plan, own_ref, across_ref, in_ref, t1_ref, t2_ref, t2i_ref, t1i_ref, twiddle_ref, out_ref, high_ref, low_ref, back_high, back_low, turn_ref, mixed_ref):
    position = across_ref[0] * plan.gx + own_ref[0]
    cols, groups, deep, count = plan.cols, plan.groups, plan.deep, plan.devices
    width, size = lanes, 2 * lanes
    for start in range(0, 2 * groups * cols, lanes):
        block = in_ref[:, :, start : start + lanes].reshape(size, lanes).T
        high_ref[start : start + lanes, :], low_ref[start : start + lanes, :] = halves(block)
    step = 2 * groups * cols // 4
    for start in range(0, 2 * groups * cols, step):
        rows = slice(start, start + step)
        mixed_ref[rows, :] = times_table((high_ref[rows, :], low_ref[rows, :]), t1_ref[...])
    cos, sin = twiddle_ref[0], twiddle_ref[1]
    lane = lax.broadcasted_iota(jnp.int32, (1, width), 1)
    q, t = lane % deep, lane // deep
    w = lax.broadcasted_iota(jnp.int32, (cols, width), 0)
    ky = wave_square(t + count * w, plan.length_y)
    m = position * deep + q
    special = jnp.broadcast_to((position == 0) & (q == 0), (cols, width))
    results = []
    for g in range(groups):
        sides = []
        for field in range(2):
            part = mixed_ref[(field * groups + g) * cols : (field * groups + g + 1) * cols, :]
            re, im = part[:, :width], part[:, width:]
            sides.append(jnp.concatenate([re * cos + im * sin, im * cos - re * sin], 0))
        spectra = table_times(t2_ref[...], halves(jnp.concatenate(sides, 1)))
        ur, vr = spectra[:cols, :width], spectra[:cols, width:]
        ui, vi = spectra[cols:, :width], spectra[cols:, width:]
        half = lanes // 2
        if g == 0:
            index = jnp.where(m < half, plan.radix * m, plan.radix // 2 + plan.radix * (m - half))
        else:
            index = g + plan.radix * m
        damping, across = spectral_kernels(wave_square(index, plan.length_x) + ky)
        out_r, out_i = across * (damping * ur - vr), across * (damping * ui - vi)
        if g == 0:
            out_r = jnp.where(special, across * (damping * ur - ui), out_r)
            out_i = jnp.where(special, across * (damping * ui + ur), out_i)
            damping, across = spectral_kernels(np.float32(math.pi) ** 2 + ky)
            extra = jnp.concatenate([across * (damping * vr - vi), across * (damping * vi + vr)], 0)
        results.append(jnp.concatenate([out_r, out_i], 0))
    results.append(extra)
    for g in range(0, groups + 1, 2):
        pair = results[g : g + 2]
        back = table_times(t2i_ref[...], halves(jnp.concatenate(pair, 1)))
        for k in range(len(pair)):
            re, im = back[:cols, k * width : (k + 1) * width], back[cols:, k * width : (k + 1) * width]
            turned = jnp.concatenate([re * cos - im * sin, im * cos + re * sin], 1)
            place = slice((g + k) * cols, (g + k + 1) * cols)
            back_high[place, :], back_low[place, :] = halves(turned)
    total = (groups + 1) * cols
    cuts = [total * k // 2 // 16 * 16 for k in range(2)] + [total]
    for start, stop in zip(cuts, cuts[1:]):
        rows = slice(start, stop)
        turn_ref[rows, :] = times_table((back_high[rows, :], back_low[rows, :]), t1i_ref[...])
    place = lax.broadcasted_iota(jnp.int32, (cols, size), 1)
    moved = (position == 0) & (place % plan.rows == deep)
    extra = turn_ref[groups * cols : (groups + 1) * cols, :]
    turn_ref[:cols, :] = jnp.where(moved, pltpu.roll(extra, deep, 1), turn_ref[:cols, :])
    for start in range(0, groups * cols, lanes):
        block = turn_ref[start : start + lanes, :].T.reshape(count, plan.rows, lanes)
        keep = min(lanes, groups * cols - start)
        real, imag = block[:, :deep], block[:, deep:]
        if keep < lanes:
            place = lax.broadcasted_iota(jnp.int32, real.shape, 2)
            out_ref[:, :, 2 * start : 2 * start + 2 * keep] = jnp.where(place < keep, real, pltpu.roll(imag, keep, 2))[:, :, : 2 * keep]
        else:
            out_ref[:, :, 2 * start : 2 * start + lanes] = real
            out_ref[:, :, 2 * start + lanes : 2 * start + 2 * lanes] = imag


def inverse_kernel(plan, own_ref, in_ref, twiddle_ref, table_ref, *refs):
    out_refs, (line_ref, turn_ref, mid_ref) = refs[: plan.gx], refs[plan.gx :]
    own = own_ref[0]
    cols, groups, here = plan.cols, plan.groups, plan.here
    size = 2 * lanes
    total = groups * cols
    for start in range(0, total, lanes):
        keep = min(lanes, total - start)
        real = in_ref[:, :, 2 * start : 2 * start + lanes]
        imag = pltpu.roll(real, keep, 2) if keep < lanes else in_ref[:, :, 2 * start + lanes : 2 * start + 2 * lanes]
        block = jnp.concatenate([real, imag], 1).reshape(size, lanes)
        turn_ref[start : start + keep, :] = block.T[:keep]
    mid_ref[:cols, :] = times_table(halves(turn_ref[:cols, :]), table_ref[1])
    mid_ref[cols:, :] = times_table(halves(turn_ref[cols:, :]), table_ref[0])
    step_rows = 16

    def chunk(index, carry):
        row = pl.multiple_of(index * step_rows, step_rows)
        real, imag = [], []
        for g in range(1, groups):
            place = pl.ds(g * cols + row, step_rows)
            re, im = mid_ref[place, :lanes], mid_ref[place, lanes:]
            cos, sin = twiddle_ref[0, g : g + 1, :], twiddle_ref[1, g : g + 1, :]
            real.append(re * cos - im * sin)
            imag.append(im * cos + re * sin)
        place = pl.ds(row, step_rows)
        values = radix_inverse(mid_ref[place, :lanes], mid_ref[place, lanes:], real, imag)
        for n, value in enumerate(values):
            line_ref[n, place, :] = value
        return carry

    lax.fori_loop(0, cols // step_rows, chunk, 0, unroll=True)
    for step in range(plan.gx):
        for a in range(here):
            out_refs[step][a] = line_ref[(own ^ step) * here + a]


def final_kernel(plan, own_ref, *refs):
    pieces, (out_hbm, line_ref, block_ref, sems) = refs[: plan.gx], refs[plan.gx :]
    own = own_ref[0]
    sent = []
    for a in range(plan.here):
        for step in range(plan.gx):
            start = pl.multiple_of((own ^ step) * plan.cols, 8)
            line_ref[a, pl.ds(start, plan.cols), :] = pieces[step][a]
        block_ref[a] = line_ref[a].T
        sent.append(pltpu.make_async_copy(block_ref.at[a], out_hbm.at[pl.ds(a * lanes, lanes), :], sems.at[a]))
        sent[-1].start()
    for copy in sent:
        copy.wait()


def make_final(plan, own, pieces, shape):
    whole = pl.BlockSpec(memory_space=pltpu.VMEM)
    run = pl.pallas_call(
        lambda *refs: final_kernel(plan, *refs),
        out_shape=real_array(*shape),
        in_specs=[pl.BlockSpec(memory_space=pltpu.SMEM)] + [whole] * plan.gx,
        out_specs=pl.BlockSpec(memory_space=pl.ANY),
        scratch_shapes=[
            pltpu.VMEM((plan.here, shape[1], lanes), jnp.float32),
            pltpu.VMEM((plan.here, lanes, shape[1]), jnp.float32),
            pltpu.SemaphoreType.DMA((plan.here,)),
        ],
        compiler_params=pltpu.CompilerParams(vmem_limit_bytes=16 << 20),
    )
    return run(own, *pieces)


def swap_gx(plan, pieces):
    got = [pieces[0]]
    for step in range(1, plan.gx):
        got.append(lax.ppermute(pieces[step], "gx", [(k, k ^ step) for k in range(plan.gx)]))
    return got


def build_kernels(plan):
    vmem, f32, bf16 = pltpu.VMEM, jnp.float32, jnp.bfloat16
    size, cols, groups = 2 * lanes, plan.cols, plan.groups
    half = groups * cols
    pieces = [real_array(plan.here, cols, lanes)] * plan.gx
    line = vmem((plan.radix, cols, lanes), f32)

    def local(thickness, bed_uplift, flux_x, flux_y, mass_balance, ice_mask):
        own, across_y = lax.axis_index("gx").reshape(1), lax.axis_index("gy").reshape(1)
        fields = (thickness, flux_x, flux_y, mass_balance, ice_mask)
        uplift = send_uplift(plan, own, across_y, bed_uplift, flux_x, flux_y)
        lines_u = swap_gx(plan, uplift)
        load = make_load(plan, own, fields)
        lines_v = swap_gx(plan, load)
        twiddle = plan.slot_twiddle()
        tables = np.stack([table_halves(table) for table in plan.slot_matrix()])
        (tails_u,) = call(lambda *refs: tails_kernel(plan, *refs), [real_array(plan.gx, plan.tail, lanes)], [], [], *lines_u)
        side = passed_along(tails_u, "gy", 1)
        partial = make_forward(plan, own, lines_u, (twiddle, tables))
        (spectrum,) = make_forward(plan, own, lines_v, (twiddle, tables), (tails_u, side, *partial))
        thickness_new = make_thickness(plan, own, fields, (tails_u, side))
        received = exchange_all(spectrum)
        source, across = plan.source_matrix(), plan.line_matrix()
        scale = np.float32(1.0 / plan.length_y)
        tables = [table_halves(table) for table in (source, across, across.T * scale, source.T)]
        (middle,) = call(
            lambda *refs: middle_kernel(plan, *refs),
            [real_array(plan.devices, plan.deep, 2 * half)],
            [vmem((2 * half, size), bf16)] * 2 + [vmem((half + cols, size), bf16)] * 2 + [vmem((half + cols, size), f32), vmem((2 * half, size), f32)],
            [own, across_y],
            *([received] + tables + [plan.line_twiddle()]),
        )
        back = exchange_all(middle)
        inverse = np.stack([table_halves(table) for table in plan.slot_inverse()])
        bed = call(
            lambda *refs: inverse_kernel(plan, *refs),
            pieces,
            [line] + [vmem((half, size), f32)] * 2,
            [own],
            *(back, twiddle, inverse),
        )
        lines_b = swap_gx(plan, bed)
        bed_new = make_final(plan, own, lines_b, thickness.shape)
        return thickness_new, bed_new

    return local


def build(plan):
    if plan.devices * plan.rows == 2 * lanes and plan.cols % 16 == 0 and plan.radix <= 16 and plan.gx in (2, 4, 8) and plan.groups * plan.cols % lanes in (0, lanes // 2):
        return build_kernels(plan)

    def local(thickness, bed_uplift, flux_x, flux_y, mass_balance, ice_mask):
        lower_face = passed_along(flux_x[-1:, :], "gx", 1)
        left_face = passed_along(flux_y[:, -1:], "gy", 1)
        flux_below = jnp.concatenate([lower_face, flux_x[:-1, :]], axis=0)
        flux_left = jnp.concatenate([left_face, flux_y[:, :-1]], axis=1)
        divergence = flux_x - flux_below + flux_y - flux_left
        trial = thickness + time_step * (mass_balance - divergence)
        thickness_new = jnp.where(ice_mask == 2, 0.0, jnp.maximum(trial, 0.0))
        load = jnp.where(ice_mask == 0, thickness_new - thickness, 0.0)
        fields = jnp.stack([to_lines(plan, bed_uplift), to_lines(plan, load)], 1)
        lines = exchange_gx(fields)
        lines = lines.transpose(1, 0, 2, 3, 4).reshape(2, plan.radix, plan.cols, lanes)
        received = exchange_all(forward_x(plan, lines))
        position = lax.axis_index("gy") * plan.gx + lax.axis_index("gx")
        back = exchange_all(middle_y(plan, received, position))
        bed = inverse_x(plan, back)
        bed = jnp.stack(bed).reshape(plan.gx, plan.here, plan.cols, lanes)
        bed = exchange_gx(bed)
        bed_new = bed.transpose(1, 3, 0, 2).reshape(plan.here * lanes, plan.gx * plan.cols)
        return thickness_new, bed_new

    return local


def solution(mesh):
    spec = P("gx", "gy")

    def step(*args):
        length_x, length_y = args[0].shape
        plan = Plan(mesh, length_x, length_y)
        body = jax.shard_map(build(plan), mesh=mesh, in_specs=(spec,) * 6, out_specs=(spec, spec), check_vma=False)
        return body(*args)

    return step
```
